32 devices in a mesh: gx: 4 (over x, core), gy: 8 (over z, y).
Axes of the slice: x: 2, y: 2, z: 4, core: 2. Of those that a mesh axis runs over, the one named last changes fastest.
Arguments:
- right_side: float32 [32, 64, 512], P('gx', 'gy'), may hold values from -18 to 18
- inverse_density: float32 [32, 64, 512], P('gx', 'gy'), may hold values from 0.01 to 10
Outputs:
- correction: float32 [32, 64, 512], P('gx', 'gy')
- residual: float32 [32, 64, 512], P('gx', 'gy')
The draws below stay inside these ranges and needn't reach their ends.
All inputs are finite; a program needn't handle non-finite values.
Results may differ from the reference program's by a relative error of at most 0.00013.
Values sent between devices are 32-bit elements; how exact they have to be, the bound alone decides.
A program may use at most 64 MiB of HBM per device.

```python
import math
import jax
import jax.numpy as jnp
from jax import lax

CZ = 512
SWEEPS = 2
COARSE_SWEEPS = 8
NX = 32
NY = 64


def steps_of(rng, shape, pieces, low, largest):
    loudness = 1.0
    for position, shards_of in pieces:
        draws = jax.random.uniform(jax.random.fold_in(jax.random.fold_in(rng, 6), position), (shards_of,), jnp.float32, low / len(pieces), largest / len(pieces))
        loudness = loudness * jnp.repeat(jnp.exp(draws), shape[position] // shards_of).reshape((-1,) + (1,) * (len(shape) - 1 - position))
    return loudness


def gaussian(rng, extent, width, bound, pieces=(), kind=jnp.bfloat16):
    array = jax.random.normal(rng, extent, jnp.float32) * width
    if len(pieces) > 0:
        array = steps_of(rng, extent, pieces, -0.22, 0.18) * array
    return jnp.clip(array, min=-bound, max=bound).astype(kind)


def setup_inputs(seed: int = 0) -> dict:
    key_list = jax.random.split(jax.random.key(seed), 3)
    right_side = gaussian(key_list[0], (NX, NY, CZ), 3.0, 18.0, ((0, 4), (1, 8)), jnp.float32)
    inverse_density = jnp.clip(jnp.exp(math.log(10.0) - 6.9077553 * jax.random.uniform(key_list[1], (NX, NY, CZ), jnp.float32) ** steps_of(key_list[1], (NX, NY, CZ), ((0, 4), (1, 8)), -0.2, 0.2)), 0.01, 10.0)
    return {"right_side": right_side, "inverse_density": inverse_density}


def shift_down(values):
    return jnp.pad(values, ((0, 0), (0, 0), (1, 0)))[:, :, :-1]


def shift_up(values):
    return jnp.pad(values, ((0, 0), (0, 0), (0, 1)))[:, :, 1:]


def pad_plane(values):
    return jnp.pad(values, ((1, 1), (1, 1), (0, 0)))


def face_coefs(padded, scale):
    centre = padded[1:-1, 1:-1]
    faces = (
        scale * 0.5 * (centre + padded[:-2, 1:-1]),
        scale * 0.5 * (centre + padded[2:, 1:-1]),
        scale * 0.5 * (centre + padded[1:-1, :-2]),
        scale * 0.5 * (centre + padded[1:-1, 2:]),
        scale * 0.5 * (centre + shift_down(centre)),
        scale * 0.5 * (centre + shift_up(centre)),
    )
    diagonal = faces[0] + faces[1] + faces[2] + faces[3] + faces[4] + faces[5]
    return faces, diagonal


def neighbours(padded, faces):
    centre = padded[1:-1, 1:-1]
    total = faces[0] * padded[:-2, 1:-1] + faces[1] * padded[2:, 1:-1]
    total = total + faces[2] * padded[1:-1, :-2] + faces[3] * padded[1:-1, 2:]
    total = total + faces[4] * shift_down(centre) + faces[5] * shift_up(centre)
    return total


def red_cells(shape):
    along_x = lax.broadcasted_iota(jnp.int32, shape, 0)
    along_y = lax.broadcasted_iota(jnp.int32, shape, 1)
    along_z = lax.broadcasted_iota(jnp.int32, shape, 2)
    return (along_x + along_y + along_z) % 2 == 0


def smooth(field, source, faces, diagonal, sweeps):
    red = red_cells(field.shape)
    for sweep in range(sweeps):
        for colour in (red, jnp.logical_not(red)):
            update = (source + neighbours(pad_plane(field), faces)) / diagonal
            field = jnp.where(colour, update, field)
    return field


def apply_residual(field, source, faces, diagonal):
    return source - (diagonal * field - neighbours(pad_plane(field), faces))


def restrict(values):
    size_x, size_y, size_z = values.shape
    blocks = values.reshape(size_x // 2, 2, size_y // 2, 2, size_z // 2, 2)
    return jnp.mean(blocks, axis=(1, 3, 5))


def prolong(values):
    return jnp.repeat(jnp.repeat(jnp.repeat(values, 2, axis=0), 2, axis=1), 2, axis=2)


def reference(right_side, inverse_density):
    level_one = restrict(inverse_density)
    level_two = restrict(level_one)
    faces_zero, diag_zero = face_coefs(pad_plane(inverse_density), 1.0)
    faces_one, diag_one = face_coefs(pad_plane(level_one), 0.25)
    faces_two, diag_two = face_coefs(pad_plane(level_two), 0.0625)
    fine = smooth(jnp.zeros_like(right_side), right_side, faces_zero, diag_zero, SWEEPS)
    source_one = restrict(apply_residual(fine, right_side, faces_zero, diag_zero))
    middle = smooth(jnp.zeros_like(source_one), source_one, faces_one, diag_one, SWEEPS)
    source_two = restrict(apply_residual(middle, source_one, faces_one, diag_one))
    coarse = smooth(jnp.zeros_like(source_two), source_two, faces_two, diag_two, COARSE_SWEEPS)
    middle = smooth(middle + prolong(coarse), source_one, faces_one, diag_one, SWEEPS)
    fine = smooth(fine + prolong(middle), right_side, faces_zero, diag_zero, SWEEPS)
    return fine, apply_residual(fine, right_side, faces_zero, diag_zero)
```

```python
import functools

import jax
import jax.numpy as jnp
from jax import lax
from jax.experimental import pallas as pl
from jax.experimental.pallas import tpu as pltpu
from jax.sharding import PartitionSpec as P

SWEEPS = 2
COARSE_SWEEPS = 8
MESH = pl.DeviceIdType.MESH
LANES = 128
F32 = jnp.float32


def iota(shape, dim):
    return lax.broadcasted_iota(jnp.int32, shape, dim)


def lane_prev(a):
    return jnp.where(iota(a.shape, 2) == 0, 0.0, pltpu.roll(a, 1, 2))


def lane_next(a):
    return jnp.where(iota(a.shape, 2) == LANES - 1, 0.0, pltpu.roll(a, LANES - 1, 2))


def row_prev(a, halo):
    return jnp.where(iota(a.shape, 1) == 0, halo, pltpu.roll(a, 1, 1)) if a.shape[1] % 8 == 0 else jnp.concatenate(
        [halo, a[:, :-1]], axis=1
    )


def row_next(a, halo):
    rows = a.shape[1]
    return jnp.where(iota(a.shape, 1) == rows - 1, halo, pltpu.roll(a, rows - 1, 1)) if rows % 8 == 0 else jnp.concatenate(
        [a[:, 1:], halo], axis=1
    )


def even_cells(shape):
    return (iota(shape, 0) + iota(shape, 1)) % 2 == 0


REGION_Y = 16


def z_other(o, colour, first):
    shape = o[0].shape
    even = (iota(shape, 0) + iota(shape, 1)) % 2 == first % 2
    low = even if colour == 0 else jnp.logical_not(even)
    last = len(o) - 1
    out = []
    for b in range(last + 1):
        before = o[b - 1] if b > 0 else lane_prev(o[last])
        after = o[b + 1] if b < last else lane_next(o[0])
        out.append(jnp.where(low, before, after))
    return out


def around(ref, colour, x0, x1):
    other = 1 - colour
    groups = range(ref.shape[1])
    mid = [ref[other, b, x0:x1] for b in groups]
    zo = z_other(mid, colour, x0)
    return [
        (
            ref[other, b, x0 - 1 : x1 - 1],
            ref[other, b, x0 + 1 : x1 + 1],
            pltpu.roll(mid[b], 1, 1),
            pltpu.roll(mid[b], REGION_Y - 1, 1),
            mid[b],
            zo[b],
        )
        for b in groups
    ]


def split_even(zero, one):
    even = even_cells(zero.shape)
    return jnp.where(even, zero, one), jnp.where(even, one, zero)


def pair_rows(a):
    rows = a.shape[1] // 2
    a = a.reshape(a.shape[0] // 2, 2, a.shape[1], LANES)
    a = a[:, 0] + a[:, 1]
    pick = iota((a.shape[0], rows, LANES), 1)
    out = a[:, 0:1] + a[:, 1:2]
    out = jnp.broadcast_to(out, pick.shape)
    for j in range(1, rows):
        out = jnp.where(pick == j, a[:, 2 * j : 2 * j + 1] + a[:, 2 * j + 1 : 2 * j + 2], out)
    return out * 0.125


def double_rows(a):
    x, rows, _ = a.shape
    pick = iota((x, 2 * rows, LANES), 1) // 2
    out = jnp.broadcast_to(a[:, 0:1], pick.shape)
    for j in range(1, rows):
        out = jnp.where(pick == j, a[:, j : j + 1], out)
    return jnp.concatenate([out[i // 2 : i // 2 + 1] for i in range(2 * x)], axis=0)


def three(x):
    high = x.astype(jnp.bfloat16)
    rest = x - high.astype(F32)
    middle = rest.astype(jnp.bfloat16)
    low = (rest - middle.astype(F32)).astype(jnp.bfloat16)
    return high, middle, low


def permute(x, matrix, side):
    parts = [
        lax.dot_general(part, matrix, (((1,), (side,)), ((), ())), preferred_element_type=F32)
        for part in three(x)
    ]
    return (parts[0] + parts[1]) + parts[2]


def kernel(nx, ny, g_ref, c_ref, v_out, r_out, perm, k0, d0, v0, g0, k1, d1, v1, g1, k2,
           sx0, sy0, sc0, rx0, ry0, rc0, sx1, sy1, sc1, rx1, ry1, rc1, ga, gb, vc, cw, held, sem0, sem1, semx, semy, held_sem):
    gx, gy = lax.axis_index("gx"), lax.axis_index("gy")
    send = ((sx0, sy0, sc0), (sx1, sy1, sc1))
    recv = ((rx0, ry0, rc0), (rx1, ry1, rc1))
    sems = (sem0, sem1)
    size_x, size_y = g_ref.shape[:2]
    own_x, own_y, ring = (size_x, size_x // 2), (size_y, size_y // 2), (3, 4)
    near_x = {-1: gx > 0, 0: None, 1: gx < nx - 1}
    near_y = {-1: gy > 0, 0: None, 1: gy < ny - 1}

    ways = []
    for dx, dy in ((-1, 0), (1, 0), (0, -1), (0, 1), (-1, -1), (-1, 1), (1, -1), (1, 1)):
        kind = 2 if dx and dy else (0 if dx else 1)
        side = {0: (dx + 1) // 2, 1: (dy + 1) // 2, 2: (dx + 1) + (dy + 1) // 2}[kind]
        if dx and dy:
            has = jnp.logical_and(near_x[dx], near_y[dy])
        else:
            has = near_x[dx] if dx else near_y[dy]
        target = {}
        if dx:
            target["gx"] = gx + dx
        if dy:
            target["gy"] = gy + dy
        ways.append((dx, dy, kind, side, has, target))
    back = (1, 0, 3, 2, 7, 6, 5, 4)

    loads = [
        pltpu.make_async_copy(ref, held.at[n], held_sem.at[n]) for n, ref in enumerate((c_ref, g_ref))
    ]
    for load in loads:
        load.start()

    barrier = pltpu.get_barrier_semaphore()
    for s in range(1, nx):
        pl.semaphore_signal(barrier, inc=1, device_id={"gx": lax.rem(gx + s, nx)}, device_id_type=MESH)
    for s in range(1, ny):
        pl.semaphore_signal(barrier, inc=1, device_id={"gy": lax.rem(gy + s, ny)}, device_id_type=MESH)
    for dx, dy, kind, side, has, target in ways[4:]:
        @pl.when(has)
        def _():
            pl.semaphore_signal(barrier, inc=1, device_id=target, device_id_type=MESH)

    for level in range(2):
        for dx, dy, kind, side, has, target in ways:
            @pl.when(jnp.logical_not(has))
            def _():
                ref = recv[level][kind]
                ref[:, side] = jnp.zeros((ref.shape[0],) + ref.shape[2:], F32)

    for ref in (d0, v0, g0, d1, v1, g1):
        ref[...] = jnp.zeros(ref.shape, F32)
    for c in range(2):
        k1[c, 0, 7] = jnp.zeros(k1.shape[3:], F32)

    size_z = 4 * LANES
    row, col = iota((size_z, size_z), 0), iota((size_z, size_z), 1)
    perm[...] = (row == 4 * (col % LANES) + col // LANES).astype(F32).astype(jnp.bfloat16)

    def unpack(ref):
        flat = permute(ref[...].reshape(-1, size_z), perm[...], 0)
        quarters = [flat[:, q * LANES : (q + 1) * LANES].reshape(ref.shape[0], ref.shape[1], LANES) for q in range(4)]
        pairs = [split_even(quarters[2 * b], quarters[2 * b + 1]) for b in range(2)]
        return [pairs[b][0] for b in range(2)], [pairs[b][1] for b in range(2)]

    def pack(ref, red, black):
        quarters = []
        for b in range(2):
            quarters.extend(split_even(red[b], black[b]))
        flat = jnp.concatenate([q.reshape(-1, LANES) for q in quarters], axis=1)
        ref[...] = permute(flat, perm[...], 1).reshape(ref.shape)

    def coarsen(red, black):
        pair = [pair_rows(red[b] + black[b]) for b in range(len(red))]
        if len(pair) == 1:
            return pair[0]
        first, second = split_even(pair[0], pair[1])
        return [first], [second]

    def copy(level, ph, d, count, into=False):
        dx, dy, kind, side, has, target = ways[d]
        lands = d if into else back[d]
        sem = sems[level]
        return pltpu.make_async_remote_copy(
            src_ref=send[level][kind].at[ph, side, pl.ds(0, count)],
            dst_ref=recv[level][kind].at[ph, ways[lands][3], pl.ds(0, count)],
            send_sem=sem.at[0, ph, d], recv_sem=sem.at[1, ph, lands], device_id=target, device_id_type=MESH)

    def span(step, own, width, edge):
        if step == 0:
            return slice(width, width + own)
        if edge == "send":
            return slice(width, 2 * width) if step < 0 else slice(own, own + width)
        return slice(0, width) if step < 0 else slice(width + own, 2 * width + own)

    def start(level, ph, fields, count=8):
        x, y, h = own_x[level], own_y[level], ring[level]
        for dx, dy, kind, side, has, target in ways[:count]:
            for f, ref in enumerate(fields):
                send[level][kind][ph, side, f] = ref[span(dx, x, h, "send"), span(dy, y, h, "send"), :]
        for d, way in enumerate(ways[:count]):
            @pl.when(way[4])
            def _():
                copy(level, ph, d, len(fields)).start()

    def finish(level, ph, fields, count=8):
        x, y, h = own_x[level], own_y[level], ring[level]
        for d, way in enumerate(ways[:count]):
            @pl.when(way[4])
            def _():
                copy(level, ph, d, len(fields), into=True).wait_recv()
                copy(level, ph, d, len(fields)).wait_send()
        for dx, dy, kind, side, has, target in ways[:count]:
            for f, ref in enumerate(fields):
                ref[span(dx, x, h, ""), span(dy, y, h, ""), :] = recv[level][kind][ph, side, f]

    def swap(level, ph, fields, count=8):
        start(level, ph, fields, count)
        finish(level, ph, fields, count)

    def both(ref):
        return [ref.at[c, b] for c in range(2) for b in range(ref.shape[1])]

    def black(ref):
        return [ref.at[1, b] for b in range(ref.shape[1])]

    def own(level, a):
        x, y, h = own_x[level], own_y[level], ring[level]
        return a[h : h + x, h : h + y]

    def place(level, ref, fields, add=False):
        x, y, h = own_x[level], own_y[level], ring[level]
        for c in range(2):
            for b, a in enumerate(fields[c]):
                if add:
                    a = a + ref[c, b, h : h + x, h : h + y]
                ref[c, b, h : h + x, h : h + y] = a

    def gather_copy(stage, s):
        if stage == 0:
            return pltpu.make_async_remote_copy(
                src_ref=ga.at[gx], dst_ref=ga.at[gx], send_sem=semx.at[0, s], recv_sem=semx.at[1, s],
                device_id={"gx": lax.rem(gx + s, nx)}, device_id_type=MESH)
        return pltpu.make_async_remote_copy(
            src_ref=gb.at[gy], dst_ref=gb.at[gy], send_sem=semy.at[0, s], recv_sem=semy.at[1, s],
            device_id={"gy": lax.rem(gy + s, ny)}, device_id_type=MESH)

    def gather(dens, source):
        ga[gx, 0] = dens
        ga[gx, 1] = source
        for s in range(1, nx):
            gather_copy(0, s).start()
        for s in range(1, nx):
            src = lax.rem(gx + nx - s, nx)
            pltpu.make_async_remote_copy(
                src_ref=ga.at[src], dst_ref=ga.at[src], send_sem=semx.at[0, s], recv_sem=semx.at[1, s],
                device_id={"gx": src}, device_id_type=MESH).wait_recv()
            gather_copy(0, s).wait_send()
        for i in range(nx):
            gb[gy, 0, 2 * i : 2 * i + 2] = ga[i, 0]
            gb[gy, 1, 2 * i : 2 * i + 2] = ga[i, 1]
        for s in range(1, ny):
            gather_copy(1, s).start()
        for s in range(1, ny):
            src = lax.rem(gy + ny - s, ny)
            pltpu.make_async_remote_copy(
                src_ref=gb.at[src], dst_ref=gb.at[src], send_sem=semy.at[0, s], recv_sem=semy.at[1, s],
                device_id={"gy": src}, device_id_type=MESH).wait_recv()
            gather_copy(1, s).wait_send()

    def setup(kref, dens, colour, scale):
        x0, x1 = 1, dens.shape[2] - 1
        for b, near in enumerate(around(dens, colour, x0, x1)):
            here = dens[colour, b, x0:x1]
            total = None
            for f in range(6):
                face = (scale * 0.5) * (here + near[f])
                kref[colour, b, f, x0:x1] = face
                total = face if total is None else total + face
            kref[colour, b, 6, x0:x1] = total
            kref[colour, b, 7, x0:x1] = jnp.where(here > 0.0, 1.0 / total, 0.0)

    def weigh(kref, v, colour, x0, x1):
        out = []
        for b, near in enumerate(around(v, colour, x0, x1)):
            total = kref[colour, b, 0, x0:x1] * near[0]
            for f in range(1, 6):
                total = total + kref[colour, b, f, x0:x1] * near[f]
            out.append(total)
        return out

    def update(kref, g, v, colour, x0, x1):
        for b, n in enumerate(weigh(kref, v, colour, x0, x1)):
            v[colour, b, x0:x1] = (g[colour, b, x0:x1] + n) * kref[colour, b, 7, x0:x1]

    def first(kref, g, v, x0, x1):
        for b in range(v.shape[1]):
            v[0, b, x0:x1] = g[0, b, x0:x1] * kref[0, b, 7, x0:x1]

    def residual(level, kref, g, v):
        h = ring[level]
        x0, x1 = h, h + own_x[level]
        out = []
        for c in range(2):
            n = weigh(kref, v, c, x0, x1)
            out.append([
                (g[c, b, x0:x1] - (kref[c, b, 6, x0:x1] * v[c, b, x0:x1] - n[b]))[:, h : h + own_y[level]]
                for b in range(len(n))])
        return out

    loads[0].wait()
    dens = unpack(held.at[0])
    place(0, d0, dens)
    dens_one = coarsen(*dens)
    place(1, d1, dens_one)
    loads[1].wait()
    place(0, g0, unpack(held.at[1]))

    beside_x = (gx > 0).astype(jnp.int32) + (gx < nx - 1).astype(jnp.int32)
    beside_y = (gy > 0).astype(jnp.int32) + (gy < ny - 1).astype(jnp.int32)
    pl.semaphore_wait(barrier, nx + ny - 2 + beside_x * beside_y)

    start(1, 0, both(d1))
    start(0, 0, both(d0))
    start(0, 1, both(g0))
    dens_two = coarsen(*dens_one)
    inverse = [k1.at[c, 0, 7] for c in range(2)]
    finish(1, 0, both(d1))
    for c in range(2):
        setup(k1, d1, c, 0.25)
    start(1, 1, inverse)
    finish(0, 0, both(d0))
    for c in range(2):
        setup(k0, d0, c, 1.0)
    finish(0, 1, both(g0))

    low, high = ring[0], ring[0] + size_x

    def fine_sweep(ph, last):
        more = 1 if last else 0
        swap(0, ph, black(v0))
        update(k0, g0, v0, 0, low - 1 - more, high + 1 + more)
        update(k0, g0, v0, 1, low - more, high + more)

    first(k0, g0, v0, low - 1, high + 1)
    update(k0, g0, v0, 1, low, high)
    for s in range(1, SWEEPS):
        fine_sweep(1 + s, s == SWEEPS - 1)
    place(1, g1, coarsen(*residual(0, k0, g0, v0)))

    start(1, 2, both(g1))
    finish(1, 1, inverse)
    finish(1, 2, both(g1))
    wide = v1.shape[2]
    first(k1, g1, v1, 0, wide)
    for s in range(1, 2 * SWEEPS):
        update(k1, g1, v1, s % 2, s, wide - s)
    start(1, 3, both(v1))
    source_two = coarsen(*residual(1, k1, g1, v1))

    gather(dens_two, source_two)
    for j in range(ny):
        cw[0, :, 2 * j : 2 * j + 2] = gb[j, 0]
        cw[1, :, 2 * j : 2 * j + 2] = gb[j, 1]

    def sides(a):
        plane = jnp.zeros_like(a[:1])
        line = jnp.zeros_like(a[:, :1])
        return (
            jnp.concatenate([plane, a[:-1]], axis=0), jnp.concatenate([a[1:], plane], axis=0),
            row_prev(a, line), row_next(a, line), lane_prev(a), lane_next(a))

    centre = cw[0]
    total = None
    for f, near in enumerate(sides(centre)):
        face = 0.03125 * (centre + near)
        k2[f] = face
        total = face if total is None else total + face
    k2[6] = 1.0 / total
    shape = centre.shape
    red_two = (iota(shape, 0) + iota(shape, 1) + iota(shape, 2)) % 2 == 0
    cw[0] = jnp.zeros(shape, F32)

    def half(red):
        field = cw[0]
        total = cw[1]
        for f, near in enumerate(sides(field)):
            total = total + k2[f] * near
        total = total * k2[6]
        cw[0] = jnp.where(red_two, total, field) if red else jnp.where(red_two, field, total)

    def sweep(i, carry):
        half(True)
        half(False)
        return carry

    lax.fori_loop(0, COARSE_SWEEPS, sweep, 0)
    field = cw[0]
    vc[...] = jnp.zeros(vc.shape, F32)
    for j in range(ny):
        vc[1 + j, 2 : 2 + 2 * nx] = field[:, 2 * j : 2 * j + 2]
    finish(1, 3, both(v1))
    for dy in range(3):
        add = double_rows(vc[gy + dy, pl.ds(2 * gx, 6)])
        for c in range(2):
            v1[c, 0, :, 4 * dy : 4 * dy + 4] = v1[c, 0, :, 4 * dy : 4 * dy + 4] + add
    for s in range(2 * SWEEPS):
        update(k1, g1, v1, s % 2, s + 1, wide - s - 1)

    adds = [double_rows(a) for a in split_even(own(1, v1[0, 0]), own(1, v1[1, 0]))]
    place(0, v0, [adds, adds], add=True)
    for s in range(SWEEPS):
        fine_sweep(2 + SWEEPS + s, s == SWEEPS - 1)
    pack(v_out, *[[own(0, v0[c, b]) for b in range(2)] for c in range(2)])
    pack(r_out, *residual(0, k0, g0, v0))


def hand_out(v_ref, r_ref, v_out, r_out, sem):
    copies = [
        pltpu.make_async_copy(src, dst, sem.at[n]) for n, (src, dst) in enumerate(((v_ref, v_out), (r_ref, r_out)))
    ]
    for copy in copies:
        copy.start()
    for copy in copies:
        copy.wait()


def solution(mesh):
    nx, ny = mesh.shape["gx"], mesh.shape["gy"]

    def shards(right_side, inverse_density):
        x, y, z = right_side.shape
        p0, p1 = 3 + 2 * SWEEPS, 4

        def halo(phases, fields, own_x, own_y, ring):
            return [
                pltpu.VMEM((phases, 2, fields, ring, own_y, LANES), F32),
                pltpu.VMEM((phases, 2, fields, own_x, ring, LANES), F32),
                pltpu.VMEM((phases, 4, fields, ring, ring, LANES), F32),
            ]

        def level(groups, rows):
            field = pltpu.VMEM((2, groups, rows, REGION_Y, LANES), F32)
            return [pltpu.VMEM((2, groups, 8, rows, REGION_Y, LANES), F32), field, field, field]

        halo0 = halo(p0, 4, x, y, 3)
        halo1 = halo(p1, 2, x // 2, y // 2, 4)
        out = pltpu.VMEM(right_side.shape, F32)
        v, r = pl.pallas_call(
            functools.partial(kernel, nx, ny),
            out_shape=(out, out),
            in_specs=[pl.BlockSpec(memory_space=pltpu.HBM)] * 2,
            out_specs=(pl.BlockSpec(memory_space=pltpu.VMEM),) * 2,
            scratch_shapes=[
                pltpu.VMEM((z, z), jnp.bfloat16),
                *level(2, x + 6),
                *level(1, x // 2 + 8),
                pltpu.VMEM((7, nx * x // 4, ny * y // 4, LANES), F32),
                *halo0, *halo0, *halo1, *halo1,
                pltpu.VMEM((nx, 2, x // 4, y // 4, LANES), F32),
                pltpu.VMEM((ny, 2, nx * x // 4, y // 4, LANES), F32),
                pltpu.VMEM((ny + 2, nx * x // 4 + 4, y // 4, LANES), F32),
                pltpu.VMEM((2, nx * x // 4, ny * y // 4, LANES), F32),
                pltpu.VMEM((2, x, y, z), F32),
                pltpu.SemaphoreType.DMA((2, p0, 8)),
                pltpu.SemaphoreType.DMA((2, p1, 8)),
                pltpu.SemaphoreType.DMA((2, nx)),
                pltpu.SemaphoreType.DMA((2, ny)),
                pltpu.SemaphoreType.DMA((2,)),
            ],
            compiler_params=pltpu.CompilerParams(
                collective_id=0, has_side_effects=True, vmem_limit_bytes=24 * 1024 * 1024
            ),
        )(*(pltpu.with_memory_space_constraint(a, pltpu.HBM) for a in (right_side, inverse_density)))
        res = jax.ShapeDtypeStruct(right_side.shape, F32)
        return pl.pallas_call(
            hand_out,
            out_shape=(res, res),
            in_specs=[pl.BlockSpec(memory_space=pltpu.VMEM)] * 2,
            out_specs=(pl.BlockSpec(memory_space=pl.ANY),) * 2,
            scratch_shapes=[pltpu.SemaphoreType.DMA((2,))],
            compiler_params=pltpu.CompilerParams(vmem_limit_bytes=1024 * 1024),
        )(v, r)

    spec = P("gx", "gy", None)
    return jax.shard_map(shards, mesh=mesh, in_specs=(spec, spec), out_specs=(spec, spec), check_vma=False)
```

```python
import functools

import jax
import jax.numpy as jnp
from jax import lax
from jax.experimental import pallas as pl
from jax.experimental.pallas import tpu as pltpu
from jax.sharding import PartitionSpec as P

SWEEPS = 2
COARSE_SWEEPS = 8
MESH = pl.DeviceIdType.MESH
LANES = 128
F32 = jnp.float32

FINE, MID = 16, (20, 24)

WAYS = ((-1, 0), (1, 0), (0, -1), (0, 1), (-1, -1), (-1, 1), (1, -1), (1, 1),
        (-2, 0), (2, 0), (0, -2), (0, 2),
        (-2, -1), (-2, 1), (2, -1), (2, 1), (-1, -2), (-1, 2), (1, -2), (1, 2))
BACK = tuple(WAYS.index((-dy, -dx)) for dy, dx in WAYS)
YS, XS, CORNERS, NEAR = (0, 1), (2, 3), (4, 5, 6, 7), range(8)


def iota(shape, dim):
    return lax.broadcasted_iota(jnp.int32, shape, dim)


def lane_prev(a):
    return jnp.where(iota(a.shape, 2) == 0, 0.0, pltpu.roll(a, 1, 2))


def lane_next(a):
    return jnp.where(iota(a.shape, 2) == LANES - 1, 0.0, pltpu.roll(a, LANES - 1, 2))


def even_cells(shape):
    return (iota(shape, 0) + iota(shape, 1)) % 2 == 0


def z_other(o, colour, first):
    shape = o[0].shape
    even = (iota(shape, 0) + iota(shape, 1)) % 2 == first % 2
    low = even if colour == 0 else jnp.logical_not(even)
    last = len(o) - 1
    out = []
    for b in range(last + 1):
        before = o[b - 1] if b > 0 else lane_prev(o[last])
        after = o[b + 1] if b < last else lane_next(o[0])
        out.append(jnp.where(low, before, after))
    return out


def around(other, colour, y0, y1, rows):
    groups = range(other.shape[0])
    mid = [other[b, y0:y1, 0:rows] for b in groups]
    zo = z_other(mid, colour, y0)
    return [
        (
            other[b, y0 - 1 : y1 - 1, 0:rows],
            other[b, y0 + 1 : y1 + 1, 0:rows],
            pltpu.roll(mid[b], 1, 1),
            pltpu.roll(mid[b], rows - 1, 1),
            mid[b],
            zo[b],
        )
        for b in groups
    ]


def split_even(zero, one):
    even = even_cells(zero.shape)
    return jnp.where(even, zero, one), jnp.where(even, one, zero)


def pair_rows(a):
    rows = a.shape[1] // 2
    a = a.reshape(a.shape[0] // 2, 2, a.shape[1], LANES)
    a = a[:, 0] + a[:, 1]
    pick = iota((a.shape[0], rows, LANES), 1)
    out = a[:, 0:1] + a[:, 1:2]
    out = jnp.broadcast_to(out, pick.shape)
    for j in range(1, rows):
        out = jnp.where(pick == j, a[:, 2 * j : 2 * j + 1] + a[:, 2 * j + 1 : 2 * j + 2], out)
    return out * 0.125


def double_rows(a, order):
    y = a.shape[0]
    pick = iota((y, 2 * len(order), LANES), 1) // 2
    out = jnp.broadcast_to(a[:, order[0] : order[0] + 1], pick.shape)
    for n, j in enumerate(order[1:], 1):
        out = jnp.where(pick == n, a[:, j : j + 1], out)
    return jnp.concatenate([out[i // 2 : i // 2 + 1] for i in range(2 * y)], axis=0)


def three(x):
    high = x.astype(jnp.bfloat16)
    rest = x - high.astype(F32)
    middle = rest.astype(jnp.bfloat16)
    low = (rest - middle.astype(F32)).astype(jnp.bfloat16)
    return jnp.concatenate([high, middle, low], axis=0)


def permute(x, matrix, side):
    n = x.shape[0]
    out = lax.dot_general(three(x), matrix, (((1,), (side,)), ((), ())), preferred_element_type=F32)
    return (out[0:n] + out[n : 2 * n]) + out[2 * n :]


def y_own(d, w):
    return slice(4, 12) if d == 0 else (slice(12 - w, 12) if d > 0 else slice(4, 4 + w))


def y_halo(d, w):
    return slice(4, 12) if d == 0 else (slice(12, 12 + w) if d > 0 else slice(4 - w, 4))


def x_own(d, w):
    return slice(0, 8) if d == 0 else (slice(8 - w, 8) if d > 0 else slice(0, w))


def x_halo(d, w):
    return slice(0, 8) if d == 0 else (slice(8, 8 + w) if d > 0 else slice(FINE - w, FINE))


def block_part(way, far):
    dy, dx = WAYS[way]
    n = far if abs(dy) == 2 else (2 if abs(dx) == 2 and dy else 4)
    return slice(0, n) if dy > 0 else slice(4 - n, 4)


def kernel(nx, ny, g_ref, c_ref, v_out, r_out, perm, held, d0, g0, k0, ra, ba, rb, bb, bp, rc, bc, rd, bd,
           ax_s, ax_r, gx_s, gx_r, ac_s, ac_r, sx_s, sx_r, sc_s, sc_r, ex_s, ex_r, ec_s, ec_r,
           d1, g1, k1, mr, mb, mp, blk_c, blk_g, blk_x, in_c, in_g, in_x,
           gat, cc, kc, vc, held_sem, sem_a, sem_s, sem_m, sem_g):
    gx, gy = lax.axis_index("gx"), lax.axis_index("gy")

    def inside(way):
        dy, dx = WAYS[way]
        tests = []
        if dy:
            tests.append(gy + dy >= 0 if dy < 0 else gy + dy < ny)
        if dx:
            tests.append(gx + dx >= 0 if dx < 0 else gx + dx < nx)
        return tests[0] if len(tests) == 1 else jnp.logical_and(*tests)

    def device(way):
        dy, dx = WAYS[way]
        out = {}
        if dx:
            out["gx"] = gx + dx
        if dy:
            out["gy"] = gy + dy
        return out

    has = [inside(way) for way in range(len(WAYS))]
    target = [device(way) for way in range(len(WAYS))]

    def each_peer(fn):
        if nx * ny <= 64:
            for s in range(1, nx * ny):
                fn(s, s // ny, s % ny)
        else:
            def body(s, carry):
                fn(s, s // ny, lax.rem(s, ny))
                return carry
            lax.fori_loop(1, nx * ny, body, 0)

    loads = [
        pltpu.make_async_copy(ref, held.at[n], held_sem.at[n]) for n, ref in enumerate((c_ref, g_ref))
    ]
    for load in loads:
        load.start()

    barrier = pltpu.get_barrier_semaphore()

    def greet(s, sx, sy):
        pl.semaphore_signal(
            barrier, inc=1, device_id={"gx": lax.rem(gx + sx, nx), "gy": lax.rem(gy + sy, ny)}, device_id_type=MESH)

    each_peer(greet)

    for way in range(len(WAYS)):
        @pl.when(jnp.logical_not(has[way]))
        def _():
            dy, dx = WAYS[way]
            for ref in (in_c, in_g, in_x):
                ref[way] = jnp.zeros(ref.shape[1:], F32)
            if way in YS:
                for ref in (d0, g0):
                    ref[:, :, y_halo(dy, 3), 0:8] = jnp.zeros((2, 2, 3, 8, LANES), F32)
                for ref in (ba, bp, rd):
                    ref[:, y_halo(dy, 3), 0:8] = jnp.zeros((2, 3, 8, LANES), F32)
            if way in XS:
                for ref in (ax_r, gx_r, ex_r):
                    ref[way - 2] = jnp.zeros(ref.shape[1:], F32)
                for n in range(2):
                    sx_r[n, way - 2] = jnp.zeros(sx_r.shape[2:], F32)
            if way in CORNERS:
                for ref in (ac_r, ec_r):
                    ref[way - 4] = jnp.zeros(ref.shape[1:], F32)
                for n in range(2):
                    sc_r[n, way - 4] = jnp.zeros(sc_r.shape[2:], F32)
    vc[...] = jnp.zeros(vc.shape, F32)

    size_z = 4 * LANES
    row, col = iota((size_z, size_z), 0), iota((size_z, size_z), 1)
    perm[...] = (row == 4 * (col % LANES) + col // LANES).astype(F32).astype(jnp.bfloat16)

    def coarsen(red, black):
        pair = [pair_rows(red[b] + black[b]) for b in range(len(red))]
        if len(pair) == 1:
            return pair[0]
        first, second = split_even(pair[0], pair[1])
        return [first], [second]

    def remote(sem, slot, way, src, dst):
        return pltpu.make_async_remote_copy(
            src_ref=src, dst_ref=dst, send_sem=sem.at[(0, *slot, way)], recv_sem=sem.at[(1, *slot, BACK[way])],
            device_id=target[way], device_id_type=MESH)

    def arrival(sem, slot, way, src, dst):
        return pltpu.make_async_remote_copy(
            src_ref=src, dst_ref=dst, send_sem=sem.at[(0, *slot, way)], recv_sem=sem.at[(1, *slot, way)],
            device_id=target[way], device_id_type=MESH)

    def ring_messages(n, src, dst, w, x_s, x_r, c_s, c_r):
        out = []
        for way in YS:
            dy = WAYS[way][0]
            out.append(((n,), way, src.at[:, y_own(dy, w), 0:8], dst.at[:, y_halo(-dy, w), 0:8], dst.at[:, y_halo(dy, w), 0:8]))
        for way in XS:
            out.append(((n,), way, x_s.at[way - 2], x_r.at[BACK[way] - 2], x_r.at[way - 2]))
        for way in CORNERS:
            out.append(((n,), way, c_s.at[way - 4], c_r.at[BACK[way] - 4], c_r.at[way - 4]))
        return out

    def ring_pack(src, w, cw, x_s, c_s):
        for way in XS:
            x_s[way - 2] = src[:, 4:12, x_own(WAYS[way][1], w)]
        for way in CORNERS:
            dy, dx = WAYS[way]
            c_s[way - 4] = src[:, y_own(dy, cw), x_own(dx, cw)]

    def ring_unpack(dst, w, cw, x_r, c_r):
        for way in XS:
            dst[:, 4:12, x_halo(WAYS[way][1], w)] = x_r[way - 2]
        for way in CORNERS:
            dy, dx = WAYS[way]
            dst[:, y_halo(dy, cw), x_halo(dx, cw)] = c_r[way - 4]

    def messages_a():
        out = []
        for way in YS:
            dy = WAYS[way][0]
            for slot, (ref, colour, w) in enumerate(((d0, 0, 2), (g0, 0, 2), (d0, 1, 3), (g0, 1, 1))):
                out.append(((slot,), way, ref.at[colour, :, y_own(dy, w), 0:8],
                            ref.at[colour, :, y_halo(-dy, w), 0:8], ref.at[colour, :, y_halo(dy, w), 0:8]))
        for way in XS:
            out.append(((0,), way, ax_s.at[way - 2], ax_r.at[BACK[way] - 2], ax_r.at[way - 2]))
            out.append(((1,), way, gx_s.at[way - 2], gx_r.at[BACK[way] - 2], gx_r.at[way - 2]))
        for way in CORNERS:
            out.append(((0,), way, ac_s.at[way - 4], ac_r.at[BACK[way] - 4], ac_r.at[way - 4]))
        return out

    def block_messages(n, src, dst, ways, far):
        out = []
        for way in ways:
            give, take = block_part(BACK[way], far), block_part(way, far)
            lead = (slice(None),) * (len(src.shape) - 3)
            out.append(((n,), way, src.at[(*lead, give)], dst.at[(BACK[way], *lead, give)], dst.at[(way, *lead, take)]))
        return out

    def by_way(messages):
        ways = {}
        for m in messages:
            ways.setdefault(m[1], []).append(m)
        return ways.items()

    sent = []

    def start(sem, messages):
        for way, group in by_way(messages):
            @pl.when(has[way])
            def _():
                for slot, _, src, there, here in group:
                    remote(sem, slot, way, src, there).start()
        sent.append((sem, messages))

    def finish(sem, messages):
        for way, group in by_way(messages):
            @pl.when(has[way])
            def _():
                for slot, _, src, there, here in group:
                    arrival(sem, slot, way, src, here).wait_recv()

    def all_sent():
        for sem, messages in sent:
            for way, group in by_way(messages):
                @pl.when(has[way])
                def _():
                    for slot, _, src, there, here in group:
                        remote(sem, slot, way, src, there).wait_send()
        sent.clear()

    def spread(n, send):
        def body(s, sx, sy):
            to = {"gx": lax.rem(gx + sx, nx), "gy": lax.rem(gy + sy, ny)}
            copy = pltpu.make_async_remote_copy(
                src_ref=gat.at[n, gx, gy], dst_ref=gat.at[n, gx, gy], send_sem=sem_g.at[0, n, s],
                recv_sem=sem_g.at[1, n, s], device_id=to, device_id_type=MESH)
            if send:
                copy.start()
            else:
                copy.wait_send()
        each_peer(body)

    def gathered(n):
        def body(s, sx, sy):
            fx, fy = lax.rem(gx + nx - sx, nx), lax.rem(gy + ny - sy, ny)
            pltpu.make_async_remote_copy(
                src_ref=gat.at[n, fx, fy], dst_ref=gat.at[n, fx, fy], send_sem=sem_g.at[0, n, s],
                recv_sem=sem_g.at[1, n, s], device_id={"gx": fx, "gy": fy}, device_id_type=MESH).wait_recv()
        each_peer(body)

    def setup(kref, dens, colour, scale, y0, y1, rows):
        for b, near in enumerate(around(dens.at[1 - colour], colour, y0, y1, rows)):
            here = dens[colour, b, y0:y1, 0:rows]
            total = None
            for f in range(6):
                face = (scale * 0.5) * (here + near[f])
                kref[colour, b, f, y0:y1, 0:rows] = face
                total = face if total is None else total + face
            kref[colour, b, 6, y0:y1, 0:rows] = total
            kref[colour, b, 7, y0:y1, 0:rows] = jnp.where(here > 0.0, 1.0 / total, 0.0)

    def weigh(kref, other, colour, y0, y1, rows):
        out = []
        for b, near in enumerate(around(other, colour, y0, y1, rows)):
            total = kref[colour, b, 0, y0:y1, 0:rows] * near[0]
            for f in range(1, 6):
                total = total + kref[colour, b, f, y0:y1, 0:rows] * near[f]
            out.append(total)
        return out

    def update(kref, g, other, dst, colour, y0, y1, rows):
        for b, n in enumerate(weigh(kref, other, colour, y0, y1, rows)):
            dst[b, y0:y1, 0:rows] = (g[colour, b, y0:y1, 0:rows] + n) * kref[colour, b, 7, y0:y1, 0:rows]

    def first(kref, g, dst, y0, y1, rows):
        for b in range(dst.shape[0]):
            dst[b, y0:y1, 0:rows] = g[0, b, y0:y1, 0:rows] * kref[0, b, 7, y0:y1, 0:rows]

    def residual(kref, g, red, black, y0, y1, rows, x0, x1):
        out = []
        for c, (v, other) in enumerate(((red, black), (black, red))):
            n = weigh(kref, other, c, y0, y1, rows)
            out.append([
                (g[c, b, y0:y1, 0:rows] - (kref[c, b, 6, y0:y1, 0:rows] * v[b, y0:y1, 0:rows] - n[b]))[:, x0:x1]
                for b in range(len(n))])
        return out

    for load in loads:
        load.wait()
    flat = permute(held[...].reshape(-1, size_z), perm[...], 0)

    def fields(flat):
        quarters = [
            jnp.swapaxes(flat[:, q * LANES : (q + 1) * LANES].reshape(8, 8, LANES), 0, 1) for q in range(4)]
        pairs = [split_even(quarters[2 * b], quarters[2 * b + 1]) for b in range(2)]
        return [pairs[b][0] for b in range(2)], [pairs[b][1] for b in range(2)]

    dens, source = fields(flat[0:64]), fields(flat[64:128])
    for c in range(2):
        for b in range(2):
            d0[c, b, 4:12, 0:8] = dens[c][b]
            g0[c, b, 4:12, 0:8] = source[c][b]
    for way in XS:
        dx = WAYS[way][1]
        for c in range(2):
            ax_s[way - 2, c] = d0[c, :, 4:12, x_own(dx, 3)]
            gx_s[way - 2, c] = g0[c, :, 4:12, x_own(dx, 2)]
    for way in CORNERS:
        dy, dx = WAYS[way]
        for b in range(2):
            ac_s[way - 4, 2 * b : 2 * b + 2] = d0[1, b, y_own(dy, 2), x_own(dx, 2)]
            ac_s[way - 4, 4:5, b : b + 1] = d0[0, b, y_own(dy, 1), x_own(dx, 1)]
            ac_s[way - 4, 5:6, b : b + 1] = g0[0, b, y_own(dy, 1), x_own(dx, 1)]
    dens_one = coarsen(*dens)
    for c in range(2):
        blk_c[c] = dens_one[c][0]
        d1[c, 0, 8:12, 8:12] = dens_one[c][0]
    gat[0, gx, gy] = coarsen(*dens_one)

    pl.semaphore_wait(barrier, nx * ny - 1)
    start(sem_a, messages_a())
    finish(sem_a, messages_a())
    for way in XS:
        dx = WAYS[way][1]
        for c in range(2):
            d0[c, :, 4:12, x_halo(dx, 3)] = ax_r[way - 2, c]
            g0[c, :, 4:12, x_halo(dx, 2)] = gx_r[way - 2, c]
    for way in CORNERS:
        dy, dx = WAYS[way]
        for b in range(2):
            d0[1, b, y_halo(dy, 2), x_halo(dx, 2)] = ac_r[way - 4, 2 * b : 2 * b + 2]
            d0[0, b, y_halo(dy, 1), x_halo(dx, 1)] = ac_r[way - 4, 4:5, b : b + 1]
            g0[0, b, y_halo(dy, 1), x_halo(dx, 1)] = ac_r[way - 4, 5:6, b : b + 1]

    setup(k0, d0, 0, 1.0, 2, 14, FINE)
    setup(k0, d0, 1, 1.0, 3, 13, FINE)
    first(k0, g0, ra, 3, 13, FINE)
    update(k0, g0, ra, ba, 1, 4, 12, FINE)
    ring_pack(ba, 3, 2, sx_s.at[0], sc_s.at[0])
    swap = ring_messages(0, ba, ba, 3, sx_s.at[0], sx_r.at[0], sc_s.at[0], sc_r.at[0])
    start(sem_s, swap)
    part_c = block_messages(0, blk_c, in_c, range(20), 2)
    start(sem_m, part_c)
    spread(0, True)
    finish(sem_s, swap)
    ring_unpack(ba, 3, 2, sx_r.at[0], sc_r.at[0])
    update(k0, g0, ba, rb, 0, 2, 14, FINE)
    update(k0, g0, rb, bb, 1, 3, 13, FINE)
    source_one = coarsen(*residual(k0, g0, rb, bb, 4, 12, FINE, 0, 8))
    for c in range(2):
        blk_g[c] = source_one[c][0]
        g1[c, 0, 8:12, 8:12] = source_one[c][0]
    part_g = block_messages(1, blk_g, in_g, NEAR, 1)
    far_g = block_messages(1, blk_g, in_g, range(8, 12), 1)
    start(sem_m, part_g)
    start(sem_m, far_g)
    ring_pack(bb, 3, 2, sx_s.at[1], sc_s.at[1])
    keep = ring_messages(1, bb, bp, 3, sx_s.at[1], sx_r.at[1], sc_s.at[1], sc_r.at[1])
    start(sem_s, keep)

    def blocks(ref, got, ways, far):
        for way in ways:
            dy, dx = WAYS[way]
            part = block_part(way, far)
            y, x = 4 * (dy + 2), 4 * (dx + 2)
            for c in range(2):
                ref[c, 0, y + part.start : y + part.stop, x : x + 4] = got[way, c, part]

    finish(sem_m, part_c)
    blocks(d1, in_c, range(20), 2)
    for c in range(2):
        setup(k1, d1, c, 0.25, 1, 19, MID[1])

    gathered(0)
    pairs, rows = ny, 2 * nx

    def assemble(n):
        for i in range(nx):
            for p in range(2):
                cc[p, :, 2 * i : 2 * i + 2] = gat[n, i, :, p]
        even = (iota((pairs, rows, LANES), 1) + iota((pairs, rows, LANES), 2)) % 2 == 0
        return jnp.where(even, cc[0], cc[1]), jnp.where(even, cc[1], cc[0])

    shape = (pairs, rows, LANES)
    tested = (iota(shape, 1) + iota(shape, 2)) % 2

    def beside(other, colour):
        low = tested == colour
        return (
            jnp.where(low, jnp.concatenate([other[-1:], other[:-1]], axis=0), other),
            jnp.where(low, other, jnp.concatenate([other[1:], other[:1]], axis=0)),
            pltpu.roll(other, 1, 1), pltpu.roll(other, rows - 1, 1),
            pltpu.roll(other, 1, 2), pltpu.roll(other, LANES - 1, 2))

    centre = assemble(0)
    for c in range(2):
        low = tested == c
        edges = (
            jnp.logical_and(low, iota(shape, 0) == 0),
            jnp.logical_and(jnp.logical_not(low), iota(shape, 0) == pairs - 1),
            iota(shape, 1) == 0, iota(shape, 1) == rows - 1, iota(shape, 2) == 0, iota(shape, 2) == LANES - 1)
        total, faces = None, []
        for near, edge in zip(beside(centre[1 - c], c), edges):
            face = 0.03125 * (centre[c] + jnp.where(edge, 0.0, near))
            total = face if total is None else total + face
            faces.append(face)
        inverse = 1.0 / total
        for f in range(6):
            kc[c, f] = jnp.where(edges[f], 0.0, faces[f] * inverse)
        kc[c, 6] = inverse

    finish(sem_m, part_g)
    blocks(g1, in_g, NEAR, 1)
    first(k1, g1, mr, 4, 16, 16)
    update(k1, g1, mr, mb, 1, 5, 15, 16)
    update(k1, g1, mb, mr, 0, 6, 14, 16)
    update(k1, g1, mr, mb, 1, 7, 13, 16)
    gat[1, gx, gy] = coarsen(*residual(k1, g1, mr, mb, 8, 12, 16, 8, 12))
    spread(1, True)
    blk_x[...] = mb[0, 8:12, 8:12]
    part_x = block_messages(2, blk_x, in_x, range(20), 2)
    start(sem_m, part_x)

    gathered(1)
    right = assemble(1)
    for c in range(2):
        kc[c, 7] = right[c] * kc[c, 6]

    def half(other, colour):
        total = kc[colour, 7]
        for f, near in enumerate(beside(other, colour)):
            total = total + kc[colour, f] * near
        return total

    def sweep(i, carry):
        red = half(carry[1], 0)
        return red, half(red, 1)

    red = kc[0, 7]
    red, black = lax.fori_loop(1, COARSE_SWEEPS, sweep, (red, half(red, 1)))
    even = tested == 0
    for i in range(nx):
        cut = slice(2 * i, 2 * i + 2)
        vc[2 + i, 2 : 2 + ny, 0] = jnp.where(even, red, black)[:, cut]
        vc[2 + i, 2 : 2 + ny, 1] = jnp.where(even, black, red)[:, cut]

    finish(sem_m, part_x)
    finish(sem_m, far_g)
    blocks(g1, in_g, range(8, 12), 1)
    mp[0, 8:12, 8:12] = blk_x[...]
    for way in range(20):
        dy, dx = WAYS[way]
        part = block_part(way, 2)
        y, x = 4 * (dy + 2), 4 * (dx + 2)
        mp[0, y + part.start : y + part.stop, x : x + 4] = in_x[way, part]
    for dx in range(5):
        window = vc[gx + dx, pl.ds(gy, 5)].reshape(10, 2, LANES)
        mp[0, :, 4 * dx : 4 * dx + 4] = mp[0, :, 4 * dx : 4 * dx + 4] + double_rows(window, (0, 1))
    update(k1, g1, mp, mr, 0, 3, 17, MID[1])
    update(k1, g1, mr, mb, 1, 4, 16, MID[1])
    update(k1, g1, mb, mr, 0, 5, 15, MID[1])
    update(k1, g1, mr, mb, 1, 6, 14, MID[1])

    finish(sem_s, keep)
    bp[:, 4:12, 0:8] = bb[:, 4:12, 0:8]
    ring_unpack(bp, 3, 2, sx_r.at[1], sc_r.at[1])
    half_z = split_even(mr[0, 6:14], mb[0, 6:14])
    for b in range(2):
        bp[b] = bp[b] + double_rows(half_z[b], (8, 9, 10, 11, 12, 13, 6, 7))
    update(k0, g0, bp, rc, 0, 2, 14, FINE)
    update(k0, g0, rc, bc, 1, 3, 13, FINE)
    update(k0, g0, bc, rd, 0, 4, 12, FINE)
    ring_pack(rd, 2, 1, ex_s, ec_s)
    last = ring_messages(2, rd, rd, 2, ex_s, ex_r, ec_s, ec_r)
    all_sent()
    for n in range(2):
        spread(n, False)
    start(sem_s, last)
    finish(sem_s, last)
    ring_unpack(rd, 2, 1, ex_r, ec_r)
    update(k0, g0, rd, bd, 1, 3, 13, FINE)
    left = residual(k0, g0, rd, bd, 4, 12, FINE, 0, 8)

    def lay(red, black):
        quarters = []
        for b in range(2):
            quarters.extend(split_even(red[b], black[b]))
        return jnp.concatenate([jnp.swapaxes(q, 0, 1).reshape(64, LANES) for q in quarters], axis=1)

    field = [[ref[b, 4:12, 0:8] for b in range(2)] for ref in (rd, bd)]
    flat = permute(jnp.concatenate([lay(*field), lay(*left)], axis=0), perm[...], 1)
    v_out[...] = flat[0:64].reshape(v_out.shape)
    r_out[...] = flat[64:128].reshape(r_out.shape)
    all_sent()


def hand_out(v_ref, r_ref, v_out, r_out, sem):
    copies = [
        pltpu.make_async_copy(src, dst, sem.at[n]) for n, (src, dst) in enumerate(((v_ref, v_out), (r_ref, r_out)))
    ]
    for copy in copies:
        copy.start()
    for copy in copies:
        copy.wait()


def solution(mesh):
    nx, ny = mesh.shape["gx"], mesh.shape["gy"]

    def shards(right_side, inverse_density):
        x, y, z = right_side.shape
        assert (x, y, z) == (8, 8, 4 * LANES)

        def vmem(*shape):
            return pltpu.VMEM((*shape, LANES), F32)

        fine = (2, FINE, FINE)
        mid = (1, *MID)
        result = pltpu.VMEM(right_side.shape, F32)
        v, r = pl.pallas_call(
            functools.partial(kernel, nx, ny),
            out_shape=(result, result),
            in_specs=[pl.BlockSpec(memory_space=pl.ANY)] * 2,
            out_specs=(pl.BlockSpec(memory_space=pltpu.VMEM),) * 2,
            scratch_shapes=[
                pltpu.VMEM((z, z), jnp.bfloat16),
                pltpu.VMEM((2, x, y, z), F32),
                vmem(2, *fine), vmem(2, *fine), vmem(2, 2, 8, FINE, FINE),
                *[vmem(*fine)] * 9,
                *[vmem(2, 2, 2, 8, 3)] * 2, *[vmem(2, 2, 2, 8, 2)] * 2, *[vmem(4, 6, 2)] * 2,
                *[vmem(2, 2, 2, 8, 3)] * 2, *[vmem(2, 4, 2, 2, 2)] * 2,
                *[vmem(2, 2, 8, 2)] * 2, *[vmem(4, 2, 1, 1)] * 2,
                vmem(2, *mid), vmem(2, *mid), vmem(2, 1, 8, *MID), *[vmem(*mid)] * 3,
                vmem(2, 4, 4), vmem(2, 4, 4), vmem(4, 4),
                vmem(len(WAYS), 2, 4, 4), vmem(len(WAYS), 2, 4, 4), vmem(len(WAYS), 4, 4),
                vmem(2, nx, ny, 2, 2), vmem(2, ny, 2 * nx), vmem(2, 8, ny, 2 * nx), vmem(nx + 4, ny + 4, 2, 2),
                pltpu.SemaphoreType.DMA((2,)),
                pltpu.SemaphoreType.DMA((2, 4, 8)),
                pltpu.SemaphoreType.DMA((2, 3, 8)),
                pltpu.SemaphoreType.DMA((2, 3, len(WAYS))),
                pltpu.SemaphoreType.DMA((2, 2, nx * ny)),
            ],
            compiler_params=pltpu.CompilerParams(
                collective_id=0, has_side_effects=True, vmem_limit_bytes=40 * 1024 * 1024
            ),
        )(*(pltpu.with_memory_space_constraint(a, pltpu.HBM) for a in (right_side, inverse_density)))
        out = jax.ShapeDtypeStruct(right_side.shape, F32)
        return pl.pallas_call(
            hand_out,
            out_shape=(out, out),
            in_specs=[pl.BlockSpec(memory_space=pltpu.VMEM)] * 2,
            out_specs=(pl.BlockSpec(memory_space=pl.ANY),) * 2,
            scratch_shapes=[pltpu.SemaphoreType.DMA((2,))],
            compiler_params=pltpu.CompilerParams(vmem_limit_bytes=1024 * 1024),
        )(v, r)

    spec = P("gx", "gy", None)
    return jax.shard_map(shards, mesh=mesh, in_specs=(spec, spec), out_specs=(spec, spec), check_vma=False)
```

```python
import functools
import math

import jax
import jax.numpy as jnp
from jax import lax
from jax.experimental import pallas as pl
from jax.experimental.pallas import tpu as pltpu
from jax.sharding import PartitionSpec as P

SWEEPS = 2
COARSE_SWEEPS = 8
MESH = pl.DeviceIdType.MESH
LANES = 128
F32 = jnp.float32

FINE, MID = 16, (20, 24)

WAYS = ((-1, 0), (1, 0), (0, -1), (0, 1), (-1, -1), (-1, 1), (1, -1), (1, 1),
        (-2, 0), (2, 0), (0, -2), (0, 2),
        (-2, -1), (-2, 1), (2, -1), (2, 1), (-1, -2), (-1, 2), (1, -2), (1, 2))
BACK = tuple(WAYS.index((-dy, -dx)) for dy, dx in WAYS)
ARGS, SWAP, KEEP, LAST, MID_C, MID_G, FAR_G, MID_X = range(8)
GATHER = (8, 9)
PHASES = 10
YS, XS, CORNERS, NEAR = (0, 1), (2, 3), (4, 5, 6, 7), range(8)


def iota(shape, dim):
    return lax.broadcasted_iota(jnp.int32, shape, dim)


def lane_prev(a):
    return jnp.where(iota(a.shape, 2) == 0, 0.0, pltpu.roll(a, 1, 2))


def lane_next(a):
    return jnp.where(iota(a.shape, 2) == LANES - 1, 0.0, pltpu.roll(a, LANES - 1, 2))


def even_cells(shape):
    return (iota(shape, 0) + iota(shape, 1)) % 2 == 0


def z_other(o, colour, first):
    shape = o[0].shape
    even = (iota(shape, 0) + iota(shape, 1)) % 2 == first % 2
    low = even if colour == 0 else jnp.logical_not(even)
    last = len(o) - 1
    out = []
    for b in range(last + 1):
        before = o[b - 1] if b > 0 else lane_prev(o[last])
        after = o[b + 1] if b < last else lane_next(o[0])
        out.append(jnp.where(low, before, after))
    return out


def around(other, colour, y0, y1, rows):
    groups = range(other.shape[0])
    mid = [other[b, y0:y1, 0:rows] for b in groups]
    zo = z_other(mid, colour, y0)
    return [
        (
            other[b, y0 - 1 : y1 - 1, 0:rows],
            other[b, y0 + 1 : y1 + 1, 0:rows],
            pltpu.roll(mid[b], 1, 1),
            pltpu.roll(mid[b], rows - 1, 1),
            mid[b],
            zo[b],
        )
        for b in groups
    ]


def split_even(zero, one):
    even = even_cells(zero.shape)
    return jnp.where(even, zero, one), jnp.where(even, one, zero)


def pair_rows(a):
    rows = a.shape[1] // 2
    a = a.reshape(a.shape[0] // 2, 2, a.shape[1], LANES)
    a = a[:, 0] + a[:, 1]
    pick = iota((a.shape[0], rows, LANES), 1)
    out = a[:, 0:1] + a[:, 1:2]
    out = jnp.broadcast_to(out, pick.shape)
    for j in range(1, rows):
        out = jnp.where(pick == j, a[:, 2 * j : 2 * j + 1] + a[:, 2 * j + 1 : 2 * j + 2], out)
    return out * 0.125


def double_rows(a, order):
    y = a.shape[0]
    pick = iota((y, 2 * len(order), LANES), 1) // 2
    out = jnp.broadcast_to(a[:, order[0] : order[0] + 1], pick.shape)
    for n, j in enumerate(order[1:], 1):
        out = jnp.where(pick == n, a[:, j : j + 1], out)
    return jnp.concatenate([out[i // 2 : i // 2 + 1] for i in range(2 * y)], axis=0)


def three(x):
    high = x.astype(jnp.bfloat16)
    rest = x - high.astype(F32)
    middle = rest.astype(jnp.bfloat16)
    low = (rest - middle.astype(F32)).astype(jnp.bfloat16)
    return jnp.concatenate([high, middle, low], axis=0)


def permute(x, matrix, side):
    n = x.shape[0]
    out = lax.dot_general(three(x), matrix, (((1,), (side,)), ((), ())), preferred_element_type=F32)
    return (out[0:n] + out[n : 2 * n]) + out[2 * n :]


def y_own(d, w):
    return slice(4, 12) if d == 0 else (slice(12 - w, 12) if d > 0 else slice(4, 4 + w))


def y_halo(d, w):
    return slice(4, 12) if d == 0 else (slice(12, 12 + w) if d > 0 else slice(4 - w, 4))


def x_own(d, w):
    return slice(0, 8) if d == 0 else (slice(8 - w, 8) if d > 0 else slice(0, w))


def x_halo(d, w):
    return slice(0, 8) if d == 0 else (slice(8, 8 + w) if d > 0 else slice(FINE - w, FINE))


def block_part(way, far):
    dy, dx = WAYS[way]
    n = far if abs(dy) == 2 else (2 if abs(dx) == 2 and dy else 4)
    return slice(0, n) if dy > 0 else slice(4 - n, 4)


def kernel(nx, ny, g_ref, c_ref, v_out, r_out, perm, held, d0, g0, k0, ra, ba, rb, bb, bp, rc, bc, rd, bd,
           ax_s, ax_r, gx_s, gx_r, ac_s, ac_r, sx_s, sx_r, sc_s, sc_r, ex_s, ex_r, ec_s, ec_r,
           d1, g1, k1, mr, mb, mp, blk_c, blk_g, blk_x, in_c, in_g, in_x,
           gat, cc, kc, vc, zero_y, bulk, held_sem, out_sem, gone_sem, in_sem):
    gx, gy = lax.axis_index("gx"), lax.axis_index("gy")

    def inside(way):
        dy, dx = WAYS[way]
        tests = []
        if dy:
            tests.append(gy + dy >= 0 if dy < 0 else gy + dy < ny)
        if dx:
            tests.append(gx + dx >= 0 if dx < 0 else gx + dx < nx)
        return tests[0] if len(tests) == 1 else jnp.logical_and(*tests)

    def device(way):
        dy, dx = WAYS[way]
        out = {}
        if dx:
            out["gx"] = gx + dx
        if dy:
            out["gy"] = gy + dy
        return out

    has = [inside(way) for way in range(len(WAYS))]
    target = [device(way) for way in range(len(WAYS))]

    def each_peer(fn):
        if nx * ny <= 64:
            for s in range(1, nx * ny):
                fn(s, s // ny, s % ny)
        else:
            def body(s, carry):
                fn(s, s // ny, lax.rem(s, ny))
                return carry
            lax.fori_loop(1, nx * ny, body, 0)

    loads = [
        pltpu.make_async_copy(ref, held.at[n], held_sem.at[n]) for n, ref in enumerate((c_ref, g_ref))
    ]
    for load in loads:
        load.start()

    barrier = pltpu.get_barrier_semaphore()

    def greet(s, sx, sy):
        pl.semaphore_signal(
            barrier, inc=1, device_id={"gx": lax.rem(gx + sx, nx), "gy": lax.rem(gy + sy, ny)}, device_id_type=MESH)

    each_peer(greet)

    for ref in (ax_r, gx_r, ex_r):
        ref[2] = jnp.zeros(ref.shape[1:], F32)
    for ref in (ac_r, ec_r):
        ref[4] = jnp.zeros(ref.shape[1:], F32)
    for n in range(2):
        sx_r[n, 2] = jnp.zeros(sx_r.shape[2:], F32)
        sc_r[n, 4] = jnp.zeros(sc_r.shape[2:], F32)
    for ref in (in_c, in_g, in_x):
        ref[len(WAYS)] = jnp.zeros(ref.shape[1:], F32)
    zero_y[...] = jnp.zeros(zero_y.shape, F32)
    vc[...] = jnp.zeros(vc.shape, F32)

    size_z = 4 * LANES
    row, col = iota((size_z, size_z), 0), iota((size_z, size_z), 1)
    perm[...] = (row == 4 * (col % LANES) + col // LANES).astype(F32).astype(jnp.bfloat16)

    def coarsen(red, black):
        pair = [pair_rows(red[b] + black[b]) for b in range(len(red))]
        if len(pair) == 1:
            return pair[0]
        first, second = split_even(pair[0], pair[1])
        return [first], [second]

    def remote(phase, way, src, dst):
        return pltpu.make_async_remote_copy(
            src_ref=src, dst_ref=dst, send_sem=out_sem.at[way], recv_sem=in_sem.at[phase],
            device_id=target[way], device_id_type=MESH)

    def size(ref):
        return math.prod(ref.shape[:-1])

    def take(sem, rows):
        pltpu.make_async_copy(bulk.at[0:rows], bulk.at[0:rows], sem).wait()

    def ring_messages(src, dst, w, x_s, x_r, c_s, c_r):
        out = []
        for way in YS:
            dy = WAYS[way][0]
            out.append((way, src.at[:, y_own(dy, w), 0:8], dst.at[:, y_halo(-dy, w), 0:8], dst.at[:, y_halo(dy, w), 0:8], zero_y.at[:, 0:w]))
        for way in XS:
            out.append((way, x_s.at[way - 2], x_r.at[BACK[way] - 2], x_r.at[way - 2], x_r.at[2]))
        for way in CORNERS:
            out.append((way, c_s.at[way - 4], c_r.at[BACK[way] - 4], c_r.at[way - 4], c_r.at[4]))
        return out

    def ring_pack(src, cw, x_s, c_s):
        for way in XS:
            x_s[way - 2] = src[:, 4:12, x_own(WAYS[way][1], x_s.shape[-2])]
        for way in CORNERS:
            dy, dx = WAYS[way]
            c_s[way - 4] = src[:, y_own(dy, cw), x_own(dx, cw)]

    def ring_unpack(dst, cw, x_r, c_r):
        for way in XS:
            dst[:, 4:12, x_halo(WAYS[way][1], x_r.shape[-2])] = x_r[way - 2]
        for way in CORNERS:
            dy, dx = WAYS[way]
            dst[:, y_halo(dy, cw), x_halo(dx, cw)] = c_r[way - 4]

    def messages_a():
        out = []
        for way in YS:
            dy = WAYS[way][0]
            for ref, colour, w in ((d0, 0, 2), (g0, 0, 2), (d0, 1, 3), (g0, 1, 1)):
                out.append((way, ref.at[colour, :, y_own(dy, w), 0:8],
                            ref.at[colour, :, y_halo(-dy, w), 0:8], ref.at[colour, :, y_halo(dy, w), 0:8],
                            zero_y.at[:, 0:w]))
        for way in XS:
            out.append((way, ax_s.at[way - 2], ax_r.at[BACK[way] - 2], ax_r.at[way - 2], ax_r.at[2]))
            out.append((way, gx_s.at[way - 2], gx_r.at[BACK[way] - 2], gx_r.at[way - 2], gx_r.at[2]))
        for way in CORNERS:
            out.append((way, ac_s.at[way - 4], ac_r.at[BACK[way] - 4], ac_r.at[way - 4], ac_r.at[4]))
        return out

    def block_messages(src, dst, ways, far):
        out = []
        for way in ways:
            give, got = block_part(BACK[way], far), block_part(way, far)
            lead = (slice(None),) * (len(src.shape) - 3)
            out.append((way, src.at[(*lead, give)], dst.at[(BACK[way], *lead, give)], dst.at[(way, *lead, got)],
                        dst.at[(len(WAYS), *lead, got)]))
        return out

    def by_way(messages):
        ways = {}
        for m in messages:
            ways.setdefault(m[0], []).append(m)
        return ways.items()

    sent = {}

    def start(phase, messages):
        for way, group in by_way(messages):
            @pl.when(has[way])
            def _():
                for _, src, there, here, zeros in group:
                    remote(phase, way, src, there).start()

            @pl.when(jnp.logical_not(has[way]))
            def _():
                for _, src, there, here, zeros in group:
                    pltpu.make_async_copy(zeros, here, in_sem.at[phase]).start()

            sent[way] = sent.get(way, 0) + sum(size(m[1]) for m in group)

    def finish(phase, messages):
        take(in_sem.at[phase], sum(size(m[3]) for m in messages))

    def all_sent():
        for way, rows in sent.items():
            @pl.when(has[way])
            def _():
                take(out_sem.at[way], rows)
        for n in range(2):
            take(gone_sem.at[n], (nx * ny - 1) * size(gat.at[0, 0]))

    me = gx * ny + gy

    def spread(n):
        def body(s, sx, sy):
            pltpu.make_async_remote_copy(
                src_ref=gat.at[n, me], dst_ref=gat.at[n, me], send_sem=gone_sem.at[n], recv_sem=in_sem.at[GATHER[n]],
                device_id={"gx": lax.rem(gx + sx, nx), "gy": lax.rem(gy + sy, ny)}, device_id_type=MESH).start()
        each_peer(body)

    def gathered(n):
        take(in_sem.at[GATHER[n]], (nx * ny - 1) * size(gat.at[0, 0]))

    def setup(kref, dens, colour, scale, y0, y1, rows):
        for b, near in enumerate(around(dens.at[1 - colour], colour, y0, y1, rows)):
            here = dens[colour, b, y0:y1, 0:rows]
            total = None
            for f in range(6):
                face = (scale * 0.5) * (here + near[f])
                kref[colour, b, f, y0:y1, 0:rows] = face
                total = face if total is None else total + face
            kref[colour, b, 6, y0:y1, 0:rows] = total
            kref[colour, b, 7, y0:y1, 0:rows] = jnp.where(here > 0.0, 1.0 / total, 0.0)

    def weigh(kref, other, colour, y0, y1, rows):
        out = []
        for b, near in enumerate(around(other, colour, y0, y1, rows)):
            total = kref[colour, b, 0, y0:y1, 0:rows] * near[0]
            for f in range(1, 6):
                total = total + kref[colour, b, f, y0:y1, 0:rows] * near[f]
            out.append(total)
        return out

    def update(kref, g, other, dst, colour, y0, y1, rows):
        for b, n in enumerate(weigh(kref, other, colour, y0, y1, rows)):
            dst[b, y0:y1, 0:rows] = (g[colour, b, y0:y1, 0:rows] + n) * kref[colour, b, 7, y0:y1, 0:rows]

    def first(kref, g, dst, y0, y1, rows):
        for b in range(dst.shape[0]):
            dst[b, y0:y1, 0:rows] = g[0, b, y0:y1, 0:rows] * kref[0, b, 7, y0:y1, 0:rows]

    def residual(kref, g, red, black, y0, y1, rows, x0, x1):
        out = []
        for c, (v, other) in enumerate(((red, black), (black, red))):
            n = weigh(kref, other, c, y0, y1, rows)
            out.append([
                (g[c, b, y0:y1, 0:rows] - (kref[c, b, 6, y0:y1, 0:rows] * v[b, y0:y1, 0:rows] - n[b]))[:, x0:x1]
                for b in range(len(n))])
        return out

    for load in loads:
        load.wait()
    flat = permute(held[...].reshape(-1, size_z), perm[...], 0)

    def fields(flat):
        quarters = [
            jnp.swapaxes(flat[:, q * LANES : (q + 1) * LANES].reshape(8, 8, LANES), 0, 1) for q in range(4)]
        pairs = [split_even(quarters[2 * b], quarters[2 * b + 1]) for b in range(2)]
        return [pairs[b][0] for b in range(2)], [pairs[b][1] for b in range(2)]

    dens, source = fields(flat[0:64]), fields(flat[64:128])
    for c in range(2):
        for b in range(2):
            d0[c, b, 4:12, 0:8] = dens[c][b]
            g0[c, b, 4:12, 0:8] = source[c][b]
    for way in XS:
        dx = WAYS[way][1]
        for c in range(2):
            ax_s[way - 2, c] = d0[c, :, 4:12, x_own(dx, 4)]
            gx_s[way - 2, c] = g0[c, :, 4:12, x_own(dx, 2)]
    for way in CORNERS:
        dy, dx = WAYS[way]
        for b in range(2):
            ac_s[way - 4, 2 * b : 2 * b + 2] = d0[1, b, y_own(dy, 2), x_own(dx, 2)]
            ac_s[way - 4, 4:5, b : b + 1] = d0[0, b, y_own(dy, 1), x_own(dx, 1)]
            ac_s[way - 4, 5:6, b : b + 1] = g0[0, b, y_own(dy, 1), x_own(dx, 1)]
    dens_one = coarsen(*dens)
    for c in range(2):
        blk_c[c] = dens_one[c][0]
        d1[c, 0, 8:12, 8:12] = dens_one[c][0]
    gat[0, me] = coarsen(*dens_one)

    pl.semaphore_wait(barrier, nx * ny - 1)
    start(ARGS, messages_a())
    finish(ARGS, messages_a())
    for way in XS:
        dx = WAYS[way][1]
        for c in range(2):
            d0[c, :, 4:12, x_halo(dx, 4)] = ax_r[way - 2, c]
            g0[c, :, 4:12, x_halo(dx, 2)] = gx_r[way - 2, c]
    for way in CORNERS:
        dy, dx = WAYS[way]
        for b in range(2):
            d0[1, b, y_halo(dy, 2), x_halo(dx, 2)] = ac_r[way - 4, 2 * b : 2 * b + 2]
            d0[0, b, y_halo(dy, 1), x_halo(dx, 1)] = ac_r[way - 4, 4:5, b : b + 1]
            g0[0, b, y_halo(dy, 1), x_halo(dx, 1)] = ac_r[way - 4, 5:6, b : b + 1]

    setup(k0, d0, 0, 1.0, 2, 14, FINE)
    setup(k0, d0, 1, 1.0, 3, 13, FINE)
    first(k0, g0, ra, 3, 13, FINE)
    update(k0, g0, ra, ba, 1, 4, 12, FINE)
    ring_pack(ba, 2, sx_s.at[0], sc_s.at[0])
    swap = ring_messages(ba, ba, 3, sx_s.at[0], sx_r.at[0], sc_s.at[0], sc_r.at[0])
    start(SWAP, swap)
    part_c = block_messages(blk_c, in_c, range(20), 2)
    start(MID_C, part_c)
    spread(0)
    finish(SWAP, swap)
    ring_unpack(ba, 2, sx_r.at[0], sc_r.at[0])
    update(k0, g0, ba, rb, 0, 2, 14, FINE)
    update(k0, g0, rb, bb, 1, 3, 13, FINE)
    source_one = coarsen(*residual(k0, g0, rb, bb, 4, 12, FINE, 0, 8))
    for c in range(2):
        blk_g[c] = source_one[c][0]
        g1[c, 0, 8:12, 8:12] = source_one[c][0]
    part_g = block_messages(blk_g, in_g, NEAR, 1)
    far_g = block_messages(blk_g, in_g, range(8, 12), 1)
    start(MID_G, part_g)
    start(FAR_G, far_g)
    ring_pack(bb, 2, sx_s.at[1], sc_s.at[1])
    keep = ring_messages(bb, bp, 3, sx_s.at[1], sx_r.at[1], sc_s.at[1], sc_r.at[1])
    start(KEEP, keep)

    def blocks(ref, got, ways, far):
        for way in ways:
            dy, dx = WAYS[way]
            part = block_part(way, far)
            y, x = 4 * (dy + 2), 4 * (dx + 2)
            for c in range(2):
                ref[c, 0, y + part.start : y + part.stop, x : x + 4] = got[way, c, part]

    finish(MID_C, part_c)
    blocks(d1, in_c, range(20), 2)
    for c in range(2):
        setup(k1, d1, c, 0.25, 1, 19, MID[1])

    gathered(0)
    pairs, rows = ny, 2 * nx

    def assemble(n):
        for i in range(nx):
            for p in range(2):
                cc[p, :, 2 * i : 2 * i + 2] = gat[n, i * ny : (i + 1) * ny, p]
        even = (iota((pairs, rows, LANES), 1) + iota((pairs, rows, LANES), 2)) % 2 == 0
        return jnp.where(even, cc[0], cc[1]), jnp.where(even, cc[1], cc[0])

    shape = (pairs, rows, LANES)
    tested = (iota(shape, 1) + iota(shape, 2)) % 2

    def beside(other, colour):
        low = tested == colour
        return (
            jnp.where(low, jnp.concatenate([other[-1:], other[:-1]], axis=0), other),
            jnp.where(low, other, jnp.concatenate([other[1:], other[:1]], axis=0)),
            pltpu.roll(other, 1, 1), pltpu.roll(other, rows - 1, 1),
            pltpu.roll(other, 1, 2), pltpu.roll(other, LANES - 1, 2))

    centre = assemble(0)
    for c in range(2):
        low = tested == c
        edges = (
            jnp.logical_and(low, iota(shape, 0) == 0),
            jnp.logical_and(jnp.logical_not(low), iota(shape, 0) == pairs - 1),
            iota(shape, 1) == 0, iota(shape, 1) == rows - 1, iota(shape, 2) == 0, iota(shape, 2) == LANES - 1)
        total, faces = None, []
        for near, edge in zip(beside(centre[1 - c], c), edges):
            face = 0.03125 * (centre[c] + jnp.where(edge, 0.0, near))
            total = face if total is None else total + face
            faces.append(face)
        inverse = 1.0 / total
        for f in range(6):
            kc[c, f] = jnp.where(edges[f], 0.0, faces[f] * inverse)
        kc[c, 6] = inverse

    finish(MID_G, part_g)
    blocks(g1, in_g, NEAR, 1)
    first(k1, g1, mr, 4, 16, 16)
    update(k1, g1, mr, mb, 1, 5, 15, 16)
    update(k1, g1, mb, mr, 0, 6, 14, 16)
    update(k1, g1, mr, mb, 1, 7, 13, 16)
    gat[1, me] = coarsen(*residual(k1, g1, mr, mb, 8, 12, 16, 8, 12))
    spread(1)
    blk_x[...] = mb[0, 8:12, 8:12]
    part_x = block_messages(blk_x, in_x, range(20), 2)
    start(MID_X, part_x)

    gathered(1)
    right = assemble(1)
    for c in range(2):
        kc[c, 7] = right[c] * kc[c, 6]

    def half(other, colour):
        total = kc[colour, 7]
        for f, near in enumerate(beside(other, colour)):
            total = total + kc[colour, f] * near
        return total

    def sweep(i, carry):
        red = half(carry[1], 0)
        return red, half(red, 1)

    red = kc[0, 7]
    red, black = lax.fori_loop(1, COARSE_SWEEPS, sweep, (red, half(red, 1)))
    even = tested == 0
    for i in range(nx):
        cut = slice(2 * i, 2 * i + 2)
        vc[2 + i, 2 : 2 + ny, 0] = jnp.where(even, red, black)[:, cut]
        vc[2 + i, 2 : 2 + ny, 1] = jnp.where(even, black, red)[:, cut]

    finish(MID_X, part_x)
    finish(FAR_G, far_g)
    blocks(g1, in_g, range(8, 12), 1)
    mp[0, 8:12, 8:12] = blk_x[...]
    for way in range(20):
        dy, dx = WAYS[way]
        part = block_part(way, 2)
        y, x = 4 * (dy + 2), 4 * (dx + 2)
        mp[0, y + part.start : y + part.stop, x : x + 4] = in_x[way, part]
    for dx in range(5):
        window = vc[gx + dx, pl.ds(gy, 5)].reshape(10, 2, LANES)
        mp[0, :, 4 * dx : 4 * dx + 4] = mp[0, :, 4 * dx : 4 * dx + 4] + double_rows(window, (0, 1))
    update(k1, g1, mp, mr, 0, 3, 17, MID[1])
    update(k1, g1, mr, mb, 1, 4, 16, MID[1])
    update(k1, g1, mb, mr, 0, 5, 15, MID[1])
    update(k1, g1, mr, mb, 1, 6, 14, MID[1])

    finish(KEEP, keep)
    bp[:, 4:12, 0:8] = bb[:, 4:12, 0:8]
    ring_unpack(bp, 2, sx_r.at[1], sc_r.at[1])
    half_z = split_even(mr[0, 6:14], mb[0, 6:14])
    for b in range(2):
        bp[b] = bp[b] + double_rows(half_z[b], (8, 9, 10, 11, 12, 13, 6, 7))
    update(k0, g0, bp, rc, 0, 2, 14, FINE)
    update(k0, g0, rc, bc, 1, 3, 13, FINE)
    update(k0, g0, bc, rd, 0, 4, 12, FINE)
    ring_pack(rd, 1, ex_s, ec_s)
    last = ring_messages(rd, rd, 2, ex_s, ex_r, ec_s, ec_r)
    start(LAST, last)
    finish(LAST, last)
    ring_unpack(rd, 1, ex_r, ec_r)
    update(k0, g0, rd, bd, 1, 3, 13, FINE)
    left = residual(k0, g0, rd, bd, 4, 12, FINE, 0, 8)

    def lay(red, black):
        quarters = []
        for b in range(2):
            quarters.extend(split_even(red[b], black[b]))
        return jnp.concatenate([jnp.swapaxes(q, 0, 1).reshape(64, LANES) for q in quarters], axis=1)

    field = [[ref[b, 4:12, 0:8] for b in range(2)] for ref in (rd, bd)]
    flat = permute(jnp.concatenate([lay(*field), lay(*left)], axis=0), perm[...], 1)
    v_out[...] = flat[0:64].reshape(v_out.shape)
    r_out[...] = flat[64:128].reshape(r_out.shape)
    all_sent()


def hand_out(v_ref, r_ref, v_out, r_out, sem):
    copies = [
        pltpu.make_async_copy(src, dst, sem.at[n]) for n, (src, dst) in enumerate(((v_ref, v_out), (r_ref, r_out)))
    ]
    for copy in copies:
        copy.start()
    for copy in copies:
        copy.wait()


def solution(mesh):
    nx, ny = mesh.shape["gx"], mesh.shape["gy"]

    def shards(right_side, inverse_density):
        x, y, z = right_side.shape
        assert (x, y, z) == (8, 8, 4 * LANES)

        def vmem(*shape):
            return pltpu.VMEM((*shape, LANES), F32)

        fine = (2, FINE, FINE)
        mid = (1, *MID)
        result = pltpu.VMEM(right_side.shape, F32)
        v, r = pl.pallas_call(
            functools.partial(kernel, nx, ny),
            out_shape=(result, result),
            in_specs=[pl.BlockSpec(memory_space=pl.ANY)] * 2,
            out_specs=(pl.BlockSpec(memory_space=pltpu.VMEM),) * 2,
            scratch_shapes=[
                pltpu.VMEM((z, z), jnp.bfloat16),
                pltpu.VMEM((2, x, y, z), F32),
                vmem(2, *fine), vmem(2, *fine), vmem(2, 2, 8, FINE, FINE),
                *[vmem(*fine)] * 9,
                vmem(2, 2, 2, 8, 4), vmem(3, 2, 2, 8, 4), vmem(2, 2, 2, 8, 2), vmem(3, 2, 2, 8, 2), vmem(4, 6, 2), vmem(5, 6, 2),
                vmem(2, 2, 2, 8, 4), vmem(2, 3, 2, 8, 4), vmem(2, 4, 2, 2, 2), vmem(2, 5, 2, 2, 2),
                vmem(2, 2, 8, 2), vmem(3, 2, 8, 2), vmem(4, 2, 1, 1), vmem(5, 2, 1, 1),
                vmem(2, *mid), vmem(2, *mid), vmem(2, 1, 8, *MID), *[vmem(*mid)] * 3,
                vmem(2, 4, 4), vmem(2, 4, 4), vmem(4, 4),
                *[vmem(len(WAYS) + 1, 2, 4, 4)] * 2, vmem(len(WAYS) + 1, 4, 4),
                vmem(2, nx * ny, 2, 2), vmem(2, ny, 2 * nx), vmem(2, 8, ny, 2 * nx), vmem(nx + 4, ny + 4, 2, 2),
                vmem(2, 3, 8), vmem(2048),
                pltpu.SemaphoreType.DMA((2,)),
                pltpu.SemaphoreType.DMA((len(WAYS),)),
                pltpu.SemaphoreType.DMA((2,)),
                pltpu.SemaphoreType.DMA((PHASES,)),
            ],
            compiler_params=pltpu.CompilerParams(
                collective_id=0, has_side_effects=True, vmem_limit_bytes=40 * 1024 * 1024
            ),
        )(*(pltpu.with_memory_space_constraint(a, pltpu.HBM) for a in (right_side, inverse_density)))
        out = jax.ShapeDtypeStruct(right_side.shape, F32)
        return pl.pallas_call(
            hand_out,
            out_shape=(out, out),
            in_specs=[pl.BlockSpec(memory_space=pltpu.VMEM)] * 2,
            out_specs=(pl.BlockSpec(memory_space=pl.ANY),) * 2,
            scratch_shapes=[pltpu.SemaphoreType.DMA((2,))],
            compiler_params=pltpu.CompilerParams(vmem_limit_bytes=1024 * 1024),
        )(v, r)

    spec = P("gx", "gy", None)
    return jax.shard_map(shards, mesh=mesh, in_specs=(spec, spec), out_specs=(spec, spec), check_vma=False)
```

```python
import functools
import math

import jax
import jax.numpy as jnp
from jax import lax
from jax.experimental import pallas as pl
from jax.experimental.pallas import tpu as pltpu
from jax.sharding import PartitionSpec as P

SWEEPS = 2
COARSE_SWEEPS = 8
MESH = pl.DeviceIdType.MESH
LANES = 128
F32 = jnp.float32

FINE, MID = 16, (20, 24)

WAYS = ((-1, 0), (1, 0), (0, -1), (0, 1), (-1, -1), (-1, 1), (1, -1), (1, 1),
        (-2, 0), (2, 0), (0, -2), (0, 2),
        (-2, -1), (-2, 1), (2, -1), (2, 1), (-1, -2), (-1, 2), (1, -2), (1, 2))
BACK = tuple(WAYS.index((-dy, -dx)) for dy, dx in WAYS)
FIRST, MORE, SWAP, KEEP, LAST, MID_C, STRIP, MID_G, FAR_G, MID_X = range(10)
GATHER, LINE, PLANE = 10, 11, 12
PHASES = 13
YS, XS, CORNERS, NEAR = (0, 1), (2, 3), (4, 5, 6, 7), range(8)


def iota(shape, dim):
    return lax.broadcasted_iota(jnp.int32, shape, dim)


def lane_prev(a):
    return jnp.where(iota(a.shape, 2) == 0, 0.0, pltpu.roll(a, 1, 2))


def lane_next(a):
    return jnp.where(iota(a.shape, 2) == LANES - 1, 0.0, pltpu.roll(a, LANES - 1, 2))


def even_cells(shape):
    return (iota(shape, 0) + iota(shape, 1)) % 2 == 0


def z_other(o, colour, first):
    shape = o[0].shape
    even = (iota(shape, 0) + iota(shape, 1)) % 2 == first % 2
    low = even if colour == 0 else jnp.logical_not(even)
    last = len(o) - 1
    out = []
    for b in range(last + 1):
        before = o[b - 1] if b > 0 else lane_prev(o[last])
        after = o[b + 1] if b < last else lane_next(o[0])
        out.append(jnp.where(low, before, after))
    return out


def around(other, colour, y0, y1, rows):
    groups = range(other.shape[0])
    mid = [other[b, y0:y1, 0:rows] for b in groups]
    zo = z_other(mid, colour, y0)
    return [
        (
            other[b, y0 - 1 : y1 - 1, 0:rows],
            other[b, y0 + 1 : y1 + 1, 0:rows],
            pltpu.roll(mid[b], 1, 1),
            pltpu.roll(mid[b], rows - 1, 1),
            mid[b],
            zo[b],
        )
        for b in groups
    ]


def split_even(zero, one):
    even = even_cells(zero.shape)
    return jnp.where(even, zero, one), jnp.where(even, one, zero)


def pair_rows(a):
    rows = a.shape[1] // 2
    a = a.reshape(a.shape[0] // 2, 2, a.shape[1], LANES)
    a = a[:, 0] + a[:, 1]
    pick = iota((a.shape[0], rows, LANES), 1)
    out = a[:, 0:1] + a[:, 1:2]
    out = jnp.broadcast_to(out, pick.shape)
    for j in range(1, rows):
        out = jnp.where(pick == j, a[:, 2 * j : 2 * j + 1] + a[:, 2 * j + 1 : 2 * j + 2], out)
    return out * 0.125


def double_rows(a, order):
    y = a.shape[0]
    pick = iota((y, 2 * len(order), LANES), 1) // 2
    out = jnp.broadcast_to(a[:, order[0] : order[0] + 1], pick.shape)
    for n, j in enumerate(order[1:], 1):
        out = jnp.where(pick == n, a[:, j : j + 1], out)
    return jnp.concatenate([out[i // 2 : i // 2 + 1] for i in range(2 * y)], axis=0)


def three(x):
    high = x.astype(jnp.bfloat16)
    rest = x - high.astype(F32)
    middle = rest.astype(jnp.bfloat16)
    low = (rest - middle.astype(F32)).astype(jnp.bfloat16)
    return jnp.concatenate([high, middle, low], axis=0)


def permute(x, matrix, side):
    n = x.shape[0]
    out = lax.dot_general(three(x), matrix, (((1,), (side,)), ((), ())), preferred_element_type=F32)
    return (out[0:n] + out[n : 2 * n]) + out[2 * n :]


def y_own(d, w):
    return slice(4, 12) if d == 0 else (slice(12 - w, 12) if d > 0 else slice(4, 4 + w))


def y_halo(d, w):
    return slice(4, 12) if d == 0 else (slice(12, 12 + w) if d > 0 else slice(4 - w, 4))


def x_own(d, w):
    return slice(0, 8) if d == 0 else (slice(8 - w, 8) if d > 0 else slice(0, w))


def x_halo(d, w):
    return slice(0, 8) if d == 0 else (slice(8, 8 + w) if d > 0 else slice(FINE - w, FINE))


def outer(part, d):
    return slice(part.stop - 1, part.stop) if d > 0 else slice(part.start, part.start + 1)


def block_part(way, far):
    dy, dx = WAYS[way]
    n = far if abs(dy) == 2 else (2 if abs(dx) == 2 and dy else 4)
    return slice(0, n) if dy > 0 else slice(4 - n, 4)


def kernel(nx, ny, g_ref, c_ref, v_out, r_out, perm, held, d0, g0, k0, ra, ba, rb, bb, bp, rc, bc, rd, bd,
           ax_s, ax_r, gx_s, gx_r, an_s, an_r, ac_s, ac_r, sx_s, sx_r, sc_s, sc_r, ex_s, ex_r, ec_s, ec_r,
           d1, g1, k1, mr, mb, mp, strip, blk_g, blk_x, in_c, in_g, in_x,
           gat, cc, kc, vc, zero_y, bulk, held_sem, out_sem, gone_sem, in_sem):
    gx, gy = lax.axis_index("gx"), lax.axis_index("gy")

    def inside(way):
        dy, dx = WAYS[way]
        tests = []
        if dy:
            tests.append(gy + dy >= 0 if dy < 0 else gy + dy < ny)
        if dx:
            tests.append(gx + dx >= 0 if dx < 0 else gx + dx < nx)
        return tests[0] if len(tests) == 1 else jnp.logical_and(*tests)

    def device(way):
        dy, dx = WAYS[way]
        out = {}
        if dx:
            out["gx"] = gx + dx
        if dy:
            out["gy"] = gy + dy
        return out

    has = [inside(way) for way in range(len(WAYS))]
    target = [device(way) for way in range(len(WAYS))]

    def each_peer(fn):
        if nx * ny <= 64:
            for s in range(1, nx * ny):
                fn(s, s // ny, s % ny)
        else:
            def body(s, carry):
                fn(s, s // ny, lax.rem(s, ny))
                return carry
            lax.fori_loop(1, nx * ny, body, 0)

    loads = [
        pltpu.make_async_copy(ref.at[i : i + 2], held.at[n, i : i + 2], held_sem)
        for n, ref in enumerate((c_ref, g_ref)) for i in range(0, 8, 2)
    ]
    for load in loads:
        load.start()

    barrier = pltpu.get_barrier_semaphore()

    def greet(s, sx, sy):
        pl.semaphore_signal(
            barrier, inc=1, device_id={"gx": lax.rem(gx + sx, nx), "gy": lax.rem(gy + sy, ny)}, device_id_type=MESH)

    each_peer(greet)

    for ref in (ax_r, gx_r, ex_r):
        ref[2] = jnp.zeros(ref.shape[1:], F32)
    for ref in (an_r, ac_r, ec_r):
        ref[4] = jnp.zeros(ref.shape[1:], F32)
    for n in range(2):
        sx_r[n, 2] = jnp.zeros(sx_r.shape[2:], F32)
        sc_r[n, 4] = jnp.zeros(sc_r.shape[2:], F32)
    in_c[4] = jnp.zeros(in_c.shape[1:], F32)
    for ref in (in_g, in_x):
        ref[len(WAYS)] = jnp.zeros(ref.shape[1:], F32)
    zero_y[...] = jnp.zeros(zero_y.shape, F32)
    vc[...] = jnp.zeros(vc.shape, F32)

    size_z = 4 * LANES
    row, col = iota((size_z, size_z), 0), iota((size_z, size_z), 1)
    perm[...] = (row == 4 * (col % LANES) + col // LANES).astype(F32).astype(jnp.bfloat16)

    def coarsen(red, black):
        pair = [pair_rows(red[b] + black[b]) for b in range(len(red))]
        if len(pair) == 1:
            return pair[0]
        first, second = split_even(pair[0], pair[1])
        return [first], [second]

    def remote(phase, way, src, dst):
        return pltpu.make_async_remote_copy(
            src_ref=src, dst_ref=dst, send_sem=out_sem.at[way], recv_sem=in_sem.at[phase],
            device_id=target[way], device_id_type=MESH)

    def size(ref):
        return math.prod(ref.shape[:-1])

    def take(sem, rows):
        pltpu.make_async_copy(bulk.at[0:rows], bulk.at[0:rows], sem).wait()

    def ring_messages(src, dst, w, x_s, x_r, c_s, c_r):
        out = []
        for way in YS:
            dy = WAYS[way][0]
            out.append((way, src.at[:, y_own(dy, w), 0:8], dst.at[:, y_halo(-dy, w), 0:8], dst.at[:, y_halo(dy, w), 0:8], zero_y.at[:, 0:w]))
        for way in XS:
            out.append((way, x_s.at[way - 2], x_r.at[BACK[way] - 2], x_r.at[way - 2], x_r.at[2]))
        for way in CORNERS:
            out.append((way, c_s.at[way - 4], c_r.at[BACK[way] - 4], c_r.at[way - 4], c_r.at[4]))
        return out

    def ring_pack(src, cw, x_s, c_s):
        for way in XS:
            x_s[way - 2] = src[:, 4:12, x_own(WAYS[way][1], x_s.shape[-2])]
        for way in CORNERS:
            dy, dx = WAYS[way]
            c_s[way - 4] = src[:, y_own(dy, cw), x_own(dx, cw)]

    def ring_unpack(dst, cw, x_r, c_r):
        for way in XS:
            dst[:, 4:12, x_halo(WAYS[way][1], x_r.shape[-2])] = x_r[way - 2]
        for way in CORNERS:
            dy, dx = WAYS[way]
            dst[:, y_halo(dy, cw), x_halo(dx, cw)] = c_r[way - 4]

    def rows_y(ref, colour, w, only, way):
        dy = WAYS[way][0]
        own, there, here = y_own(dy, w), y_halo(-dy, w), y_halo(dy, w)
        if only:
            own, there, here = (outer(a, d) for a, d in ((own, -dy), (there, -dy), (here, dy)))
        n = 1 if only else w
        return (way, ref.at[colour, :, own, 0:8], ref.at[colour, :, there, 0:8], ref.at[colour, :, here, 0:8],
                zero_y.at[:, 0:n])

    def messages_first():
        out = []
        for way in YS:
            for ref, colour, w in ((d0, 0, 1), (d0, 1, 2), (g0, 0, 1)):
                out.append(rows_y(ref, colour, w, False, way))
        for way in CORNERS:
            out.append((way, an_s.at[way - 4], an_r.at[BACK[way] - 4], an_r.at[way - 4], an_r.at[4]))
        for way in XS:
            out.append((way, ax_s.at[way - 2], ax_r.at[BACK[way] - 2], ax_r.at[way - 2], ax_r.at[2]))
            out.append((way, gx_s.at[way - 2], gx_r.at[BACK[way] - 2], gx_r.at[way - 2], gx_r.at[2]))
        return out

    def messages_more():
        out = []
        for way in YS:
            for ref, colour, w in ((d0, 0, 2), (d0, 1, 3), (g0, 0, 2), (g0, 1, 1)):
                out.append(rows_y(ref, colour, w, True, way))
        for way in CORNERS:
            out.append((way, ac_s.at[way - 4], ac_r.at[BACK[way] - 4], ac_r.at[way - 4], ac_r.at[4]))
        return out

    def block_messages(src, dst, ways, far):
        out = []
        for way in ways:
            give, got = block_part(BACK[way], far), block_part(way, far)
            lead = (slice(None),) * (len(src.shape) - 3)
            out.append((way, src.at[(*lead, give)], dst.at[(BACK[way], *lead, give)], dst.at[(way, *lead, got)],
                        dst.at[(len(WAYS), *lead, got)]))
        return out

    def near_part(way, c):
        n = 4 if way in XS else ((4, 3)[c] if way in YS else (3, 2)[c])
        dy = WAYS[way][0]
        return slice(0, n) if dy > 0 else slice(4 - n, 4)

    def near_more(way, c):
        n = {YS: (0, 4), XS: (0, 0), CORNERS: (4, 3)}[YS if way in YS else (XS if way in XS else CORNERS)][c]
        dy = WAYS[way][0]
        return (slice(n - 1, n) if dy > 0 else slice(4 - n, 5 - n)) if n else None

    def source_message(way, c, part):
        give, got = part(BACK[way], c), part(way, c)
        return (way, blk_g.at[c, give], in_g.at[BACK[way], c, give], in_g.at[way, c, got], in_g.at[len(WAYS), c, got])

    def sources(part):
        for way in NEAR:
            y, x = (4 * (d + 2) for d in WAYS[way])
            for c in range(2):
                rows = part(way, c)
                if rows:
                    g1[c, 0, y + rows.start : y + rows.stop, x : x + 4] = in_g[way, c, rows]

    def column_messages():
        out = []
        for way in (0, 1, 8, 9):
            dy = WAYS[way][0]
            give, there, here = {
                -1: (slice(6, 10), slice(10, 14), slice(2, 6)), 1: (slice(6, 10), slice(2, 6), slice(10, 14)),
                -2: (slice(6, 8), slice(14, 16), slice(0, 2)), 2: (slice(8, 10), slice(0, 2), slice(14, 16))}[dy]
            out.append((way, strip.at[:, give], strip.at[:, there], strip.at[:, here], in_c.at[4, :, give]))
        return out

    def strip_messages():
        out = []
        for n, way in enumerate((2, 3, 10, 11)):
            part = slice(0, 16) if n < 2 else slice(4, 12)
            out.append((way, strip.at[:, part], in_c.at[n ^ 1, :, part], in_c.at[n, :, part], in_c.at[4, :, part]))
        return out

    def columns():
        for c in range(2):
            d1[c, 0, 2:18, 8:12] = strip[c]
            for n, way in enumerate((2, 3, 10, 11)):
                part = slice(0, 16) if n < 2 else slice(4, 12)
                x = 4 * (WAYS[way][1] + 2)
                d1[c, 0, 2 + part.start : 2 + part.stop, x : x + 4] = in_c[n, c, part]

    def by_way(messages):
        ways = {}
        for m in messages:
            ways.setdefault(m[0], []).append(m)
        return ways.items()

    sent = {}

    def start(phase, messages):
        for way, group in by_way(messages):
            @pl.when(has[way])
            def _():
                for _, src, there, here, zeros in group:
                    remote(phase, way, src, there).start()

            @pl.when(jnp.logical_not(has[way]))
            def _():
                for _, src, there, here, zeros in group:
                    pltpu.make_async_copy(zeros, here, in_sem.at[phase]).start()

            sent[way] = sent.get(way, 0) + sum(size(m[1]) for m in group)

    def finish(phase, messages):
        take(in_sem.at[phase], sum(size(m[3]) for m in messages))

    def all_sent():
        for way, rows in sent.items():
            @pl.when(has[way])
            def _():
                take(out_sem.at[way], rows)
        for n, slots in enumerate((nx * ny - 1, ny - 1, (nx - 1) * ny)):
            take(gone_sem.at[n], slots * slot)

    me = gx * ny + gy
    def spread():
        def body(s, sx, sy):
            pltpu.make_async_remote_copy(
                src_ref=gat.at[1, me], dst_ref=gat.at[1, me], send_sem=gone_sem.at[0], recv_sem=in_sem.at[GATHER],
                device_id={"gx": lax.rem(gx + sx, nx), "gy": lax.rem(gy + sy, ny)}, device_id_type=MESH).start()
        each_peer(body)

    slot = size(gat.at[0, 0])

    def along_y():
        for sy in range(1, ny):
            pltpu.make_async_remote_copy(
                src_ref=gat.at[0, me], dst_ref=gat.at[0, me], send_sem=gone_sem.at[1], recv_sem=in_sem.at[LINE],
                device_id={"gy": lax.rem(gy + sy, ny)}, device_id_type=MESH).start()

    def along_x():
        take(in_sem.at[LINE], (ny - 1) * slot)
        line = gat.at[0, pl.ds(gx * ny, ny)]
        for sx in range(1, nx):
            pltpu.make_async_remote_copy(
                src_ref=line, dst_ref=line, send_sem=gone_sem.at[2], recv_sem=in_sem.at[PLANE],
                device_id={"gx": lax.rem(gx + sx, nx)}, device_id_type=MESH).start()

    def setup(kref, dens, colour, scale, y0, y1, rows):
        for b, near in enumerate(around(dens.at[1 - colour], colour, y0, y1, rows)):
            here = dens[colour, b, y0:y1, 0:rows]
            total = None
            for f in range(6):
                face = (scale * 0.5) * (here + near[f])
                kref[colour, b, f, y0:y1, 0:rows] = face
                total = face if total is None else total + face
            kref[colour, b, 6, y0:y1, 0:rows] = total
            kref[colour, b, 7, y0:y1, 0:rows] = jnp.where(here > 0.0, 1.0 / total, 0.0)

    def weigh(kref, other, colour, y0, y1, rows):
        out = []
        for b, near in enumerate(around(other, colour, y0, y1, rows)):
            total = kref[colour, b, 0, y0:y1, 0:rows] * near[0]
            for f in range(1, 6):
                total = total + kref[colour, b, f, y0:y1, 0:rows] * near[f]
            out.append(total)
        return out

    def update(kref, g, other, dst, colour, y0, y1, rows):
        for b, n in enumerate(weigh(kref, other, colour, y0, y1, rows)):
            dst[b, y0:y1, 0:rows] = (g[colour, b, y0:y1, 0:rows] + n) * kref[colour, b, 7, y0:y1, 0:rows]

    def first(kref, g, dst, y0, y1, rows):
        for b in range(dst.shape[0]):
            dst[b, y0:y1, 0:rows] = g[0, b, y0:y1, 0:rows] * kref[0, b, 7, y0:y1, 0:rows]

    def residual(kref, g, red, black, y0, y1, rows, x0, x1):
        out = []
        for c, (v, other) in enumerate(((red, black), (black, red))):
            n = weigh(kref, other, c, y0, y1, rows)
            out.append([
                (g[c, b, y0:y1, 0:rows] - (kref[c, b, 6, y0:y1, 0:rows] * v[b, y0:y1, 0:rows] - n[b]))[:, x0:x1]
                for b in range(len(n))])
        return out

    pltpu.make_async_copy(held, held, held_sem).wait()
    flat = permute(held[...].reshape(-1, size_z), perm[...], 0)

    def fields(flat):
        quarters = [
            jnp.swapaxes(flat[:, q * LANES : (q + 1) * LANES].reshape(8, 8, LANES), 0, 1) for q in range(4)]
        pairs = [split_even(quarters[2 * b], quarters[2 * b + 1]) for b in range(2)]
        return [pairs[b][0] for b in range(2)], [pairs[b][1] for b in range(2)]

    dens, source = fields(flat[0:64]), fields(flat[64:128])
    for c in range(2):
        for b in range(2):
            d0[c, b, 4:12, 0:8] = dens[c][b]
            g0[c, b, 4:12, 0:8] = source[c][b]
    for way in XS:
        dx = WAYS[way][1]
        for c in range(2):
            ax_s[way - 2, c] = d0[c, :, 4:12, x_own(dx, 4)]
            gx_s[way - 2, c] = g0[c, :, 4:12, x_own(dx, 2)]
    for way in CORNERS:
        dy, dx = WAYS[way]
        for b in range(2):
            ac_s[way - 4, 2 * b : 2 * b + 2] = d0[1, b, y_own(dy, 2), x_own(dx, 2)]
            an_s[way - 4, :, b : b + 1] = d0[1, b, y_own(dy, 1), x_own(dx, 1)]
            ac_s[way - 4, 4:5, b : b + 1] = d0[0, b, y_own(dy, 1), x_own(dx, 1)]
            ac_s[way - 4, 5:6, b : b + 1] = g0[0, b, y_own(dy, 1), x_own(dx, 1)]
    dens_one = coarsen(*dens)
    for c in range(2):
        strip[c, 6:10] = dens_one[c][0]
    gat[0, me] = coarsen(*dens_one)

    pl.semaphore_wait(barrier, nx * ny - 1)
    first_part, more_part = messages_first(), messages_more()
    start(FIRST, first_part)
    start(MORE, more_part)
    part_c, part_s = column_messages(), strip_messages()
    start(MID_C, part_c)
    along_y()
    finish(FIRST, first_part)
    for way in XS:
        dx = WAYS[way][1]
        for c in range(2):
            d0[c, :, 4:12, x_halo(dx, 4)] = ax_r[way - 2, c]
            g0[c, :, 4:12, x_halo(dx, 2)] = gx_r[way - 2, c]
    for way in CORNERS:
        dy, dx = WAYS[way]
        for b in range(2):
            d0[1, b, y_halo(dy, 1), x_halo(dx, 1)] = an_r[way - 4, :, b : b + 1]

    setup(k0, d0, 0, 1.0, 3, 13, FINE)
    setup(k0, d0, 1, 1.0, 4, 12, FINE)
    first(k0, g0, ra, 3, 13, FINE)
    update(k0, g0, ra, ba, 1, 4, 12, FINE)
    ring_pack(ba, 2, sx_s.at[0], sc_s.at[0])
    swap = ring_messages(ba, ba, 3, sx_s.at[0], sx_r.at[0], sc_s.at[0], sc_r.at[0])
    start(SWAP, swap)
    finish(MID_C, part_c)
    start(STRIP, part_s)
    finish(MORE, more_part)
    for way in CORNERS:
        dy, dx = WAYS[way]
        for b in range(2):
            d0[1, b, y_halo(dy, 2), x_halo(dx, 2)] = ac_r[way - 4, 2 * b : 2 * b + 2]
            d0[0, b, y_halo(dy, 1), x_halo(dx, 1)] = ac_r[way - 4, 4:5, b : b + 1]
            g0[0, b, y_halo(dy, 1), x_halo(dx, 1)] = ac_r[way - 4, 5:6, b : b + 1]
    setup(k0, d0, 0, 1.0, 2, 14, FINE)
    setup(k0, d0, 1, 1.0, 3, 13, FINE)
    along_x()
    finish(SWAP, swap)
    ring_unpack(ba, 2, sx_r.at[0], sc_r.at[0])
    update(k0, g0, ba, rb, 0, 2, 14, FINE)
    update(k0, g0, rb, bb, 1, 3, 13, FINE)
    source_one = coarsen(*residual(k0, g0, rb, bb, 4, 12, FINE, 0, 8))
    for c in range(2):
        blk_g[c] = source_one[c][0]
        g1[c, 0, 8:12, 8:12] = source_one[c][0]
    part_g, far_g = [], block_messages(blk_g, in_g, range(8, 12), 1)
    for way in NEAR:
        for c in range(2):
            part_g.append(source_message(way, c, near_part))
            if near_more(way, c):
                far_g.append(source_message(way, c, near_more))
    start(MID_G, part_g)
    start(FAR_G, far_g)
    ring_pack(bb, 2, sx_s.at[1], sc_s.at[1])
    keep = ring_messages(bb, bp, 3, sx_s.at[1], sx_r.at[1], sc_s.at[1], sc_r.at[1])
    start(KEEP, keep)

    def blocks(ref, got, ways, far):
        for way in ways:
            dy, dx = WAYS[way]
            part = block_part(way, far)
            y, x = 4 * (dy + 2), 4 * (dx + 2)
            for c in range(2):
                ref[c, 0, y + part.start : y + part.stop, x : x + 4] = got[way, c, part]

    finish(STRIP, part_s)
    columns()
    for c in range(2):
        setup(k1, d1, c, 0.25, 1, 19, MID[1])

    take(in_sem.at[PLANE], (nx - 1) * ny * slot)
    pairs, rows = ny, 2 * nx

    def assemble(n):
        for i in range(nx):
            for p in range(2):
                cc[p, :, 2 * i : 2 * i + 2] = gat[n, i * ny : (i + 1) * ny, p]
        even = (iota((pairs, rows, LANES), 1) + iota((pairs, rows, LANES), 2)) % 2 == 0
        return jnp.where(even, cc[0], cc[1]), jnp.where(even, cc[1], cc[0])

    shape = (pairs, rows, LANES)
    tested = (iota(shape, 1) + iota(shape, 2)) % 2

    def beside(other, colour):
        low = tested == colour
        return (
            jnp.where(low, jnp.concatenate([other[-1:], other[:-1]], axis=0), other),
            jnp.where(low, other, jnp.concatenate([other[1:], other[:1]], axis=0)),
            pltpu.roll(other, 1, 1), pltpu.roll(other, rows - 1, 1),
            pltpu.roll(other, 1, 2), pltpu.roll(other, LANES - 1, 2))

    centre = assemble(0)
    for c in range(2):
        low = tested == c
        edges = (
            jnp.logical_and(low, iota(shape, 0) == 0),
            jnp.logical_and(jnp.logical_not(low), iota(shape, 0) == pairs - 1),
            iota(shape, 1) == 0, iota(shape, 1) == rows - 1, iota(shape, 2) == 0, iota(shape, 2) == LANES - 1)
        total, faces = None, []
        for near, edge in zip(beside(centre[1 - c], c), edges):
            face = 0.03125 * (centre[c] + jnp.where(edge, 0.0, near))
            total = face if total is None else total + face
            faces.append(face)
        inverse = 1.0 / total
        for f in range(6):
            kc[c, f] = jnp.where(edges[f], 0.0, faces[f] * inverse)
        kc[c, 6] = inverse

    finish(MID_G, part_g)
    sources(near_part)
    first(k1, g1, mr, 4, 16, 16)
    update(k1, g1, mr, mb, 1, 5, 15, 16)
    update(k1, g1, mb, mr, 0, 6, 14, 16)
    update(k1, g1, mr, mb, 1, 7, 13, 16)
    gat[1, me] = coarsen(*residual(k1, g1, mr, mb, 8, 12, 16, 8, 12))
    spread()
    blk_x[...] = mb[0, 8:12, 8:12]
    part_x = block_messages(blk_x, in_x, range(20), 2)
    start(MID_X, part_x)

    take(in_sem.at[GATHER], (nx * ny - 1) * slot)
    right = assemble(1)
    for c in range(2):
        kc[c, 7] = right[c] * kc[c, 6]

    def half(other, colour):
        total = kc[colour, 7]
        for f, near in enumerate(beside(other, colour)):
            total = total + kc[colour, f] * near
        return total

    def sweep(i, carry):
        red = half(carry[1], 0)
        return red, half(red, 1)

    red = kc[0, 7]
    red, black = lax.fori_loop(1, COARSE_SWEEPS, sweep, (red, half(red, 1)))
    even = tested == 0
    for i in range(nx):
        cut = slice(2 * i, 2 * i + 2)
        vc[2 + i, 2 : 2 + ny, 0] = jnp.where(even, red, black)[:, cut]
        vc[2 + i, 2 : 2 + ny, 1] = jnp.where(even, black, red)[:, cut]

    finish(MID_X, part_x)
    finish(FAR_G, far_g)
    blocks(g1, in_g, range(8, 12), 1)
    sources(near_more)
    mp[0, 8:12, 8:12] = blk_x[...]
    for way in range(20):
        dy, dx = WAYS[way]
        part = block_part(way, 2)
        y, x = 4 * (dy + 2), 4 * (dx + 2)
        mp[0, y + part.start : y + part.stop, x : x + 4] = in_x[way, part]
    for dx in range(5):
        window = vc[gx + dx, pl.ds(gy, 5)].reshape(10, 2, LANES)
        mp[0, :, 4 * dx : 4 * dx + 4] = mp[0, :, 4 * dx : 4 * dx + 4] + double_rows(window, (0, 1))
    update(k1, g1, mp, mr, 0, 3, 17, MID[1])
    update(k1, g1, mr, mb, 1, 4, 16, MID[1])
    update(k1, g1, mb, mr, 0, 5, 15, MID[1])
    update(k1, g1, mr, mb, 1, 6, 14, MID[1])

    finish(KEEP, keep)
    bp[:, 4:12, 0:8] = bb[:, 4:12, 0:8]
    ring_unpack(bp, 2, sx_r.at[1], sc_r.at[1])
    half_z = split_even(mr[0, 6:14], mb[0, 6:14])
    for b in range(2):
        bp[b] = bp[b] + double_rows(half_z[b], (8, 9, 10, 11, 12, 13, 6, 7))
    update(k0, g0, bp, rc, 0, 2, 14, FINE)
    update(k0, g0, rc, bc, 1, 3, 13, FINE)
    update(k0, g0, bc, rd, 0, 4, 12, FINE)
    ring_pack(rd, 1, ex_s, ec_s)
    last = ring_messages(rd, rd, 2, ex_s, ex_r, ec_s, ec_r)
    start(LAST, last)
    finish(LAST, last)
    ring_unpack(rd, 1, ex_r, ec_r)
    update(k0, g0, rd, bd, 1, 3, 13, FINE)
    left = residual(k0, g0, rd, bd, 4, 12, FINE, 0, 8)

    def lay(red, black):
        quarters = []
        for b in range(2):
            quarters.extend(split_even(red[b], black[b]))
        return jnp.concatenate([jnp.swapaxes(q, 0, 1).reshape(64, LANES) for q in quarters], axis=1)

    field = [[ref[b, 4:12, 0:8] for b in range(2)] for ref in (rd, bd)]
    flat = permute(jnp.concatenate([lay(*field), lay(*left)], axis=0), perm[...], 1)
    v_out[...] = flat[0:64].reshape(v_out.shape)
    r_out[...] = flat[64:128].reshape(r_out.shape)
    all_sent()


def hand_out(v_ref, r_ref, v_out, r_out, sem):
    copies = [
        pltpu.make_async_copy(src, dst, sem.at[n]) for n, (src, dst) in enumerate(((v_ref, v_out), (r_ref, r_out)))
    ]
    for copy in copies:
        copy.start()
    for copy in copies:
        copy.wait()


def solution(mesh):
    nx, ny = mesh.shape["gx"], mesh.shape["gy"]

    def shards(right_side, inverse_density):
        x, y, z = right_side.shape
        assert (x, y, z) == (8, 8, 4 * LANES)

        def vmem(*shape):
            return pltpu.VMEM((*shape, LANES), F32)

        fine = (2, FINE, FINE)
        mid = (1, *MID)
        result = pltpu.VMEM(right_side.shape, F32)
        v, r = pl.pallas_call(
            functools.partial(kernel, nx, ny),
            out_shape=(result, result),
            in_specs=[pl.BlockSpec(memory_space=pl.ANY)] * 2,
            out_specs=(pl.BlockSpec(memory_space=pltpu.VMEM),) * 2,
            scratch_shapes=[
                pltpu.VMEM((z, z), jnp.bfloat16),
                pltpu.VMEM((2, x, y, z), F32),
                vmem(2, *fine), vmem(2, *fine), vmem(2, 2, 8, FINE, FINE),
                *[vmem(*fine)] * 9,
                vmem(2, 2, 2, 8, 4), vmem(3, 2, 2, 8, 4), vmem(2, 2, 2, 8, 2), vmem(3, 2, 2, 8, 2), vmem(4, 1, 2), vmem(5, 1, 2), vmem(4, 6, 2), vmem(5, 6, 2),
                vmem(2, 2, 2, 8, 4), vmem(2, 3, 2, 8, 4), vmem(2, 4, 2, 2, 2), vmem(2, 5, 2, 2, 2),
                vmem(2, 2, 8, 2), vmem(3, 2, 8, 2), vmem(4, 2, 1, 1), vmem(5, 2, 1, 1),
                vmem(2, *mid), vmem(2, *mid), vmem(2, 1, 8, *MID), *[vmem(*mid)] * 3,
                vmem(2, 16, 4), vmem(2, 4, 4), vmem(4, 4),
                vmem(5, 2, 16, 4), vmem(len(WAYS) + 1, 2, 4, 4), vmem(len(WAYS) + 1, 4, 4),
                vmem(2, nx * ny, 2, 2), vmem(2, ny, 2 * nx), vmem(2, 8, ny, 2 * nx), vmem(nx + 4, ny + 4, 2, 2),
                vmem(2, 3, 8), vmem(2048),
                pltpu.SemaphoreType.DMA,
                pltpu.SemaphoreType.DMA((len(WAYS),)),
                pltpu.SemaphoreType.DMA((3,)),
                pltpu.SemaphoreType.DMA((PHASES,)),
            ],
            compiler_params=pltpu.CompilerParams(
                collective_id=0, has_side_effects=True, vmem_limit_bytes=40 * 1024 * 1024
            ),
        )(*(pltpu.with_memory_space_constraint(a, pltpu.HBM) for a in (right_side, inverse_density)))
        out = jax.ShapeDtypeStruct(right_side.shape, F32)
        return pl.pallas_call(
            hand_out,
            out_shape=(out, out),
            in_specs=[pl.BlockSpec(memory_space=pltpu.VMEM)] * 2,
            out_specs=(pl.BlockSpec(memory_space=pl.ANY),) * 2,
            scratch_shapes=[pltpu.SemaphoreType.DMA((2,))],
            compiler_params=pltpu.CompilerParams(vmem_limit_bytes=1024 * 1024),
        )(v, r)

    spec = P("gx", "gy", None)
    return jax.shard_map(shards, mesh=mesh, in_specs=(spec, spec), out_specs=(spec, spec), check_vma=False)
```

```python
import functools
import math

import jax
import jax.numpy as jnp
from jax import lax
from jax.experimental import pallas as pl
from jax.experimental.pallas import tpu as pltpu
from jax.sharding import PartitionSpec as P

SWEEPS = 2
COARSE_SWEEPS = 8
MESH = pl.DeviceIdType.MESH
LANES = 128
F32 = jnp.float32

FINE, MID = 16, (20, 16)

WAYS = ((-1, 0), (1, 0), (0, -1), (0, 1), (-1, -1), (-1, 1), (1, -1), (1, 1),
        (-2, 0), (2, 0), (0, -2), (0, 2),
        (-2, -1), (-2, 1), (2, -1), (2, 1), (-1, -2), (-1, 2), (1, -2), (1, 2))
BACK = tuple(WAYS.index((-dy, -dx)) for dy, dx in WAYS)
FIRST, MORE, SWAP, KEEP, LAST, MID_C, STRIP, MID_G, FAR_G, MID_X = range(10)
GATHER, LINE, PLANE = 10, 11, 12
PHASES = 13
YS, XS, CORNERS, NEAR = (0, 1), (2, 3), (4, 5, 6, 7), range(8)


def iota(shape, dim):
    return lax.broadcasted_iota(jnp.int32, shape, dim)


def lane_prev(a):
    return jnp.where(iota(a.shape, 2) == 0, 0.0, pltpu.roll(a, 1, 2))


def lane_next(a):
    return jnp.where(iota(a.shape, 2) == LANES - 1, 0.0, pltpu.roll(a, LANES - 1, 2))


def even_cells(shape):
    return (iota(shape, 0) + iota(shape, 1)) % 2 == 0


def z_other(o, colour, first):
    shape = o[0].shape
    even = (iota(shape, 0) + iota(shape, 1)) % 2 == first % 2
    low = even if colour == 0 else jnp.logical_not(even)
    last = len(o) - 1
    out = []
    for b in range(last + 1):
        before = o[b - 1] if b > 0 else lane_prev(o[last])
        after = o[b + 1] if b < last else lane_next(o[0])
        out.append(jnp.where(low, before, after))
    return out


def around(other, colour, y0, y1, rows):
    groups = range(other.shape[0])
    mid = [other[b, y0:y1, 0:rows] for b in groups]
    zo = z_other(mid, colour, y0)
    return [
        (
            other[b, y0 - 1 : y1 - 1, 0:rows],
            other[b, y0 + 1 : y1 + 1, 0:rows],
            pltpu.roll(mid[b], 1, 1),
            pltpu.roll(mid[b], rows - 1, 1),
            mid[b],
            zo[b],
        )
        for b in groups
    ]


def split_even(zero, one):
    even = even_cells(zero.shape)
    return jnp.where(even, zero, one), jnp.where(even, one, zero)


def pair_rows(a):
    rows = a.shape[1] // 2
    a = a.reshape(a.shape[0] // 2, 2, a.shape[1], LANES)
    a = a[:, 0] + a[:, 1]
    pick = iota((a.shape[0], rows, LANES), 1)
    out = a[:, 0:1] + a[:, 1:2]
    out = jnp.broadcast_to(out, pick.shape)
    for j in range(1, rows):
        out = jnp.where(pick == j, a[:, 2 * j : 2 * j + 1] + a[:, 2 * j + 1 : 2 * j + 2], out)
    return out * 0.125


def double_rows(a, order):
    y = a.shape[0]
    pick = iota((y, 2 * len(order), LANES), 1) // 2
    out = jnp.broadcast_to(a[:, order[0] : order[0] + 1], pick.shape)
    for n, j in enumerate(order[1:], 1):
        out = jnp.where(pick == n, a[:, j : j + 1], out)
    return jnp.concatenate([out[i // 2 : i // 2 + 1] for i in range(2 * y)], axis=0)


def three(x):
    high = x.astype(jnp.bfloat16)
    rest = x - high.astype(F32)
    middle = rest.astype(jnp.bfloat16)
    low = (rest - middle.astype(F32)).astype(jnp.bfloat16)
    return jnp.concatenate([high, middle, low], axis=0)


def permute(x, matrix, side):
    n = x.shape[0]
    out = lax.dot_general(three(x), matrix, (((1,), (side,)), ((), ())), preferred_element_type=F32)
    return (out[0:n] + out[n : 2 * n]) + out[2 * n :]


def y_own(d, w):
    return slice(4, 12) if d == 0 else (slice(12 - w, 12) if d > 0 else slice(4, 4 + w))


def y_halo(d, w):
    return slice(4, 12) if d == 0 else (slice(12, 12 + w) if d > 0 else slice(4 - w, 4))


def x_own(d, w):
    return slice(0, 8) if d == 0 else (slice(8 - w, 8) if d > 0 else slice(0, w))


def x_halo(d, w):
    return slice(0, 8) if d == 0 else (slice(8, 8 + w) if d > 0 else slice(FINE - w, FINE))


def columns_of(dx):
    start = 6 + 4 * dx
    low, high = max(start, 0), min(start + 4, MID[1])
    return slice(low, high), slice(low - start, high - start)


def outer(part, d):
    return slice(part.stop - 1, part.stop) if d > 0 else slice(part.start, part.start + 1)


def block_part(way, far):
    dy, dx = WAYS[way]
    n = far if abs(dy) == 2 else (2 if abs(dx) == 2 and dy else 4)
    return slice(0, n) if dy > 0 else slice(4 - n, 4)


def kernel(nx, ny, g_ref, c_ref, v_out, r_out, perm, held, d0, g0, k0, ra, ba, rb, bb, bp, rc, bc, rd, bd,
           ax_s, ax_r, gx_s, gx_r, an_s, an_r, ac_s, ac_r, sx_s, sx_r, sc_s, sc_r, ex_s, ex_r, ec_s, ec_r,
           d1, g1, k1, mr, mb, mp, strip, blk_g, blk_x, in_c, in_g, in_x,
           gat, cc, kc, vc, zero_y, bulk, held_sem, lead_sem, out_sem, gone_sem, in_sem):
    gx, gy = lax.axis_index("gx"), lax.axis_index("gy")

    def inside(way):
        dy, dx = WAYS[way]
        tests = []
        if dy:
            tests.append(gy + dy >= 0 if dy < 0 else gy + dy < ny)
        if dx:
            tests.append(gx + dx >= 0 if dx < 0 else gx + dx < nx)
        return tests[0] if len(tests) == 1 else jnp.logical_and(*tests)

    def device(way):
        dy, dx = WAYS[way]
        out = {}
        if dx:
            out["gx"] = gx + dx
        if dy:
            out["gy"] = gy + dy
        return out

    has = [inside(way) for way in range(len(WAYS))]
    target = [device(way) for way in range(len(WAYS))]

    def each_peer(fn):
        if nx * ny <= 64:
            for s in range(1, nx * ny):
                fn(s, s // ny, s % ny)
        else:
            def body(s, carry):
                fn(s, s // ny, lax.rem(s, ny))
                return carry
            lax.fori_loop(1, nx * ny, body, 0)

    loads = [
        pltpu.make_async_copy(ref.at[i : i + 2], held.at[n, i : i + 2], held_sem)
        for n, ref in enumerate((c_ref, g_ref)) for i in range(0, 8, 2)
    ]
    for load in loads:
        load.start()

    barrier = pltpu.get_barrier_semaphore()

    def greet(s, sx, sy):
        pl.semaphore_signal(
            barrier, inc=1, device_id={"gx": lax.rem(gx + sx, nx), "gy": lax.rem(gy + sy, ny)}, device_id_type=MESH)

    each_peer(greet)

    for ref in (ax_r, gx_r, ex_r):
        ref[2] = jnp.zeros(ref.shape[1:], F32)
    for ref in (an_r, ac_r, ec_r):
        ref[4] = jnp.zeros(ref.shape[1:], F32)
    for n in range(2):
        sx_r[n, 2] = jnp.zeros(sx_r.shape[2:], F32)
        sc_r[n, 4] = jnp.zeros(sc_r.shape[2:], F32)
    in_c[4] = jnp.zeros(in_c.shape[1:], F32)
    for ref in (in_g, in_x):
        ref[len(WAYS)] = jnp.zeros(ref.shape[1:], F32)
    zero_y[...] = jnp.zeros(zero_y.shape, F32)
    vc[...] = jnp.zeros(vc.shape, F32)

    size_z = 4 * LANES
    row, col = iota((size_z, size_z), 0), iota((size_z, size_z), 1)
    perm[...] = (row == 4 * (col % LANES) + col // LANES).astype(F32).astype(jnp.bfloat16)

    def coarsen(red, black):
        pair = [pair_rows(red[b] + black[b]) for b in range(len(red))]
        if len(pair) == 1:
            return pair[0]
        first, second = split_even(pair[0], pair[1])
        return [first], [second]

    def remote(phase, way, src, dst):
        lead = phase == FIRST and way in YS
        return pltpu.make_async_remote_copy(
            src_ref=src, dst_ref=dst, send_sem=lead_sem.at[way] if lead else out_sem.at[way], recv_sem=in_sem.at[phase],
            device_id=target[way], device_id_type=MESH)

    def size(ref):
        return math.prod(ref.shape[:-1])

    def take(sem, rows):
        pltpu.make_async_copy(bulk.at[0:rows], bulk.at[0:rows], sem).wait()

    def ring_messages(src, dst, w, x_s, x_r, c_s, c_r):
        out = []
        for way in YS:
            dy = WAYS[way][0]
            out.append((way, src.at[:, y_own(dy, w), 0:8], dst.at[:, y_halo(-dy, w), 0:8], dst.at[:, y_halo(dy, w), 0:8], zero_y.at[:, 0:w]))
        for way in XS:
            out.append((way, x_s.at[way - 2], x_r.at[BACK[way] - 2], x_r.at[way - 2], x_r.at[2]))
        for way in CORNERS:
            out.append((way, c_s.at[way - 4], c_r.at[BACK[way] - 4], c_r.at[way - 4], c_r.at[4]))
        return out

    def ring_pack(src, cw, x_s, c_s):
        for way in XS:
            x_s[way - 2] = src[:, 4:12, x_own(WAYS[way][1], x_s.shape[-2])]
        for way in CORNERS:
            dy, dx = WAYS[way]
            c_s[way - 4] = src[:, y_own(dy, cw), x_own(dx, cw)]

    def ring_unpack(dst, cw, x_r, c_r):
        for way in XS:
            dst[:, 4:12, x_halo(WAYS[way][1], x_r.shape[-2])] = x_r[way - 2]
        for way in CORNERS:
            dy, dx = WAYS[way]
            dst[:, y_halo(dy, cw), x_halo(dx, cw)] = c_r[way - 4]

    def rows_y(ref, colour, w, only, way):
        dy = WAYS[way][0]
        own, there, here = y_own(dy, w), y_halo(-dy, w), y_halo(dy, w)
        if only:
            own, there, here = (outer(a, d) for a, d in ((own, -dy), (there, -dy), (here, dy)))
        n = 1 if only else w
        return (way, ref.at[colour, :, own, 0:8], ref.at[colour, :, there, 0:8], ref.at[colour, :, here, 0:8],
                zero_y.at[:, 0:n])

    def messages_first():
        out = []
        for way in YS:
            for ref, colour, w in ((d0, 0, 1), (d0, 1, 2), (g0, 0, 1)):
                out.append(rows_y(ref, colour, w, False, way))
        for way in CORNERS:
            out.append((way, an_s.at[way - 4], an_r.at[BACK[way] - 4], an_r.at[way - 4], an_r.at[4]))
        for way in XS:
            out.append((way, ax_s.at[way - 2], ax_r.at[BACK[way] - 2], ax_r.at[way - 2], ax_r.at[2]))
            out.append((way, gx_s.at[way - 2], gx_r.at[BACK[way] - 2], gx_r.at[way - 2], gx_r.at[2]))
        return out

    def messages_more():
        out = []
        for way in YS:
            for ref, colour, w in ((d0, 0, 2), (d0, 1, 3), (g0, 0, 2), (g0, 1, 1)):
                out.append(rows_y(ref, colour, w, True, way))
        for way in CORNERS:
            out.append((way, ac_s.at[way - 4], ac_r.at[BACK[way] - 4], ac_r.at[way - 4], ac_r.at[4]))
        return out

    def block_messages(src, dst, ways, far):
        out = []
        for way in ways:
            give, got = block_part(BACK[way], far), block_part(way, far)
            lead = (slice(None),) * (len(src.shape) - 3)
            out.append((way, src.at[(*lead, give)], dst.at[(BACK[way], *lead, give)], dst.at[(way, *lead, got)],
                        dst.at[(len(WAYS), *lead, got)]))
        return out

    def near_part(way, c):
        n = 4 if way in XS else ((4, 3)[c] if way in YS else (3, 2)[c])
        dy = WAYS[way][0]
        return slice(0, n) if dy > 0 else slice(4 - n, 4)

    def near_more(way, c):
        n = {YS: (0, 4), XS: (0, 0), CORNERS: (4, 3)}[YS if way in YS else (XS if way in XS else CORNERS)][c]
        dy = WAYS[way][0]
        return (slice(n - 1, n) if dy > 0 else slice(4 - n, 5 - n)) if n else None

    def source_message(way, c, part):
        give, got = part(BACK[way], c), part(way, c)
        return (way, blk_g.at[c, give], in_g.at[BACK[way], c, give], in_g.at[way, c, got], in_g.at[len(WAYS), c, got])

    def sources(part):
        for way in NEAR:
            y, (to, of) = 4 * (WAYS[way][0] + 2), columns_of(WAYS[way][1])
            for c in range(2):
                rows = part(way, c)
                if rows:
                    g1[c, 0, y + rows.start : y + rows.stop, to] = in_g[way, c, rows, of]

    def column_messages():
        out = []
        for way in (0, 1, 8, 9):
            dy = WAYS[way][0]
            give, there, here = {
                -1: (slice(6, 10), slice(10, 14), slice(2, 6)), 1: (slice(6, 10), slice(2, 6), slice(10, 14)),
                -2: (slice(6, 8), slice(14, 16), slice(0, 2)), 2: (slice(8, 10), slice(0, 2), slice(14, 16))}[dy]
            out.append((way, strip.at[:, give], strip.at[:, there], strip.at[:, here], in_c.at[4, :, give]))
        return out

    def strip_messages():
        out = []
        for n, way in enumerate((2, 3, 10, 11)):
            part = slice(0, 16) if n < 2 else slice(4, 12)
            out.append((way, strip.at[:, part], in_c.at[n ^ 1, :, part], in_c.at[n, :, part], in_c.at[4, :, part]))
        return out

    def columns():
        for c in range(2):
            d1[c, 0, 2:18, 6:10] = strip[c]
            for n, way in enumerate((2, 3, 10, 11)):
                part = slice(0, 16) if n < 2 else slice(4, 12)
                to, of = columns_of(WAYS[way][1])
                d1[c, 0, 2 + part.start : 2 + part.stop, to] = in_c[n, c, part, of]

    def by_way(messages):
        ways = {}
        for m in messages:
            ways.setdefault(m[0], []).append(m)
        return ways.items()

    sent = {}

    def start(phase, messages):
        for way, group in by_way(messages):
            @pl.when(has[way])
            def _():
                for _, src, there, here, zeros in group:
                    remote(phase, way, src, there).start()

            @pl.when(jnp.logical_not(has[way]))
            def _():
                for _, src, there, here, zeros in group:
                    pltpu.make_async_copy(zeros, here, in_sem.at[phase]).start()

            if phase != FIRST or way not in YS:
                sent[way] = sent.get(way, 0) + sum(size(m[1]) for m in group)

    def finish(phase, messages):
        take(in_sem.at[phase], sum(size(m[3]) for m in messages))

    def first_sent():
        for way in YS:
            @pl.when(has[way])
            def _():
                take(lead_sem.at[way], sum(size(m[1]) for m in first_part if m[0] == way))

    def all_sent():
        for way, rows in sent.items():
            @pl.when(has[way])
            def _():
                take(out_sem.at[way], rows)
        for n, slots in enumerate((nx * ny - 1, ny - 1, (nx - 1) * ny)):
            take(gone_sem.at[n], slots * slot)

    me = gx * ny + gy
    def spread():
        def body(s, sx, sy):
            pltpu.make_async_remote_copy(
                src_ref=gat.at[1, me], dst_ref=gat.at[1, me], send_sem=gone_sem.at[0], recv_sem=in_sem.at[GATHER],
                device_id={"gx": lax.rem(gx + sx, nx), "gy": lax.rem(gy + sy, ny)}, device_id_type=MESH).start()
        each_peer(body)

    slot = size(gat.at[0, 0])

    def along_y():
        for sy in range(1, ny):
            pltpu.make_async_remote_copy(
                src_ref=gat.at[0, me], dst_ref=gat.at[0, me], send_sem=gone_sem.at[1], recv_sem=in_sem.at[LINE],
                device_id={"gy": lax.rem(gy + sy, ny)}, device_id_type=MESH).start()

    def along_x():
        take(in_sem.at[LINE], (ny - 1) * slot)
        line = gat.at[0, pl.ds(gx * ny, ny)]
        for sx in range(1, nx):
            pltpu.make_async_remote_copy(
                src_ref=line, dst_ref=line, send_sem=gone_sem.at[2], recv_sem=in_sem.at[PLANE],
                device_id={"gx": lax.rem(gx + sx, nx)}, device_id_type=MESH).start()

    def setup(kref, dens, colour, scale, y0, y1, rows):
        for b, near in enumerate(around(dens.at[1 - colour], colour, y0, y1, rows)):
            here = dens[colour, b, y0:y1, 0:rows]
            total = None
            for f in range(6):
                face = (scale * 0.5) * (here + near[f])
                kref[colour, b, f, y0:y1, 0:rows] = face
                total = face if total is None else total + face
            kref[colour, b, 6, y0:y1, 0:rows] = total
            kref[colour, b, 7, y0:y1, 0:rows] = jnp.where(here > 0.0, 1.0 / total, 0.0)

    def weigh(kref, other, colour, y0, y1, rows):
        out = []
        for b, near in enumerate(around(other, colour, y0, y1, rows)):
            total = kref[colour, b, 0, y0:y1, 0:rows] * near[0]
            for f in range(1, 6):
                total = total + kref[colour, b, f, y0:y1, 0:rows] * near[f]
            out.append(total)
        return out

    def update(kref, g, other, dst, colour, y0, y1, rows):
        for b, n in enumerate(weigh(kref, other, colour, y0, y1, rows)):
            dst[b, y0:y1, 0:rows] = (g[colour, b, y0:y1, 0:rows] + n) * kref[colour, b, 7, y0:y1, 0:rows]

    def first(kref, g, dst, y0, y1, rows):
        for b in range(dst.shape[0]):
            dst[b, y0:y1, 0:rows] = g[0, b, y0:y1, 0:rows] * kref[0, b, 7, y0:y1, 0:rows]

    def residual(kref, g, red, black, y0, y1, rows, x0, x1):
        out = []
        for c, (v, other) in enumerate(((red, black), (black, red))):
            n = weigh(kref, other, c, y0, y1, rows)
            out.append([
                (g[c, b, y0:y1, 0:rows] - (kref[c, b, 6, y0:y1, 0:rows] * v[b, y0:y1, 0:rows] - n[b]))[:, x0:x1]
                for b in range(len(n))])
        return out

    pltpu.make_async_copy(held, held, held_sem).wait()
    flat = permute(held[...].reshape(-1, size_z), perm[...], 0)

    def fields(flat):
        quarters = [
            jnp.swapaxes(flat[:, q * LANES : (q + 1) * LANES].reshape(8, 8, LANES), 0, 1) for q in range(4)]
        pairs = [split_even(quarters[2 * b], quarters[2 * b + 1]) for b in range(2)]
        return [pairs[b][0] for b in range(2)], [pairs[b][1] for b in range(2)]

    dens, source = fields(flat[0:64]), fields(flat[64:128])
    for c in range(2):
        for b in range(2):
            d0[c, b, 4:12, 0:8] = dens[c][b]
            g0[c, b, 4:12, 0:8] = source[c][b]
    for way in XS:
        dx = WAYS[way][1]
        for c in range(2):
            ax_s[way - 2, c] = d0[c, :, 4:12, x_own(dx, 4)]
            gx_s[way - 2, c] = g0[c, :, 4:12, x_own(dx, 2)]
    for way in CORNERS:
        dy, dx = WAYS[way]
        for b in range(2):
            ac_s[way - 4, 2 * b : 2 * b + 2] = d0[1, b, y_own(dy, 2), x_own(dx, 2)]
            an_s[way - 4, :, b : b + 1] = d0[1, b, y_own(dy, 1), x_own(dx, 1)]
            ac_s[way - 4, 4:5, b : b + 1] = d0[0, b, y_own(dy, 1), x_own(dx, 1)]
            ac_s[way - 4, 5:6, b : b + 1] = g0[0, b, y_own(dy, 1), x_own(dx, 1)]
    dens_one = coarsen(*dens)
    for c in range(2):
        strip[c, 6:10] = dens_one[c][0]
    gat[0, me] = coarsen(*dens_one)

    pl.semaphore_wait(barrier, nx * ny - 1)
    first_part, more_part = messages_first(), messages_more()
    start(FIRST, first_part)
    first_sent()
    start(MORE, more_part)
    part_c, part_s = column_messages(), strip_messages()
    start(MID_C, part_c)
    along_y()
    finish(FIRST, first_part)
    for way in XS:
        dx = WAYS[way][1]
        for c in range(2):
            d0[c, :, 4:12, x_halo(dx, 4)] = ax_r[way - 2, c]
            g0[c, :, 4:12, x_halo(dx, 2)] = gx_r[way - 2, c]
    for way in CORNERS:
        dy, dx = WAYS[way]
        for b in range(2):
            d0[1, b, y_halo(dy, 1), x_halo(dx, 1)] = an_r[way - 4, :, b : b + 1]

    setup(k0, d0, 0, 1.0, 3, 13, FINE)
    setup(k0, d0, 1, 1.0, 4, 12, FINE)
    first(k0, g0, ra, 3, 13, FINE)
    update(k0, g0, ra, ba, 1, 4, 12, FINE)
    ring_pack(ba, 2, sx_s.at[0], sc_s.at[0])
    swap = ring_messages(ba, ba, 3, sx_s.at[0], sx_r.at[0], sc_s.at[0], sc_r.at[0])
    start(SWAP, swap)
    finish(MID_C, part_c)
    start(STRIP, part_s)
    finish(MORE, more_part)
    for way in CORNERS:
        dy, dx = WAYS[way]
        for b in range(2):
            d0[1, b, y_halo(dy, 2), x_halo(dx, 2)] = ac_r[way - 4, 2 * b : 2 * b + 2]
            d0[0, b, y_halo(dy, 1), x_halo(dx, 1)] = ac_r[way - 4, 4:5, b : b + 1]
            g0[0, b, y_halo(dy, 1), x_halo(dx, 1)] = ac_r[way - 4, 5:6, b : b + 1]
    setup(k0, d0, 0, 1.0, 2, 14, FINE)
    setup(k0, d0, 1, 1.0, 3, 13, FINE)
    along_x()
    finish(SWAP, swap)
    ring_unpack(ba, 2, sx_r.at[0], sc_r.at[0])
    update(k0, g0, ba, rb, 0, 2, 14, FINE)
    update(k0, g0, rb, bb, 1, 3, 13, FINE)
    source_one = coarsen(*residual(k0, g0, rb, bb, 4, 12, FINE, 0, 8))
    for c in range(2):
        blk_g[c] = source_one[c][0]
        g1[c, 0, 8:12, 6:10] = source_one[c][0]
    part_g, far_g = [], block_messages(blk_g, in_g, range(8, 12), 1)
    for way in NEAR:
        for c in range(2):
            part_g.append(source_message(way, c, near_part))
            if near_more(way, c):
                far_g.append(source_message(way, c, near_more))
    start(MID_G, part_g)

    def blocks(ref, got, ways, far):
        for way in ways:
            dy, dx = WAYS[way]
            part = block_part(way, far)
            y, (to, of) = 4 * (dy + 2), columns_of(dx)
            for c in range(2):
                ref[c, 0, y + part.start : y + part.stop, to] = got[way, c, part, of]

    finish(STRIP, part_s)
    columns()
    for c in range(2):
        setup(k1, d1, c, 0.25, 3 + c, 17 - c, MID[1])

    take(in_sem.at[PLANE], (nx - 1) * ny * slot)
    pairs, rows = ny, 2 * nx

    def assemble(n):
        for i in range(nx):
            for p in range(2):
                cc[p, :, 2 * i : 2 * i + 2] = gat[n, i * ny : (i + 1) * ny, p]
        even = (iota((pairs, rows, LANES), 1) + iota((pairs, rows, LANES), 2)) % 2 == 0
        return jnp.where(even, cc[0], cc[1]), jnp.where(even, cc[1], cc[0])

    shape = (pairs, rows, LANES)
    tested = (iota(shape, 1) + iota(shape, 2)) % 2

    def beside(other, colour):
        low = tested == colour
        return (
            jnp.where(low, jnp.concatenate([other[-1:], other[:-1]], axis=0), other),
            jnp.where(low, other, jnp.concatenate([other[1:], other[:1]], axis=0)),
            pltpu.roll(other, 1, 1), pltpu.roll(other, rows - 1, 1),
            pltpu.roll(other, 1, 2), pltpu.roll(other, LANES - 1, 2))

    centre = assemble(0)
    for c in range(2):
        low = tested == c
        edges = (
            jnp.logical_and(low, iota(shape, 0) == 0),
            jnp.logical_and(jnp.logical_not(low), iota(shape, 0) == pairs - 1),
            iota(shape, 1) == 0, iota(shape, 1) == rows - 1, iota(shape, 2) == 0, iota(shape, 2) == LANES - 1)
        total, faces = None, []
        for near, edge in zip(beside(centre[1 - c], c), edges):
            face = 0.03125 * (centre[c] + jnp.where(edge, 0.0, near))
            total = face if total is None else total + face
            faces.append(face)
        inverse = 1.0 / total
        for f in range(6):
            kc[c, f] = jnp.where(edges[f], 0.0, faces[f] * inverse)
        kc[c, 6] = inverse

    finish(MID_G, part_g)
    sources(near_part)
    first(k1, g1, mr, 4, 16, 16)
    update(k1, g1, mr, mb, 1, 5, 15, 16)
    update(k1, g1, mb, mr, 0, 6, 14, 16)
    update(k1, g1, mr, mb, 1, 7, 13, 16)
    gat[1, me] = coarsen(*residual(k1, g1, mr, mb, 8, 12, 16, 6, 10))
    spread()
    start(FAR_G, far_g)
    ring_pack(bb, 2, sx_s.at[1], sc_s.at[1])
    keep = ring_messages(bb, bp, 3, sx_s.at[1], sx_r.at[1], sc_s.at[1], sc_r.at[1])
    start(KEEP, keep)
    blk_x[...] = mb[0, 8:12, 6:10]
    part_x = block_messages(blk_x, in_x, range(20), 2)
    start(MID_X, part_x)

    take(in_sem.at[GATHER], (nx * ny - 1) * slot)
    right = assemble(1)
    for c in range(2):
        kc[c, 7] = right[c] * kc[c, 6]

    def half(other, colour):
        total = kc[colour, 7]
        for f, near in enumerate(beside(other, colour)):
            total = total + kc[colour, f] * near
        return total

    def sweep(i, carry):
        red = half(carry[1], 0)
        return red, half(red, 1)

    red = kc[0, 7]
    red, black = lax.fori_loop(1, COARSE_SWEEPS, sweep, (red, half(red, 1)), unroll=True)
    even = tested == 0
    for i in range(nx):
        cut = slice(2 * i, 2 * i + 2)
        vc[2 + i, 2 : 2 + ny, 0] = jnp.where(even, red, black)[:, cut]
        vc[2 + i, 2 : 2 + ny, 1] = jnp.where(even, black, red)[:, cut]

    finish(MID_X, part_x)
    finish(FAR_G, far_g)
    blocks(g1, in_g, range(8, 12), 1)
    sources(near_more)
    mp[0, 8:12, 6:10] = blk_x[...]
    for way in range(20):
        dy, dx = WAYS[way]
        part = block_part(way, 2)
        y, (to, of) = 4 * (dy + 2), columns_of(dx)
        mp[0, y + part.start : y + part.stop, to] = in_x[way, part, of]
    for dx in range(5):
        window = vc[gx + dx, pl.ds(gy, 5)].reshape(10, 2, LANES)
        to, of = columns_of(dx - 2)
        mp[0, :, to] = mp[0, :, to] + double_rows(window, (0, 1))[:, of]
    update(k1, g1, mp, mr, 0, 3, 17, MID[1])
    update(k1, g1, mr, mb, 1, 4, 16, MID[1])
    update(k1, g1, mb, mr, 0, 5, 15, MID[1])
    update(k1, g1, mr, mb, 1, 6, 14, MID[1])

    finish(KEEP, keep)
    bp[:, 4:12, 0:8] = bb[:, 4:12, 0:8]
    ring_unpack(bp, 2, sx_r.at[1], sc_r.at[1])
    half_z = split_even(mr[0, 6:14], mb[0, 6:14])
    for b in range(2):
        bp[b] = bp[b] + double_rows(half_z[b], (6, 7, 8, 9, 10, 11, 4, 5))
    update(k0, g0, bp, rc, 0, 2, 14, FINE)
    update(k0, g0, rc, bc, 1, 3, 13, FINE)
    update(k0, g0, bc, rd, 0, 4, 12, FINE)
    ring_pack(rd, 1, ex_s, ec_s)
    last = ring_messages(rd, rd, 2, ex_s, ex_r, ec_s, ec_r)
    start(LAST, last)
    finish(LAST, last)
    ring_unpack(rd, 1, ex_r, ec_r)
    update(k0, g0, rd, bd, 1, 3, 13, FINE)
    left = residual(k0, g0, rd, bd, 4, 12, FINE, 0, 8)

    def lay(red, black):
        quarters = []
        for b in range(2):
            quarters.extend(split_even(red[b], black[b]))
        return jnp.concatenate([jnp.swapaxes(q, 0, 1).reshape(64, LANES) for q in quarters], axis=1)

    field = [[ref[b, 4:12, 0:8] for b in range(2)] for ref in (rd, bd)]
    flat = permute(jnp.concatenate([lay(*field), lay(*left)], axis=0), perm[...], 1)
    v_out[...] = flat[0:64].reshape(v_out.shape)
    r_out[...] = flat[64:128].reshape(r_out.shape)
    all_sent()


def hand_out(v_ref, r_ref, v_out, r_out, sem):
    pairs = ((v_ref, v_out), (r_ref, r_out))
    for n, (src, dst) in enumerate(pairs):
        for i in range(0, src.shape[0], 2):
            pltpu.make_async_copy(src.at[i : i + 2], dst.at[i : i + 2], sem.at[n]).start()
    for n, (src, dst) in enumerate(pairs):
        pltpu.make_async_copy(src, dst, sem.at[n]).wait()


def solution(mesh):
    nx, ny = mesh.shape["gx"], mesh.shape["gy"]

    def shards(right_side, inverse_density):
        x, y, z = right_side.shape
        assert (x, y, z) == (8, 8, 4 * LANES)

        def vmem(*shape):
            return pltpu.VMEM((*shape, LANES), F32)

        fine = (2, FINE, FINE)
        mid = (1, *MID)
        result = pltpu.VMEM(right_side.shape, F32)
        v, r = pl.pallas_call(
            functools.partial(kernel, nx, ny),
            out_shape=(result, result),
            in_specs=[pl.BlockSpec(memory_space=pl.ANY)] * 2,
            out_specs=(pl.BlockSpec(memory_space=pltpu.VMEM),) * 2,
            scratch_shapes=[
                pltpu.VMEM((z, z), jnp.bfloat16),
                pltpu.VMEM((2, x, y, z), F32),
                vmem(2, *fine), vmem(2, *fine), vmem(2, 2, 8, FINE, FINE),
                *[vmem(*fine)] * 9,
                vmem(2, 2, 2, 8, 4), vmem(3, 2, 2, 8, 4), vmem(2, 2, 2, 8, 2), vmem(3, 2, 2, 8, 2), vmem(4, 1, 2), vmem(5, 1, 2), vmem(4, 6, 2), vmem(5, 6, 2),
                vmem(2, 2, 2, 8, 4), vmem(2, 3, 2, 8, 4), vmem(2, 4, 2, 2, 2), vmem(2, 5, 2, 2, 2),
                vmem(2, 2, 8, 2), vmem(3, 2, 8, 2), vmem(4, 2, 1, 1), vmem(5, 2, 1, 1),
                vmem(2, *mid), vmem(2, *mid), vmem(2, 1, 8, *MID), *[vmem(*mid)] * 3,
                vmem(2, 16, 4), vmem(2, 4, 4), vmem(4, 4),
                vmem(5, 2, 16, 4), vmem(len(WAYS) + 1, 2, 4, 4), vmem(len(WAYS) + 1, 4, 4),
                vmem(2, nx * ny, 2, 2), vmem(2, ny, 2 * nx), vmem(2, 8, ny, 2 * nx), vmem(nx + 4, ny + 4, 2, 2),
                vmem(2, 3, 8), vmem(2048),
                pltpu.SemaphoreType.DMA,
                pltpu.SemaphoreType.DMA((2,)),
                pltpu.SemaphoreType.DMA((len(WAYS),)),
                pltpu.SemaphoreType.DMA((3,)),
                pltpu.SemaphoreType.DMA((PHASES,)),
            ],
            compiler_params=pltpu.CompilerParams(
                collective_id=0, has_side_effects=True, vmem_limit_bytes=40 * 1024 * 1024
            ),
        )(*(pltpu.with_memory_space_constraint(a, pltpu.HBM) for a in (right_side, inverse_density)))
        out = jax.ShapeDtypeStruct(right_side.shape, F32)
        return pl.pallas_call(
            hand_out,
            out_shape=(out, out),
            in_specs=[pl.BlockSpec(memory_space=pltpu.VMEM)] * 2,
            out_specs=(pl.BlockSpec(memory_space=pl.ANY),) * 2,
            scratch_shapes=[pltpu.SemaphoreType.DMA((2,))],
            compiler_params=pltpu.CompilerParams(vmem_limit_bytes=1024 * 1024),
        )(v, r)

    spec = P("gx", "gy", None)
    return jax.shard_map(shards, mesh=mesh, in_specs=(spec, spec), out_specs=(spec, spec), check_vma=False)
```

```python
import functools
import math

import jax
import jax.numpy as jnp
from jax import lax
from jax.experimental import pallas as pl
from jax.experimental.pallas import tpu as pltpu
from jax.sharding import PartitionSpec as P

SWEEPS = 2
COARSE_SWEEPS = 8
MESH = pl.DeviceIdType.MESH
LANES = 128
F32 = jnp.float32

FINE, MID = 16, (20, 16)

WAYS = ((-1, 0), (1, 0), (0, -1), (0, 1), (-1, -1), (-1, 1), (1, -1), (1, 1),
        (-2, 0), (2, 0), (0, -2), (0, 2),
        (-2, -1), (-2, 1), (2, -1), (2, 1), (-1, -2), (-1, 2), (1, -2), (1, 2))
BACK = tuple(WAYS.index((-dy, -dx)) for dy, dx in WAYS)
FIRST, MORE, SWAP, KEEP, LAST, MID_C, STRIP, MID_G, FAR_G, MID_X = range(10)
GATHER, LINE, PLANE = 10, 11, 12
PHASES = 13
YS, XS, CORNERS, NEAR = (0, 1), (2, 3), (4, 5, 6, 7), range(8)


def iota(shape, dim):
    return lax.broadcasted_iota(jnp.int32, shape, dim)


def lane_prev(a):
    return jnp.where(iota(a.shape, 2) == 0, 0.0, pltpu.roll(a, 1, 2))


def lane_next(a):
    return jnp.where(iota(a.shape, 2) == LANES - 1, 0.0, pltpu.roll(a, LANES - 1, 2))


def even_cells(shape):
    return (iota(shape, 0) + iota(shape, 1)) % 2 == 0


def z_other(o, colour, first):
    shape = o[0].shape
    even = (iota(shape, 0) + iota(shape, 1)) % 2 == first % 2
    low = even if colour == 0 else jnp.logical_not(even)
    last = len(o) - 1
    out = []
    for b in range(last + 1):
        before = o[b - 1] if b > 0 else lane_prev(o[last])
        after = o[b + 1] if b < last else lane_next(o[0])
        out.append(jnp.where(low, before, after))
    return out


def around(other, colour, y0, y1, rows):
    groups = range(other.shape[0])
    mid = [other[b, y0:y1, 0:rows] for b in groups]
    zo = z_other(mid, colour, y0)
    return [
        (
            other[b, y0 - 1 : y1 - 1, 0:rows],
            other[b, y0 + 1 : y1 + 1, 0:rows],
            pltpu.roll(mid[b], 1, 1),
            pltpu.roll(mid[b], rows - 1, 1),
            mid[b],
            zo[b],
        )
        for b in groups
    ]


def split_even(zero, one):
    even = even_cells(zero.shape)
    return jnp.where(even, zero, one), jnp.where(even, one, zero)


def pair_rows(a):
    rows = a.shape[1] // 2
    a = a.reshape(a.shape[0] // 2, 2, a.shape[1], LANES)
    a = a[:, 0] + a[:, 1]
    pick = iota((a.shape[0], rows, LANES), 1)
    out = a[:, 0:1] + a[:, 1:2]
    out = jnp.broadcast_to(out, pick.shape)
    for j in range(1, rows):
        out = jnp.where(pick == j, a[:, 2 * j : 2 * j + 1] + a[:, 2 * j + 1 : 2 * j + 2], out)
    return out * 0.125


def double_rows(a, order):
    y = a.shape[0]
    pick = iota((y, 2 * len(order), LANES), 1) // 2
    out = jnp.broadcast_to(a[:, order[0] : order[0] + 1], pick.shape)
    for n, j in enumerate(order[1:], 1):
        out = jnp.where(pick == n, a[:, j : j + 1], out)
    return jnp.concatenate([out[i // 2 : i // 2 + 1] for i in range(2 * y)], axis=0)


def three(x):
    high = x.astype(jnp.bfloat16)
    rest = x - high.astype(F32)
    middle = rest.astype(jnp.bfloat16)
    low = (rest - middle.astype(F32)).astype(jnp.bfloat16)
    return jnp.concatenate([high, middle, low], axis=0)


def permute(x, matrix, side):
    n = x.shape[0]
    out = lax.dot_general(three(x), matrix, (((1,), (side,)), ((), ())), preferred_element_type=F32)
    return (out[0:n] + out[n : 2 * n]) + out[2 * n :]


def y_own(d, w):
    return slice(4, 12) if d == 0 else (slice(12 - w, 12) if d > 0 else slice(4, 4 + w))


def y_halo(d, w):
    return slice(4, 12) if d == 0 else (slice(12, 12 + w) if d > 0 else slice(4 - w, 4))


def x_own(d, w):
    return slice(0, 8) if d == 0 else (slice(8 - w, 8) if d > 0 else slice(0, w))


def x_halo(d, w):
    return slice(0, 8) if d == 0 else (slice(8, 8 + w) if d > 0 else slice(FINE - w, FINE))


def columns_of(dx):
    start = 6 + 4 * dx
    low, high = max(start, 0), min(start + 4, MID[1])
    return slice(low, high), slice(low - start, high - start)


def outer(part, d):
    return slice(part.stop - 1, part.stop) if d > 0 else slice(part.start, part.start + 1)


def block_part(way, far):
    dy, dx = WAYS[way]
    n = far if abs(dy) == 2 else (2 if abs(dx) == 2 and dy else 4)
    return slice(0, n) if dy > 0 else slice(4 - n, 4)


def kernel(nx, ny, g_ref, c_ref, v_out, r_out, perm, held, d0, g0, k0, ra, ba, rb, bb, bp, rc, bc, rd, bd,
           ax_s, ax_r, gx_s, gx_r, an_s, an_r, ac_s, ac_r, sx_s, sx_r, sc_s, sc_r, ex_s, ex_r, ec_s, ec_r,
           d1, g1, k1, mr, mb, mp, strip, blk_g, blk_x, in_c, in_g, in_x,
           gat, cc, kc, vc, zero_y, bulk, held_sem, lead_sem, out_sem, in_sem):
    gx, gy = lax.axis_index("gx"), lax.axis_index("gy")

    def inside(way):
        dy, dx = WAYS[way]
        tests = []
        if dy:
            tests.append(gy + dy >= 0 if dy < 0 else gy + dy < ny)
        if dx:
            tests.append(gx + dx >= 0 if dx < 0 else gx + dx < nx)
        return tests[0] if len(tests) == 1 else jnp.logical_and(*tests)

    def device(way):
        dy, dx = WAYS[way]
        out = {}
        if dx:
            out["gx"] = gx + dx
        if dy:
            out["gy"] = gy + dy
        return out

    has = [inside(way) for way in range(len(WAYS))]
    target = [device(way) for way in range(len(WAYS))]

    def each_peer(fn):
        if nx * ny <= 64:
            for s in range(1, nx * ny):
                fn(s, s // ny, s % ny)
        else:
            def body(s, carry):
                fn(s, s // ny, lax.rem(s, ny))
                return carry
            lax.fori_loop(1, nx * ny, body, 0)

    loads = [
        pltpu.make_async_copy(ref.at[i : i + 2], held.at[n, i : i + 2], held_sem)
        for n, ref in enumerate((c_ref, g_ref)) for i in range(0, 8, 2)
    ]
    for load in loads:
        load.start()

    barrier = pltpu.get_barrier_semaphore()

    def greet(s, sx, sy):
        pl.semaphore_signal(
            barrier, inc=1, device_id={"gx": lax.rem(gx + sx, nx), "gy": lax.rem(gy + sy, ny)}, device_id_type=MESH)

    each_peer(greet)

    for ref in (ax_r, gx_r, ex_r):
        ref[2] = jnp.zeros(ref.shape[1:], F32)
    for ref in (an_r, ac_r, ec_r):
        ref[4] = jnp.zeros(ref.shape[1:], F32)
    for n in range(2):
        sx_r[n, 2] = jnp.zeros(sx_r.shape[2:], F32)
        sc_r[n, 4] = jnp.zeros(sc_r.shape[2:], F32)
    in_c[4] = jnp.zeros(in_c.shape[1:], F32)
    for ref in (in_g, in_x):
        ref[len(WAYS)] = jnp.zeros(ref.shape[1:], F32)
    zero_y[...] = jnp.zeros(zero_y.shape, F32)
    vc[...] = jnp.zeros(vc.shape, F32)

    size_z = 4 * LANES
    row, col = iota((size_z, size_z), 0), iota((size_z, size_z), 1)
    perm[...] = (row == 4 * (col % LANES) + col // LANES).astype(F32).astype(jnp.bfloat16)

    def coarsen(red, black):
        pair = [pair_rows(red[b] + black[b]) for b in range(len(red))]
        if len(pair) == 1:
            return pair[0]
        first, second = split_even(pair[0], pair[1])
        return [first], [second]

    def remote(phase, way, src, dst):
        lead = phase == FIRST and way in YS
        return pltpu.make_async_remote_copy(
            src_ref=src, dst_ref=dst, send_sem=lead_sem.at[way] if lead else out_sem, recv_sem=in_sem.at[phase],
            device_id=target[way], device_id_type=MESH)

    def size(ref):
        return math.prod(ref.shape[:-1])

    def take(sem, rows):
        pltpu.make_async_copy(bulk.at[0:rows], bulk.at[0:rows], sem).wait()

    def ring_messages(src, dst, w, x_s, x_r, c_s, c_r):
        out = []
        for way in YS:
            dy = WAYS[way][0]
            out.append((way, src.at[:, y_own(dy, w), 0:8], dst.at[:, y_halo(-dy, w), 0:8], dst.at[:, y_halo(dy, w), 0:8], zero_y.at[:, 0:w]))
        for way in XS:
            out.append((way, x_s.at[way - 2], x_r.at[BACK[way] - 2], x_r.at[way - 2], x_r.at[2]))
        for way in CORNERS:
            out.append((way, c_s.at[way - 4], c_r.at[BACK[way] - 4], c_r.at[way - 4], c_r.at[4]))
        return out

    def ring_pack(src, cw, x_s, c_s):
        for way in XS:
            x_s[way - 2] = src[:, 4:12, x_own(WAYS[way][1], x_s.shape[-2])]
        for way in CORNERS:
            dy, dx = WAYS[way]
            c_s[way - 4] = src[:, y_own(dy, cw), x_own(dx, cw)]

    def ring_unpack(dst, cw, x_r, c_r):
        for way in XS:
            dst[:, 4:12, x_halo(WAYS[way][1], x_r.shape[-2])] = x_r[way - 2]
        for way in CORNERS:
            dy, dx = WAYS[way]
            dst[:, y_halo(dy, cw), x_halo(dx, cw)] = c_r[way - 4]

    def rows_y(ref, colour, w, only, way):
        dy = WAYS[way][0]
        own, there, here = y_own(dy, w), y_halo(-dy, w), y_halo(dy, w)
        if only:
            own, there, here = (outer(a, d) for a, d in ((own, -dy), (there, -dy), (here, dy)))
        n = 1 if only else w
        return (way, ref.at[colour, :, own, 0:8], ref.at[colour, :, there, 0:8], ref.at[colour, :, here, 0:8],
                zero_y.at[:, 0:n])

    def messages_first():
        out = []
        for way in YS:
            for ref, colour, w in ((d0, 0, 1), (d0, 1, 2), (g0, 0, 1)):
                out.append(rows_y(ref, colour, w, False, way))
        for way in CORNERS:
            out.append((way, an_s.at[way - 4], an_r.at[BACK[way] - 4], an_r.at[way - 4], an_r.at[4]))
        for way in XS:
            out.append((way, ax_s.at[way - 2], ax_r.at[BACK[way] - 2], ax_r.at[way - 2], ax_r.at[2]))
            out.append((way, gx_s.at[way - 2], gx_r.at[BACK[way] - 2], gx_r.at[way - 2], gx_r.at[2]))
        return out

    def messages_more():
        out = []
        for way in YS:
            for ref, colour, w in ((d0, 0, 2), (d0, 1, 3), (g0, 0, 2), (g0, 1, 1)):
                out.append(rows_y(ref, colour, w, True, way))
        for way in CORNERS:
            out.append((way, ac_s.at[way - 4], ac_r.at[BACK[way] - 4], ac_r.at[way - 4], ac_r.at[4]))
        return out

    def block_messages(src, dst, ways, far):
        out = []
        for way in ways:
            give, got = block_part(BACK[way], far), block_part(way, far)
            lead = (slice(None),) * (len(src.shape) - 3)
            out.append((way, src.at[(*lead, give)], dst.at[(BACK[way], *lead, give)], dst.at[(way, *lead, got)],
                        dst.at[(len(WAYS), *lead, got)]))
        return out

    def near_part(way, c):
        n = 4 if way in XS else ((4, 3)[c] if way in YS else (3, 2)[c])
        dy = WAYS[way][0]
        return slice(0, n) if dy > 0 else slice(4 - n, 4)

    def near_more(way, c):
        n = {YS: (0, 4), XS: (0, 0), CORNERS: (4, 3)}[YS if way in YS else (XS if way in XS else CORNERS)][c]
        dy = WAYS[way][0]
        return (slice(n - 1, n) if dy > 0 else slice(4 - n, 5 - n)) if n else None

    def source_message(way, c, part):
        give, got = part(BACK[way], c), part(way, c)
        return (way, blk_g.at[c, give], in_g.at[BACK[way], c, give], in_g.at[way, c, got], in_g.at[len(WAYS), c, got])

    def sources(part):
        for way in NEAR:
            y, (to, of) = 4 * (WAYS[way][0] + 2), columns_of(WAYS[way][1])
            for c in range(2):
                rows = part(way, c)
                if rows:
                    g1[c, 0, y + rows.start : y + rows.stop, to] = in_g[way, c, rows, of]

    def column_messages():
        out = []
        for way in (0, 1, 8, 9):
            dy = WAYS[way][0]
            give, there, here = {
                -1: (slice(6, 10), slice(10, 14), slice(2, 6)), 1: (slice(6, 10), slice(2, 6), slice(10, 14)),
                -2: (slice(6, 8), slice(14, 16), slice(0, 2)), 2: (slice(8, 10), slice(0, 2), slice(14, 16))}[dy]
            out.append((way, strip.at[:, give], strip.at[:, there], strip.at[:, here], in_c.at[4, :, give]))
        return out

    def strip_messages():
        out = []
        for n, way in enumerate((2, 3, 10, 11)):
            part = slice(0, 16) if n < 2 else slice(4, 12)
            out.append((way, strip.at[:, part], in_c.at[n ^ 1, :, part], in_c.at[n, :, part], in_c.at[4, :, part]))
        return out

    def columns():
        for c in range(2):
            d1[c, 0, 2:18, 6:10] = strip[c]
            for n, way in enumerate((2, 3, 10, 11)):
                part = slice(0, 16) if n < 2 else slice(4, 12)
                to, of = columns_of(WAYS[way][1])
                d1[c, 0, 2 + part.start : 2 + part.stop, to] = in_c[n, c, part, of]

    def by_way(messages):
        ways = {}
        for m in messages:
            ways.setdefault(m[0], []).append(m)
        return ways.items()

    sent = {}

    def start(phase, messages):
        for way, group in by_way(messages):
            @pl.when(has[way])
            def _():
                for _, src, there, here, zeros in group:
                    remote(phase, way, src, there).start()

            @pl.when(jnp.logical_not(has[way]))
            def _():
                for _, src, there, here, zeros in group:
                    pltpu.make_async_copy(zeros, here, in_sem.at[phase]).start()

            if phase != FIRST or way not in YS:
                sent[way] = sent.get(way, 0) + sum(size(m[1]) for m in group)

    def finish(phase, messages):
        take(in_sem.at[phase], sum(size(m[3]) for m in messages))

    def first_sent():
        for way in YS:
            @pl.when(has[way])
            def _():
                take(lead_sem.at[way], sum(size(m[1]) for m in first_part if m[0] == way))

    def all_sent():
        always = ((nx * ny - 1) + (ny - 1) + (nx - 1) * ny) * slot
        rows = {}
        for py in range(ny):
            for px in range(nx):
                there = tuple(
                    way for way, (dy, dx) in enumerate(WAYS) if 0 <= py + dy < ny and 0 <= px + dx < nx)
                rows.setdefault((min(py, 2), min(ny - 1 - py, 2), min(px, 2), min(nx - 1 - px, 2)), there)
        low_y, high_y = jnp.minimum(gy, 2), jnp.minimum(ny - 1 - gy, 2)
        low_x, high_x = jnp.minimum(gx, 2), jnp.minimum(nx - 1 - gx, 2)
        place = ((low_y * 3 + high_y) * 3 + low_x) * 3 + high_x
        for (a, b, c, d), there in rows.items():
            @pl.when(place == ((a * 3 + b) * 3 + c) * 3 + d)
            def _():
                take(out_sem, always + sum(sent[way] for way in there))

    me = gx * ny + gy
    def spread():
        def body(s, sx, sy):
            pltpu.make_async_remote_copy(
                src_ref=gat.at[1, me], dst_ref=gat.at[1, me], send_sem=out_sem, recv_sem=in_sem.at[GATHER],
                device_id={"gx": lax.rem(gx + sx, nx), "gy": lax.rem(gy + sy, ny)}, device_id_type=MESH).start()
        each_peer(body)

    slot = size(gat.at[0, 0])

    def along_y():
        for sy in range(1, ny):
            pltpu.make_async_remote_copy(
                src_ref=gat.at[0, me], dst_ref=gat.at[0, me], send_sem=out_sem, recv_sem=in_sem.at[LINE],
                device_id={"gy": lax.rem(gy + sy, ny)}, device_id_type=MESH).start()

    def along_x():
        take(in_sem.at[LINE], (ny - 1) * slot)
        line = gat.at[0, pl.ds(gx * ny, ny)]
        for sx in range(1, nx):
            pltpu.make_async_remote_copy(
                src_ref=line, dst_ref=line, send_sem=out_sem, recv_sem=in_sem.at[PLANE],
                device_id={"gx": lax.rem(gx + sx, nx)}, device_id_type=MESH).start()

    def setup(kref, dens, colour, scale, y0, y1, rows):
        for b, near in enumerate(around(dens.at[1 - colour], colour, y0, y1, rows)):
            here = dens[colour, b, y0:y1, 0:rows]
            total = None
            for f in range(6):
                face = (scale * 0.5) * (here + near[f])
                kref[colour, b, f, y0:y1, 0:rows] = face
                total = face if total is None else total + face
            kref[colour, b, 6, y0:y1, 0:rows] = total
            kref[colour, b, 7, y0:y1, 0:rows] = jnp.where(here > 0.0, 1.0 / total, 0.0)

    def weigh(kref, other, colour, y0, y1, rows):
        out = []
        for b, near in enumerate(around(other, colour, y0, y1, rows)):
            total = kref[colour, b, 0, y0:y1, 0:rows] * near[0]
            for f in range(1, 6):
                total = total + kref[colour, b, f, y0:y1, 0:rows] * near[f]
            out.append(total)
        return out

    def update(kref, g, other, dst, colour, y0, y1, rows):
        for b, n in enumerate(weigh(kref, other, colour, y0, y1, rows)):
            dst[b, y0:y1, 0:rows] = (g[colour, b, y0:y1, 0:rows] + n) * kref[colour, b, 7, y0:y1, 0:rows]

    def first(kref, g, dst, y0, y1, rows):
        for b in range(dst.shape[0]):
            dst[b, y0:y1, 0:rows] = g[0, b, y0:y1, 0:rows] * kref[0, b, 7, y0:y1, 0:rows]

    def residual(kref, g, red, black, y0, y1, rows, x0, x1):
        out = []
        for c, (v, other) in enumerate(((red, black), (black, red))):
            n = weigh(kref, other, c, y0, y1, rows)
            out.append([
                (g[c, b, y0:y1, 0:rows] - (kref[c, b, 6, y0:y1, 0:rows] * v[b, y0:y1, 0:rows] - n[b]))[:, x0:x1]
                for b in range(len(n))])
        return out

    pltpu.make_async_copy(held, held, held_sem).wait()
    flat = permute(held[...].reshape(-1, size_z), perm[...], 0)

    def fields(flat):
        quarters = [
            jnp.swapaxes(flat[:, q * LANES : (q + 1) * LANES].reshape(8, 8, LANES), 0, 1) for q in range(4)]
        pairs = [split_even(quarters[2 * b], quarters[2 * b + 1]) for b in range(2)]
        return [pairs[b][0] for b in range(2)], [pairs[b][1] for b in range(2)]

    dens, source = fields(flat[0:64]), fields(flat[64:128])
    for c in range(2):
        for b in range(2):
            d0[c, b, 4:12, 0:8] = dens[c][b]
            g0[c, b, 4:12, 0:8] = source[c][b]
    for way in XS:
        dx = WAYS[way][1]
        for c in range(2):
            ax_s[way - 2, c] = d0[c, :, 4:12, x_own(dx, 4)]
            gx_s[way - 2, c] = g0[c, :, 4:12, x_own(dx, 2)]
    for way in CORNERS:
        dy, dx = WAYS[way]
        for b in range(2):
            ac_s[way - 4, 2 * b : 2 * b + 2] = d0[1, b, y_own(dy, 2), x_own(dx, 2)]
            an_s[way - 4, :, b : b + 1] = d0[1, b, y_own(dy, 1), x_own(dx, 1)]
            ac_s[way - 4, 4:5, b : b + 1] = d0[0, b, y_own(dy, 1), x_own(dx, 1)]
            ac_s[way - 4, 5:6, b : b + 1] = g0[0, b, y_own(dy, 1), x_own(dx, 1)]
    dens_one = coarsen(*dens)
    for c in range(2):
        strip[c, 6:10] = dens_one[c][0]
    gat[0, me] = coarsen(*dens_one)

    pl.semaphore_wait(barrier, nx * ny - 1)
    first_part, more_part = messages_first(), messages_more()
    start(FIRST, first_part)
    first_sent()
    start(MORE, more_part)
    part_c, part_s = column_messages(), strip_messages()
    start(MID_C, part_c)
    along_y()
    finish(FIRST, first_part)
    for way in XS:
        dx = WAYS[way][1]
        for c in range(2):
            d0[c, :, 4:12, x_halo(dx, 4)] = ax_r[way - 2, c]
            g0[c, :, 4:12, x_halo(dx, 2)] = gx_r[way - 2, c]
    for way in CORNERS:
        dy, dx = WAYS[way]
        for b in range(2):
            d0[1, b, y_halo(dy, 1), x_halo(dx, 1)] = an_r[way - 4, :, b : b + 1]

    setup(k0, d0, 0, 1.0, 3, 13, FINE)
    setup(k0, d0, 1, 1.0, 4, 12, FINE)
    first(k0, g0, ra, 3, 13, FINE)
    update(k0, g0, ra, ba, 1, 4, 12, FINE)
    ring_pack(ba, 2, sx_s.at[0], sc_s.at[0])
    swap = ring_messages(ba, ba, 3, sx_s.at[0], sx_r.at[0], sc_s.at[0], sc_r.at[0])
    start(SWAP, swap)
    finish(MID_C, part_c)
    start(STRIP, part_s)
    finish(MORE, more_part)
    for way in CORNERS:
        dy, dx = WAYS[way]
        for b in range(2):
            d0[1, b, y_halo(dy, 2), x_halo(dx, 2)] = ac_r[way - 4, 2 * b : 2 * b + 2]
            d0[0, b, y_halo(dy, 1), x_halo(dx, 1)] = ac_r[way - 4, 4:5, b : b + 1]
            g0[0, b, y_halo(dy, 1), x_halo(dx, 1)] = ac_r[way - 4, 5:6, b : b + 1]
    setup(k0, d0, 0, 1.0, 2, 14, FINE)
    setup(k0, d0, 1, 1.0, 3, 13, FINE)
    along_x()
    finish(SWAP, swap)
    ring_unpack(ba, 2, sx_r.at[0], sc_r.at[0])
    update(k0, g0, ba, rb, 0, 2, 14, FINE)
    update(k0, g0, rb, bb, 1, 3, 13, FINE)
    source_one = coarsen(*residual(k0, g0, rb, bb, 4, 12, FINE, 0, 8))
    for c in range(2):
        blk_g[c] = source_one[c][0]
        g1[c, 0, 8:12, 6:10] = source_one[c][0]
    part_g, far_g = [], block_messages(blk_g, in_g, range(8, 12), 1)
    for way in NEAR:
        for c in range(2):
            part_g.append(source_message(way, c, near_part))
            if near_more(way, c):
                far_g.append(source_message(way, c, near_more))
    start(MID_G, part_g)

    def blocks(ref, got, ways, far):
        for way in ways:
            dy, dx = WAYS[way]
            part = block_part(way, far)
            y, (to, of) = 4 * (dy + 2), columns_of(dx)
            for c in range(2):
                ref[c, 0, y + part.start : y + part.stop, to] = got[way, c, part, of]

    finish(STRIP, part_s)
    columns()
    for c in range(2):
        setup(k1, d1, c, 0.25, 3 + c, 17 - c, MID[1])

    take(in_sem.at[PLANE], (nx - 1) * ny * slot)
    pairs, rows = ny, 2 * nx

    def assemble(n):
        for i in range(nx):
            for p in range(2):
                cc[p, :, 2 * i : 2 * i + 2] = gat[n, i * ny : (i + 1) * ny, p]
        even = (iota((pairs, rows, LANES), 1) + iota((pairs, rows, LANES), 2)) % 2 == 0
        return jnp.where(even, cc[0], cc[1]), jnp.where(even, cc[1], cc[0])

    shape = (pairs, rows, LANES)
    tested = (iota(shape, 1) + iota(shape, 2)) % 2

    def beside(other, colour):
        low = tested == colour
        return (
            jnp.where(low, jnp.concatenate([other[-1:], other[:-1]], axis=0), other),
            jnp.where(low, other, jnp.concatenate([other[1:], other[:1]], axis=0)),
            pltpu.roll(other, 1, 1), pltpu.roll(other, rows - 1, 1),
            pltpu.roll(other, 1, 2), pltpu.roll(other, LANES - 1, 2))

    centre = assemble(0)
    for c in range(2):
        low = tested == c
        edges = (
            jnp.logical_and(low, iota(shape, 0) == 0),
            jnp.logical_and(jnp.logical_not(low), iota(shape, 0) == pairs - 1),
            iota(shape, 1) == 0, iota(shape, 1) == rows - 1, iota(shape, 2) == 0, iota(shape, 2) == LANES - 1)
        total, faces = None, []
        for near, edge in zip(beside(centre[1 - c], c), edges):
            face = 0.03125 * (centre[c] + jnp.where(edge, 0.0, near))
            total = face if total is None else total + face
            faces.append(face)
        inverse = 1.0 / total
        for f in range(6):
            kc[c, f] = jnp.where(edges[f], 0.0, faces[f] * inverse)
        kc[c, 6] = inverse

    finish(MID_G, part_g)
    sources(near_part)
    first(k1, g1, mr, 4, 16, 16)
    update(k1, g1, mr, mb, 1, 5, 15, 16)
    update(k1, g1, mb, mr, 0, 6, 14, 16)
    update(k1, g1, mr, mb, 1, 7, 13, 16)
    gat[1, me] = coarsen(*residual(k1, g1, mr, mb, 8, 12, 16, 6, 10))
    spread()
    start(FAR_G, far_g)
    ring_pack(bb, 2, sx_s.at[1], sc_s.at[1])
    keep = ring_messages(bb, bp, 3, sx_s.at[1], sx_r.at[1], sc_s.at[1], sc_r.at[1])
    start(KEEP, keep)
    blk_x[...] = mb[0, 8:12, 6:10]
    part_x = block_messages(blk_x, in_x, range(20), 2)
    start(MID_X, part_x)

    take(in_sem.at[GATHER], (nx * ny - 1) * slot)
    right = assemble(1)
    for c in range(2):
        kc[c, 7] = right[c] * kc[c, 6]

    def half(other, colour):
        total = kc[colour, 7]
        for f, near in enumerate(beside(other, colour)):
            total = total + kc[colour, f] * near
        return total

    def sweep(i, carry):
        red = half(carry[1], 0)
        return red, half(red, 1)

    red = kc[0, 7]
    red, black = lax.fori_loop(1, COARSE_SWEEPS, sweep, (red, half(red, 1)), unroll=True)
    even = tested == 0
    for i in range(nx):
        cut = slice(2 * i, 2 * i + 2)
        vc[2 + i, 2 : 2 + ny, 0] = jnp.where(even, red, black)[:, cut]
        vc[2 + i, 2 : 2 + ny, 1] = jnp.where(even, black, red)[:, cut]

    finish(MID_X, part_x)
    finish(FAR_G, far_g)
    blocks(g1, in_g, range(8, 12), 1)
    sources(near_more)
    mp[0, 8:12, 6:10] = blk_x[...]
    for way in range(20):
        dy, dx = WAYS[way]
        part = block_part(way, 2)
        y, (to, of) = 4 * (dy + 2), columns_of(dx)
        mp[0, y + part.start : y + part.stop, to] = in_x[way, part, of]
    for dx in range(5):
        window = vc[gx + dx, pl.ds(gy, 5)].reshape(10, 2, LANES)
        to, of = columns_of(dx - 2)
        mp[0, :, to] = mp[0, :, to] + double_rows(window, (0, 1))[:, of]
    update(k1, g1, mp, mr, 0, 3, 17, MID[1])
    update(k1, g1, mr, mb, 1, 4, 16, MID[1])
    update(k1, g1, mb, mr, 0, 5, 15, MID[1])
    update(k1, g1, mr, mb, 1, 6, 14, MID[1])

    finish(KEEP, keep)
    bp[:, 4:12, 0:8] = bb[:, 4:12, 0:8]
    ring_unpack(bp, 2, sx_r.at[1], sc_r.at[1])
    half_z = split_even(mr[0, 6:14], mb[0, 6:14])
    for b in range(2):
        bp[b] = bp[b] + double_rows(half_z[b], (6, 7, 8, 9, 10, 11, 4, 5))
    update(k0, g0, bp, rc, 0, 2, 14, FINE)
    update(k0, g0, rc, bc, 1, 3, 13, FINE)
    update(k0, g0, bc, rd, 0, 4, 12, FINE)
    ring_pack(rd, 1, ex_s, ec_s)
    last = ring_messages(rd, rd, 2, ex_s, ex_r, ec_s, ec_r)
    start(LAST, last)
    finish(LAST, last)
    ring_unpack(rd, 1, ex_r, ec_r)
    update(k0, g0, rd, bd, 1, 3, 13, FINE)
    left = residual(k0, g0, rd, bd, 4, 12, FINE, 0, 8)

    def lay(red, black):
        quarters = []
        for b in range(2):
            quarters.extend(split_even(red[b], black[b]))
        return jnp.concatenate([jnp.swapaxes(q, 0, 1).reshape(64, LANES) for q in quarters], axis=1)

    field = [[ref[b, 4:12, 0:8] for b in range(2)] for ref in (rd, bd)]
    flat = permute(jnp.concatenate([lay(*field), lay(*left)], axis=0), perm[...], 1)
    v_out[...] = flat[0:64].reshape(v_out.shape)
    r_out[...] = flat[64:128].reshape(r_out.shape)
    all_sent()


def hand_out(v_ref, r_ref, v_out, r_out, sem):
    pairs = ((v_ref, v_out), (r_ref, r_out))
    for n, (src, dst) in enumerate(pairs):
        for i in range(0, src.shape[0], 2):
            pltpu.make_async_copy(src.at[i : i + 2], dst.at[i : i + 2], sem.at[n]).start()
    for n, (src, dst) in enumerate(pairs):
        pltpu.make_async_copy(src, dst, sem.at[n]).wait()


def solution(mesh):
    nx, ny = mesh.shape["gx"], mesh.shape["gy"]

    def shards(right_side, inverse_density):
        x, y, z = right_side.shape
        assert (x, y, z) == (8, 8, 4 * LANES)

        def vmem(*shape):
            return pltpu.VMEM((*shape, LANES), F32)

        fine = (2, FINE, FINE)
        mid = (1, *MID)
        result = pltpu.VMEM(right_side.shape, F32)
        v, r = pl.pallas_call(
            functools.partial(kernel, nx, ny),
            out_shape=(result, result),
            in_specs=[pl.BlockSpec(memory_space=pl.ANY)] * 2,
            out_specs=(pl.BlockSpec(memory_space=pltpu.VMEM),) * 2,
            scratch_shapes=[
                pltpu.VMEM((z, z), jnp.bfloat16),
                pltpu.VMEM((2, x, y, z), F32),
                vmem(2, *fine), vmem(2, *fine), vmem(2, 2, 8, FINE, FINE),
                *[vmem(*fine)] * 9,
                vmem(2, 2, 2, 8, 4), vmem(3, 2, 2, 8, 4), vmem(2, 2, 2, 8, 2), vmem(3, 2, 2, 8, 2), vmem(4, 1, 2), vmem(5, 1, 2), vmem(4, 6, 2), vmem(5, 6, 2),
                vmem(2, 2, 2, 8, 4), vmem(2, 3, 2, 8, 4), vmem(2, 4, 2, 2, 2), vmem(2, 5, 2, 2, 2),
                vmem(2, 2, 8, 2), vmem(3, 2, 8, 2), vmem(4, 2, 1, 1), vmem(5, 2, 1, 1),
                vmem(2, *mid), vmem(2, *mid), vmem(2, 1, 8, *MID), *[vmem(*mid)] * 3,
                vmem(2, 16, 4), vmem(2, 4, 4), vmem(4, 4),
                vmem(5, 2, 16, 4), vmem(len(WAYS) + 1, 2, 4, 4), vmem(len(WAYS) + 1, 4, 4),
                vmem(2, nx * ny, 2, 2), vmem(2, ny, 2 * nx), vmem(2, 8, ny, 2 * nx), vmem(nx + 4, ny + 4, 2, 2),
                vmem(2, 3, 8), vmem(6144),
                pltpu.SemaphoreType.DMA,
                pltpu.SemaphoreType.DMA((2,)),
                pltpu.SemaphoreType.DMA,
                pltpu.SemaphoreType.DMA((PHASES,)),
            ],
            compiler_params=pltpu.CompilerParams(
                collective_id=0, has_side_effects=True, vmem_limit_bytes=40 * 1024 * 1024
            ),
        )(*(pltpu.with_memory_space_constraint(a, pltpu.HBM) for a in (right_side, inverse_density)))
        out = jax.ShapeDtypeStruct(right_side.shape, F32)
        return pl.pallas_call(
            hand_out,
            out_shape=(out, out),
            in_specs=[pl.BlockSpec(memory_space=pltpu.VMEM)] * 2,
            out_specs=(pl.BlockSpec(memory_space=pl.ANY),) * 2,
            scratch_shapes=[pltpu.SemaphoreType.DMA((2,))],
            compiler_params=pltpu.CompilerParams(vmem_limit_bytes=1024 * 1024),
        )(v, r)

    spec = P("gx", "gy", None)
    return jax.shard_map(shards, mesh=mesh, in_specs=(spec, spec), out_specs=(spec, spec), check_vma=False)
```

```python
import functools
import math

import jax
import jax.numpy as jnp
from jax import lax
from jax.experimental import pallas as pl
from jax.experimental.pallas import tpu as pltpu
from jax.sharding import PartitionSpec as P

SWEEPS = 2
COARSE_SWEEPS = 8
MESH = pl.DeviceIdType.MESH
LANES = 128
F32 = jnp.float32

FINE, MID = 16, (20, 16)

WAYS = ((-1, 0), (1, 0), (0, -1), (0, 1), (-1, -1), (-1, 1), (1, -1), (1, 1),
        (-2, 0), (2, 0), (0, -2), (0, 2),
        (-2, -1), (-2, 1), (2, -1), (2, 1), (-1, -2), (-1, 2), (1, -2), (1, 2))
BACK = tuple(WAYS.index((-dy, -dx)) for dy, dx in WAYS)
FIRST, MORE, SWAP, KEEP, LAST, MID_C, STRIP, MID_G, FAR_G, MID_X = range(10)
GATHER, LINE, PLANE = 10, 11, 12
PHASES = 13
YS, XS, CORNERS, NEAR = (0, 1), (2, 3), (4, 5, 6, 7), range(8)


def iota(shape, dim):
    return lax.broadcasted_iota(jnp.int32, shape, dim)


def lane_prev(a):
    return jnp.where(iota(a.shape, 2) == 0, 0.0, pltpu.roll(a, 1, 2))


def lane_next(a):
    return jnp.where(iota(a.shape, 2) == LANES - 1, 0.0, pltpu.roll(a, LANES - 1, 2))


def even_cells(shape):
    return (iota(shape, 0) + iota(shape, 1)) % 2 == 0


def z_other(o, colour, first):
    shape = o[0].shape
    even = (iota(shape, 0) + iota(shape, 1)) % 2 == first % 2
    low = even if colour == 0 else jnp.logical_not(even)
    last = len(o) - 1
    out = []
    for b in range(last + 1):
        before = o[b - 1] if b > 0 else lane_prev(o[last])
        after = o[b + 1] if b < last else lane_next(o[0])
        out.append(jnp.where(low, before, after))
    return out


def around(other, colour, y0, y1, rows):
    groups = range(other.shape[0])
    mid = [other[b, y0:y1, 0:rows] for b in groups]
    zo = z_other(mid, colour, y0)
    return [
        (
            other[b, y0 - 1 : y1 - 1, 0:rows],
            other[b, y0 + 1 : y1 + 1, 0:rows],
            pltpu.roll(mid[b], 1, 1),
            pltpu.roll(mid[b], rows - 1, 1),
            mid[b],
            zo[b],
        )
        for b in groups
    ]


def split_even(zero, one):
    even = even_cells(zero.shape)
    return jnp.where(even, zero, one), jnp.where(even, one, zero)


def pair_rows(a):
    rows = a.shape[1] // 2
    a = a.reshape(a.shape[0] // 2, 2, a.shape[1], LANES)
    a = a[:, 0] + a[:, 1]
    pick = iota((a.shape[0], rows, LANES), 1)
    out = a[:, 0:1] + a[:, 1:2]
    out = jnp.broadcast_to(out, pick.shape)
    for j in range(1, rows):
        out = jnp.where(pick == j, a[:, 2 * j : 2 * j + 1] + a[:, 2 * j + 1 : 2 * j + 2], out)
    return out * 0.125


def double_rows(a, order):
    y = a.shape[0]
    pick = iota((y, 2 * len(order), LANES), 1) // 2
    out = jnp.broadcast_to(a[:, order[0] : order[0] + 1], pick.shape)
    for n, j in enumerate(order[1:], 1):
        out = jnp.where(pick == n, a[:, j : j + 1], out)
    return jnp.concatenate([out[i // 2 : i // 2 + 1] for i in range(2 * y)], axis=0)


def three(x):
    high = x.astype(jnp.bfloat16)
    rest = x - high.astype(F32)
    middle = rest.astype(jnp.bfloat16)
    low = (rest - middle.astype(F32)).astype(jnp.bfloat16)
    return jnp.concatenate([high, middle, low], axis=0)


def permute(x, matrix, side):
    n = x.shape[0]
    out = lax.dot_general(three(x), matrix, (((1,), (side,)), ((), ())), preferred_element_type=F32)
    return (out[0:n] + out[n : 2 * n]) + out[2 * n :]


def y_own(d, w):
    return slice(4, 12) if d == 0 else (slice(12 - w, 12) if d > 0 else slice(4, 4 + w))


def y_halo(d, w):
    return slice(4, 12) if d == 0 else (slice(12, 12 + w) if d > 0 else slice(4 - w, 4))


def x_own(d, w):
    return slice(0, 8) if d == 0 else (slice(8 - w, 8) if d > 0 else slice(0, w))


def x_halo(d, w):
    return slice(0, 8) if d == 0 else (slice(8, 8 + w) if d > 0 else slice(FINE - w, FINE))


def columns_of(dx):
    start = 6 + 4 * dx
    low, high = max(start, 0), min(start + 4, MID[1])
    return slice(low, high), slice(low - start, high - start)


def outer(part, d):
    return slice(part.stop - 1, part.stop) if d > 0 else slice(part.start, part.start + 1)


def block_part(way, far):
    dy, dx = WAYS[way]
    n = far if abs(dy) == 2 else (2 if abs(dx) == 2 and dy else 4)
    return slice(0, n) if dy > 0 else slice(4 - n, 4)


def kernel(nx, ny, g_ref, c_ref, v_out, r_out, perm, held, d0, g0, k0, ra, ba, rb, bb, bp, rc, bc, rd, bd,
           ax_s, ax_r, gx_s, gx_r, an_s, an_r, ac_s, ac_r, sx_s, sx_r, sc_s, sc_r, ex_s, ex_r, ec_s, ec_r,
           d1, g1, k1, mr, mb, mp, strip, blk_g, blk_x, in_c, in_g, in_x,
           gat, cc, kc, vc, zero_y, bulk, held_sem, lead_sem, out_sem, in_sem):
    gx, gy = lax.axis_index("gx"), lax.axis_index("gy")

    def inside(way):
        dy, dx = WAYS[way]
        tests = []
        if dy:
            tests.append(gy + dy >= 0 if dy < 0 else gy + dy < ny)
        if dx:
            tests.append(gx + dx >= 0 if dx < 0 else gx + dx < nx)
        return tests[0] if len(tests) == 1 else jnp.logical_and(*tests)

    def device(way):
        dy, dx = WAYS[way]
        out = {}
        if dx:
            out["gx"] = gx + dx
        if dy:
            out["gy"] = gy + dy
        return out

    has = [inside(way) for way in range(len(WAYS))]
    target = [device(way) for way in range(len(WAYS))]

    def each_peer(fn):
        if nx * ny <= 64:
            for s in range(1, nx * ny):
                fn(s, s // ny, s % ny)
        else:
            def body(s, carry):
                fn(s, s // ny, lax.rem(s, ny))
                return carry
            lax.fori_loop(1, nx * ny, body, 0)

    loads = [
        pltpu.make_async_copy(ref.at[i : i + 2], held.at[n, i : i + 2], held_sem)
        for n, ref in enumerate((c_ref, g_ref)) for i in range(0, 8, 2)
    ]
    for load in loads:
        load.start()

    barrier = pltpu.get_barrier_semaphore()

    def greet(s, sx, sy):
        pl.semaphore_signal(
            barrier, inc=1, device_id={"gx": lax.rem(gx + sx, nx), "gy": lax.rem(gy + sy, ny)}, device_id_type=MESH)

    each_peer(greet)

    for ref in (ax_r, gx_r, ex_r):
        ref[2] = jnp.zeros(ref.shape[1:], F32)
    for ref in (an_r, ac_r, ec_r):
        ref[4] = jnp.zeros(ref.shape[1:], F32)
    for n in range(2):
        sx_r[n, 2] = jnp.zeros(sx_r.shape[2:], F32)
        sc_r[n, 4] = jnp.zeros(sc_r.shape[2:], F32)
    in_c[4] = jnp.zeros(in_c.shape[1:], F32)
    for ref in (in_g, in_x):
        ref[len(WAYS)] = jnp.zeros(ref.shape[1:], F32)
    zero_y[...] = jnp.zeros(zero_y.shape, F32)
    vc[...] = jnp.zeros(vc.shape, F32)

    size_z = 4 * LANES
    row, col = iota((size_z, size_z), 0), iota((size_z, size_z), 1)
    perm[...] = (row == 4 * (col % LANES) + col // LANES).astype(F32).astype(jnp.bfloat16)

    def coarsen(red, black):
        pair = [pair_rows(red[b] + black[b]) for b in range(len(red))]
        if len(pair) == 1:
            return pair[0]
        first, second = split_even(pair[0], pair[1])
        return [first], [second]

    def remote(phase, way, src, dst):
        lead = phase == FIRST and way in YS
        return pltpu.make_async_remote_copy(
            src_ref=src, dst_ref=dst, send_sem=lead_sem.at[way] if lead else out_sem, recv_sem=in_sem.at[phase],
            device_id=target[way], device_id_type=MESH)

    def size(ref):
        return math.prod(ref.shape[:-1])

    def take(sem, rows):
        pltpu.make_async_copy(bulk.at[0:rows], bulk.at[0:rows], sem).wait()

    def ring_messages(src, dst, w, x_s, x_r, c_s, c_r):
        out = []
        for way in YS:
            dy = WAYS[way][0]
            out.append((way, src.at[:, y_own(dy, w), 0:8], dst.at[:, y_halo(-dy, w), 0:8], dst.at[:, y_halo(dy, w), 0:8], zero_y.at[:, 0:w]))
        for way in XS:
            out.append((way, x_s.at[way - 2], x_r.at[BACK[way] - 2], x_r.at[way - 2], x_r.at[2]))
        for way in CORNERS:
            out.append((way, c_s.at[way - 4], c_r.at[BACK[way] - 4], c_r.at[way - 4], c_r.at[4]))
        return out

    def ring_pack(src, cw, x_s, c_s):
        for way in XS:
            x_s[way - 2] = src[:, 4:12, x_own(WAYS[way][1], x_s.shape[-2])]
        for way in CORNERS:
            dy, dx = WAYS[way]
            c_s[way - 4] = src[:, y_own(dy, cw), x_own(dx, cw)]

    def ring_unpack(dst, cw, x_r, c_r):
        for way in XS:
            dst[:, 4:12, x_halo(WAYS[way][1], x_r.shape[-2])] = x_r[way - 2]
        for way in CORNERS:
            dy, dx = WAYS[way]
            dst[:, y_halo(dy, cw), x_halo(dx, cw)] = c_r[way - 4]

    def rows_y(ref, colour, w, only, way):
        dy = WAYS[way][0]
        own, there, here = y_own(dy, w), y_halo(-dy, w), y_halo(dy, w)
        if only:
            own, there, here = (outer(a, d) for a, d in ((own, -dy), (there, -dy), (here, dy)))
        n = 1 if only else w
        return (way, ref.at[colour, :, own, 0:8], ref.at[colour, :, there, 0:8], ref.at[colour, :, here, 0:8],
                zero_y.at[:, 0:n])

    def messages_first():
        out = []
        for way in YS:
            for ref, colour, w in ((d0, 0, 1), (d0, 1, 2), (g0, 0, 1)):
                out.append(rows_y(ref, colour, w, False, way))
        for way in CORNERS:
            out.append((way, an_s.at[way - 4], an_r.at[BACK[way] - 4], an_r.at[way - 4], an_r.at[4]))
        for way in XS:
            out.append((way, ax_s.at[way - 2], ax_r.at[BACK[way] - 2], ax_r.at[way - 2], ax_r.at[2]))
            out.append((way, gx_s.at[way - 2], gx_r.at[BACK[way] - 2], gx_r.at[way - 2], gx_r.at[2]))
        return out

    def messages_more():
        out = []
        for way in YS:
            for ref, colour, w in ((d0, 0, 2), (d0, 1, 3), (g0, 0, 2), (g0, 1, 1)):
                out.append(rows_y(ref, colour, w, True, way))
        for way in CORNERS:
            out.append((way, ac_s.at[way - 4], ac_r.at[BACK[way] - 4], ac_r.at[way - 4], ac_r.at[4]))
        return out

    def block_messages(src, dst, ways, far):
        out = []
        for way in ways:
            give, got = block_part(BACK[way], far), block_part(way, far)
            lead = (slice(None),) * (len(src.shape) - 3)
            out.append((way, src.at[(*lead, give)], dst.at[(BACK[way], *lead, give)], dst.at[(way, *lead, got)],
                        dst.at[(len(WAYS), *lead, got)]))
        return out

    def near_part(way, c):
        n = 4 if way in XS else ((4, 3)[c] if way in YS else (3, 2)[c])
        dy = WAYS[way][0]
        return slice(0, n) if dy > 0 else slice(4 - n, 4)

    def near_more(way, c):
        n = {YS: (0, 4), XS: (0, 0), CORNERS: (4, 3)}[YS if way in YS else (XS if way in XS else CORNERS)][c]
        dy = WAYS[way][0]
        return (slice(n - 1, n) if dy > 0 else slice(4 - n, 5 - n)) if n else None

    def source_message(way, c, part):
        give, got = part(BACK[way], c), part(way, c)
        return (way, blk_g.at[c, give], in_g.at[BACK[way], c, give], in_g.at[way, c, got], in_g.at[len(WAYS), c, got])

    def sources(part):
        for way in NEAR:
            y, (to, of) = 4 * (WAYS[way][0] + 2), columns_of(WAYS[way][1])
            for c in range(2):
                rows = part(way, c)
                if rows:
                    g1[c, 0, y + rows.start : y + rows.stop, to] = in_g[way, c, rows, of]

    def column_messages():
        out = []
        for way in (0, 1, 8, 9):
            dy = WAYS[way][0]
            give, there, here = {
                -1: (slice(6, 10), slice(10, 14), slice(2, 6)), 1: (slice(6, 10), slice(2, 6), slice(10, 14)),
                -2: (slice(6, 8), slice(14, 16), slice(0, 2)), 2: (slice(8, 10), slice(0, 2), slice(14, 16))}[dy]
            out.append((way, strip.at[:, give], strip.at[:, there], strip.at[:, here], in_c.at[4, :, give]))
        return out

    def strip_messages():
        out = []
        for n, way in enumerate((2, 3, 10, 11)):
            part = slice(0, 16) if n < 2 else slice(4, 12)
            out.append((way, strip.at[:, part], in_c.at[n ^ 1, :, part], in_c.at[n, :, part], in_c.at[4, :, part]))
        return out

    def columns():
        for c in range(2):
            d1[c, 0, 2:18, 6:10] = strip[c]
            for n, way in enumerate((2, 3, 10, 11)):
                part = slice(0, 16) if n < 2 else slice(4, 12)
                to, of = columns_of(WAYS[way][1])
                d1[c, 0, 2 + part.start : 2 + part.stop, to] = in_c[n, c, part, of]

    def by_way(messages):
        ways = {}
        for m in messages:
            ways.setdefault(m[0], []).append(m)
        return ways.items()

    sent = {}

    def start(phase, messages):
        for way, group in by_way(messages):
            @pl.when(has[way])
            def _():
                for _, src, there, here, zeros in group:
                    remote(phase, way, src, there).start()

            @pl.when(jnp.logical_not(has[way]))
            def _():
                for _, src, there, here, zeros in group:
                    pltpu.make_async_copy(zeros, here, in_sem.at[phase]).start()

            if phase != FIRST or way not in YS:
                sent[way] = sent.get(way, 0) + sum(size(m[1]) for m in group)

    def finish(phase, messages):
        take(in_sem.at[phase], sum(size(m[3]) for m in messages))

    def first_sent():
        for way in YS:
            @pl.when(has[way])
            def _():
                take(lead_sem.at[way], sum(size(m[1]) for m in first_part if m[0] == way))

    def all_sent():
        always = ((nx * ny - 1) + (ny - 1) + (nx - 1) * ny) * slot
        rows = {}
        for py in range(ny):
            for px in range(nx):
                there = tuple(
                    way for way, (dy, dx) in enumerate(WAYS) if 0 <= py + dy < ny and 0 <= px + dx < nx)
                rows.setdefault((min(py, 2), min(ny - 1 - py, 2), min(px, 2), min(nx - 1 - px, 2)), there)
        low_y, high_y = jnp.minimum(gy, 2), jnp.minimum(ny - 1 - gy, 2)
        low_x, high_x = jnp.minimum(gx, 2), jnp.minimum(nx - 1 - gx, 2)
        place = ((low_y * 3 + high_y) * 3 + low_x) * 3 + high_x
        for (a, b, c, d), there in rows.items():
            @pl.when(place == ((a * 3 + b) * 3 + c) * 3 + d)
            def _():
                take(out_sem, always + sum(sent[way] for way in there))

    me = gx * ny + gy
    def spread():
        def body(s, sx, sy):
            pltpu.make_async_remote_copy(
                src_ref=gat.at[1, me], dst_ref=gat.at[1, me], send_sem=out_sem, recv_sem=in_sem.at[GATHER],
                device_id={"gx": lax.rem(gx + sx, nx), "gy": lax.rem(gy + sy, ny)}, device_id_type=MESH).start()
        each_peer(body)

    slot = size(gat.at[0, 0])

    def along_y():
        for sy in range(1, ny):
            pltpu.make_async_remote_copy(
                src_ref=gat.at[0, me], dst_ref=gat.at[0, me], send_sem=out_sem, recv_sem=in_sem.at[LINE],
                device_id={"gy": lax.rem(gy + sy, ny)}, device_id_type=MESH).start()

    def along_x():
        take(in_sem.at[LINE], (ny - 1) * slot)
        line = gat.at[0, pl.ds(gx * ny, ny)]
        for sx in range(1, nx):
            pltpu.make_async_remote_copy(
                src_ref=line, dst_ref=line, send_sem=out_sem, recv_sem=in_sem.at[PLANE],
                device_id={"gx": lax.rem(gx + sx, nx)}, device_id_type=MESH).start()

    def setup(kref, dens, colour, scale, y0, y1, rows):
        for b, near in enumerate(around(dens.at[1 - colour], colour, y0, y1, rows)):
            here = dens[colour, b, y0:y1, 0:rows]
            total = None
            for f in range(6):
                face = (scale * 0.5) * (here + near[f])
                kref[colour, b, f, y0:y1, 0:rows] = face
                total = face if total is None else total + face
            kref[colour, b, 6, y0:y1, 0:rows] = total
            kref[colour, b, 7, y0:y1, 0:rows] = jnp.where(here > 0.0, 1.0 / total, 0.0)

    def weigh(kref, other, colour, y0, y1, rows):
        out = []
        for b, near in enumerate(around(other, colour, y0, y1, rows)):
            total = kref[colour, b, 0, y0:y1, 0:rows] * near[0]
            for f in range(1, 6):
                total = total + kref[colour, b, f, y0:y1, 0:rows] * near[f]
            out.append(total)
        return out

    def update(kref, g, other, dst, colour, y0, y1, rows):
        for b, n in enumerate(weigh(kref, other, colour, y0, y1, rows)):
            dst[b, y0:y1, 0:rows] = (g[colour, b, y0:y1, 0:rows] + n) * kref[colour, b, 7, y0:y1, 0:rows]

    def first(kref, g, dst, y0, y1, rows):
        for b in range(dst.shape[0]):
            dst[b, y0:y1, 0:rows] = g[0, b, y0:y1, 0:rows] * kref[0, b, 7, y0:y1, 0:rows]

    def residual(kref, g, red, black, y0, y1, rows, x0, x1):
        out = []
        for c, (v, other) in enumerate(((red, black), (black, red))):
            n = weigh(kref, other, c, y0, y1, rows)
            out.append([
                (g[c, b, y0:y1, 0:rows] - (kref[c, b, 6, y0:y1, 0:rows] * v[b, y0:y1, 0:rows] - n[b]))[:, x0:x1]
                for b in range(len(n))])
        return out

    pltpu.make_async_copy(held, held, held_sem).wait()
    flat = permute(held[...].reshape(-1, size_z), perm[...], 0)

    def fields(flat):
        quarters = [
            jnp.swapaxes(flat[:, q * LANES : (q + 1) * LANES].reshape(8, 8, LANES), 0, 1) for q in range(4)]
        pairs = [split_even(quarters[2 * b], quarters[2 * b + 1]) for b in range(2)]
        return [pairs[b][0] for b in range(2)], [pairs[b][1] for b in range(2)]

    dens, source = fields(flat[0:64]), fields(flat[64:128])
    for c in range(2):
        for b in range(2):
            d0[c, b, 4:12, 0:8] = dens[c][b]
            g0[c, b, 4:12, 0:8] = source[c][b]
    for way in XS:
        dx = WAYS[way][1]
        for c in range(2):
            ax_s[way - 2, c] = d0[c, :, 4:12, x_own(dx, 4)]
            gx_s[way - 2, c] = g0[c, :, 4:12, x_own(dx, 2)]
    for way in CORNERS:
        dy, dx = WAYS[way]
        for b in range(2):
            ac_s[way - 4, 2 * b : 2 * b + 2] = d0[1, b, y_own(dy, 2), x_own(dx, 2)]
            an_s[way - 4, :, b : b + 1] = d0[1, b, y_own(dy, 1), x_own(dx, 1)]
            ac_s[way - 4, 4:5, b : b + 1] = d0[0, b, y_own(dy, 1), x_own(dx, 1)]
            ac_s[way - 4, 5:6, b : b + 1] = g0[0, b, y_own(dy, 1), x_own(dx, 1)]
    dens_one = coarsen(*dens)
    for c in range(2):
        strip[c, 6:10] = dens_one[c][0]
    gat[0, me] = coarsen(*dens_one)

    pl.semaphore_wait(barrier, nx * ny - 1)
    first_part, more_part = messages_first(), messages_more()
    start(FIRST, first_part)
    first_sent()
    start(MORE, more_part)
    part_c, part_s = column_messages(), strip_messages()
    along_y()
    finish(FIRST, first_part)
    start(MID_C, part_c)
    for way in XS:
        dx = WAYS[way][1]
        for c in range(2):
            d0[c, :, 4:12, x_halo(dx, 4)] = ax_r[way - 2, c]
            g0[c, :, 4:12, x_halo(dx, 2)] = gx_r[way - 2, c]
    for way in CORNERS:
        dy, dx = WAYS[way]
        for b in range(2):
            d0[1, b, y_halo(dy, 1), x_halo(dx, 1)] = an_r[way - 4, :, b : b + 1]

    setup(k0, d0, 0, 1.0, 3, 13, FINE)
    setup(k0, d0, 1, 1.0, 4, 12, FINE)
    first(k0, g0, ra, 3, 13, FINE)
    update(k0, g0, ra, ba, 1, 4, 12, FINE)
    ring_pack(ba, 2, sx_s.at[0], sc_s.at[0])
    swap = ring_messages(ba, ba, 3, sx_s.at[0], sx_r.at[0], sc_s.at[0], sc_r.at[0])
    start(SWAP, swap)
    finish(MID_C, part_c)
    start(STRIP, part_s)
    finish(MORE, more_part)
    for way in CORNERS:
        dy, dx = WAYS[way]
        for b in range(2):
            d0[1, b, y_halo(dy, 2), x_halo(dx, 2)] = ac_r[way - 4, 2 * b : 2 * b + 2]
            d0[0, b, y_halo(dy, 1), x_halo(dx, 1)] = ac_r[way - 4, 4:5, b : b + 1]
            g0[0, b, y_halo(dy, 1), x_halo(dx, 1)] = ac_r[way - 4, 5:6, b : b + 1]
    setup(k0, d0, 0, 1.0, 2, 14, FINE)
    setup(k0, d0, 1, 1.0, 3, 13, FINE)
    along_x()
    finish(SWAP, swap)
    ring_unpack(ba, 2, sx_r.at[0], sc_r.at[0])
    update(k0, g0, ba, rb, 0, 2, 14, FINE)
    update(k0, g0, rb, bb, 1, 3, 13, FINE)
    source_one = coarsen(*residual(k0, g0, rb, bb, 4, 12, FINE, 0, 8))
    for c in range(2):
        blk_g[c] = source_one[c][0]
        g1[c, 0, 8:12, 6:10] = source_one[c][0]
    part_g, far_g = [], block_messages(blk_g, in_g, range(8, 12), 1)
    for way in NEAR:
        for c in range(2):
            part_g.append(source_message(way, c, near_part))
            if near_more(way, c):
                far_g.append(source_message(way, c, near_more))
    start(MID_G, part_g)

    def blocks(ref, got, ways, far):
        for way in ways:
            dy, dx = WAYS[way]
            part = block_part(way, far)
            y, (to, of) = 4 * (dy + 2), columns_of(dx)
            for c in range(2):
                ref[c, 0, y + part.start : y + part.stop, to] = got[way, c, part, of]

    finish(STRIP, part_s)
    columns()
    for c in range(2):
        setup(k1, d1, c, 0.25, 3 + c, 17 - c, MID[1])

    take(in_sem.at[PLANE], (nx - 1) * ny * slot)
    pairs, rows = ny, 2 * nx

    def assemble(n):
        for i in range(nx):
            for p in range(2):
                cc[p, :, 2 * i : 2 * i + 2] = gat[n, i * ny : (i + 1) * ny, p]
        even = (iota((pairs, rows, LANES), 1) + iota((pairs, rows, LANES), 2)) % 2 == 0
        return jnp.where(even, cc[0], cc[1]), jnp.where(even, cc[1], cc[0])

    shape = (pairs, rows, LANES)
    tested = (iota(shape, 1) + iota(shape, 2)) % 2

    def beside(other, colour):
        low = tested == colour
        return (
            jnp.where(low, jnp.concatenate([other[-1:], other[:-1]], axis=0), other),
            jnp.where(low, other, jnp.concatenate([other[1:], other[:1]], axis=0)),
            pltpu.roll(other, 1, 1), pltpu.roll(other, rows - 1, 1),
            pltpu.roll(other, 1, 2), pltpu.roll(other, LANES - 1, 2))

    centre = assemble(0)
    for c in range(2):
        low = tested == c
        edges = (
            jnp.logical_and(low, iota(shape, 0) == 0),
            jnp.logical_and(jnp.logical_not(low), iota(shape, 0) == pairs - 1),
            iota(shape, 1) == 0, iota(shape, 1) == rows - 1, iota(shape, 2) == 0, iota(shape, 2) == LANES - 1)
        total, faces = None, []
        for near, edge in zip(beside(centre[1 - c], c), edges):
            face = 0.03125 * (centre[c] + jnp.where(edge, 0.0, near))
            total = face if total is None else total + face
            faces.append(face)
        inverse = 1.0 / total
        for f in range(6):
            kc[c, f] = jnp.where(edges[f], 0.0, faces[f] * inverse)
        kc[c, 6] = inverse

    finish(MID_G, part_g)
    sources(near_part)
    first(k1, g1, mr, 4, 16, 16)
    update(k1, g1, mr, mb, 1, 5, 15, 16)
    update(k1, g1, mb, mr, 0, 6, 14, 16)
    update(k1, g1, mr, mb, 1, 7, 13, 16)
    gat[1, me] = coarsen(*residual(k1, g1, mr, mb, 8, 12, 16, 6, 10))
    spread()
    start(FAR_G, far_g)
    ring_pack(bb, 2, sx_s.at[1], sc_s.at[1])
    keep = ring_messages(bb, bp, 3, sx_s.at[1], sx_r.at[1], sc_s.at[1], sc_r.at[1])
    start(KEEP, keep)
    blk_x[...] = mb[0, 8:12, 6:10]
    part_x = block_messages(blk_x, in_x, range(20), 2)
    start(MID_X, part_x)

    take(in_sem.at[GATHER], (nx * ny - 1) * slot)
    right = assemble(1)
    for c in range(2):
        kc[c, 7] = right[c] * kc[c, 6]

    def half(other, colour):
        total = kc[colour, 7]
        for f, near in enumerate(beside(other, colour)):
            total = total + kc[colour, f] * near
        return total

    def sweep(i, carry):
        red = half(carry[1], 0)
        return red, half(red, 1)

    red = kc[0, 7]
    red, black = lax.fori_loop(1, COARSE_SWEEPS, sweep, (red, half(red, 1)), unroll=True)
    even = tested == 0
    for i in range(nx):
        cut = slice(2 * i, 2 * i + 2)
        vc[2 + i, 2 : 2 + ny, 0] = jnp.where(even, red, black)[:, cut]
        vc[2 + i, 2 : 2 + ny, 1] = jnp.where(even, black, red)[:, cut]

    finish(MID_X, part_x)
    finish(FAR_G, far_g)
    blocks(g1, in_g, range(8, 12), 1)
    sources(near_more)
    mp[0, 8:12, 6:10] = blk_x[...]
    for way in range(20):
        dy, dx = WAYS[way]
        part = block_part(way, 2)
        y, (to, of) = 4 * (dy + 2), columns_of(dx)
        mp[0, y + part.start : y + part.stop, to] = in_x[way, part, of]
    for dx in range(5):
        window = vc[gx + dx, pl.ds(gy, 5)].reshape(10, 2, LANES)
        to, of = columns_of(dx - 2)
        mp[0, :, to] = mp[0, :, to] + double_rows(window, (0, 1))[:, of]
    update(k1, g1, mp, mr, 0, 3, 17, MID[1])
    update(k1, g1, mr, mb, 1, 4, 16, MID[1])
    update(k1, g1, mb, mr, 0, 5, 15, MID[1])
    update(k1, g1, mr, mb, 1, 6, 14, MID[1])

    finish(KEEP, keep)
    bp[:, 4:12, 0:8] = bb[:, 4:12, 0:8]
    ring_unpack(bp, 2, sx_r.at[1], sc_r.at[1])
    half_z = split_even(mr[0, 6:14], mb[0, 6:14])
    for b in range(2):
        bp[b] = bp[b] + double_rows(half_z[b], (6, 7, 8, 9, 10, 11, 4, 5))
    update(k0, g0, bp, rc, 0, 2, 14, FINE)
    update(k0, g0, rc, bc, 1, 3, 13, FINE)
    update(k0, g0, bc, rd, 0, 4, 12, FINE)
    ring_pack(rd, 1, ex_s, ec_s)
    last = ring_messages(rd, rd, 2, ex_s, ex_r, ec_s, ec_r)
    start(LAST, last)
    finish(LAST, last)
    ring_unpack(rd, 1, ex_r, ec_r)
    update(k0, g0, rd, bd, 1, 3, 13, FINE)
    left = residual(k0, g0, rd, bd, 4, 12, FINE, 0, 8)

    def lay(red, black):
        quarters = []
        for b in range(2):
            quarters.extend(split_even(red[b], black[b]))
        return jnp.concatenate([jnp.swapaxes(q, 0, 1).reshape(64, LANES) for q in quarters], axis=1)

    field = [[ref[b, 4:12, 0:8] for b in range(2)] for ref in (rd, bd)]
    flat = permute(jnp.concatenate([lay(*field), lay(*left)], axis=0), perm[...], 1)
    v_out[...] = flat[0:64].reshape(v_out.shape)
    r_out[...] = flat[64:128].reshape(r_out.shape)
    all_sent()


def hand_out(v_ref, r_ref, v_out, r_out, sem):
    pairs = ((v_ref, v_out), (r_ref, r_out))
    for n, (src, dst) in enumerate(pairs):
        for i in range(0, src.shape[0], 2):
            pltpu.make_async_copy(src.at[i : i + 2], dst.at[i : i + 2], sem.at[n]).start()
    for n, (src, dst) in enumerate(pairs):
        pltpu.make_async_copy(src, dst, sem.at[n]).wait()


def solution(mesh):
    nx, ny = mesh.shape["gx"], mesh.shape["gy"]

    def shards(right_side, inverse_density):
        x, y, z = right_side.shape
        assert (x, y, z) == (8, 8, 4 * LANES)

        def vmem(*shape):
            return pltpu.VMEM((*shape, LANES), F32)

        fine = (2, FINE, FINE)
        mid = (1, *MID)
        result = pltpu.VMEM(right_side.shape, F32)
        v, r = pl.pallas_call(
            functools.partial(kernel, nx, ny),
            out_shape=(result, result),
            in_specs=[pl.BlockSpec(memory_space=pl.ANY)] * 2,
            out_specs=(pl.BlockSpec(memory_space=pltpu.VMEM),) * 2,
            scratch_shapes=[
                pltpu.VMEM((z, z), jnp.bfloat16),
                pltpu.VMEM((2, x, y, z), F32),
                vmem(2, *fine), vmem(2, *fine), vmem(2, 2, 8, FINE, FINE),
                *[vmem(*fine)] * 9,
                vmem(2, 2, 2, 8, 4), vmem(3, 2, 2, 8, 4), vmem(2, 2, 2, 8, 2), vmem(3, 2, 2, 8, 2), vmem(4, 1, 2), vmem(5, 1, 2), vmem(4, 6, 2), vmem(5, 6, 2),
                vmem(2, 2, 2, 8, 4), vmem(2, 3, 2, 8, 4), vmem(2, 4, 2, 2, 2), vmem(2, 5, 2, 2, 2),
                vmem(2, 2, 8, 2), vmem(3, 2, 8, 2), vmem(4, 2, 1, 1), vmem(5, 2, 1, 1),
                vmem(2, *mid), vmem(2, *mid), vmem(2, 1, 8, *MID), *[vmem(*mid)] * 3,
                vmem(2, 16, 4), vmem(2, 4, 4), vmem(4, 4),
                vmem(5, 2, 16, 4), vmem(len(WAYS) + 1, 2, 4, 4), vmem(len(WAYS) + 1, 4, 4),
                vmem(2, nx * ny, 2, 2), vmem(2, ny, 2 * nx), vmem(2, 8, ny, 2 * nx), vmem(nx + 4, ny + 4, 2, 2),
                vmem(2, 3, 8), vmem(6144),
                pltpu.SemaphoreType.DMA,
                pltpu.SemaphoreType.DMA((2,)),
                pltpu.SemaphoreType.DMA,
                pltpu.SemaphoreType.DMA((PHASES,)),
            ],
            compiler_params=pltpu.CompilerParams(
                collective_id=0, has_side_effects=True, vmem_limit_bytes=40 * 1024 * 1024
            ),
        )(*(pltpu.with_memory_space_constraint(a, pltpu.HBM) for a in (right_side, inverse_density)))
        out = jax.ShapeDtypeStruct(right_side.shape, F32)
        return pl.pallas_call(
            hand_out,
            out_shape=(out, out),
            in_specs=[pl.BlockSpec(memory_space=pltpu.VMEM)] * 2,
            out_specs=(pl.BlockSpec(memory_space=pl.ANY),) * 2,
            scratch_shapes=[pltpu.SemaphoreType.DMA((2,))],
            compiler_params=pltpu.CompilerParams(vmem_limit_bytes=1024 * 1024),
        )(v, r)

    spec = P("gx", "gy", None)
    return jax.shard_map(shards, mesh=mesh, in_specs=(spec, spec), out_specs=(spec, spec), check_vma=False)
```

```python
import functools
import math

import jax
import jax.numpy as jnp
from jax import lax
from jax.experimental import pallas as pl
from jax.experimental.pallas import tpu as pltpu
from jax.sharding import PartitionSpec as P

SWEEPS = 2
COARSE_SWEEPS = 8
MESH = pl.DeviceIdType.MESH
LANES = 128
F32 = jnp.float32

FINE, MID = 16, (20, 16)

WAYS = ((-1, 0), (1, 0), (0, -1), (0, 1), (-1, -1), (-1, 1), (1, -1), (1, 1),
        (-2, 0), (2, 0), (0, -2), (0, 2),
        (-2, -1), (-2, 1), (2, -1), (2, 1), (-1, -2), (-1, 2), (1, -2), (1, 2))
BACK = tuple(WAYS.index((-dy, -dx)) for dy, dx in WAYS)
FIRST, MORE, SWAP, KEEP, LAST, MID_C, STRIP, MID_G, FAR_G, MID_X = range(10)
GATHER, LINE, PLANE = 10, 11, 12
PHASES = 13
YS, XS, CORNERS, NEAR = (0, 1), (2, 3), (4, 5, 6, 7), range(8)


def iota(shape, dim):
    return lax.broadcasted_iota(jnp.int32, shape, dim)


def lane_prev(a):
    return jnp.where(iota(a.shape, 2) == 0, 0.0, pltpu.roll(a, 1, 2))


def lane_next(a):
    return jnp.where(iota(a.shape, 2) == LANES - 1, 0.0, pltpu.roll(a, LANES - 1, 2))


def even_cells(shape):
    return (iota(shape, 0) + iota(shape, 1)) % 2 == 0


def z_other(o, colour, first):
    shape = o[0].shape
    even = (iota(shape, 0) + iota(shape, 1)) % 2 == first % 2
    low = even if colour == 0 else jnp.logical_not(even)
    last = len(o) - 1
    out = []
    for b in range(last + 1):
        before = o[b - 1] if b > 0 else lane_prev(o[last])
        after = o[b + 1] if b < last else lane_next(o[0])
        out.append(jnp.where(low, before, after))
    return out


def around(other, colour, y0, y1, rows):
    groups = range(other.shape[0])
    mid = [other[b, y0:y1, 0:rows] for b in groups]
    zo = z_other(mid, colour, y0)
    return [
        (
            other[b, y0 - 1 : y1 - 1, 0:rows],
            other[b, y0 + 1 : y1 + 1, 0:rows],
            pltpu.roll(mid[b], 1, 1),
            pltpu.roll(mid[b], rows - 1, 1),
            mid[b],
            zo[b],
        )
        for b in groups
    ]


def split_even(zero, one):
    even = even_cells(zero.shape)
    return jnp.where(even, zero, one), jnp.where(even, one, zero)


def pair_rows(a):
    rows = a.shape[1] // 2
    a = a.reshape(a.shape[0] // 2, 2, a.shape[1], LANES)
    a = a[:, 0] + a[:, 1]
    pick = iota((a.shape[0], rows, LANES), 1)
    out = a[:, 0:1] + a[:, 1:2]
    out = jnp.broadcast_to(out, pick.shape)
    for j in range(1, rows):
        out = jnp.where(pick == j, a[:, 2 * j : 2 * j + 1] + a[:, 2 * j + 1 : 2 * j + 2], out)
    return out * 0.125


def double_rows(a, order):
    y = a.shape[0]
    pick = iota((y, 2 * len(order), LANES), 1) // 2
    out = jnp.broadcast_to(a[:, order[0] : order[0] + 1], pick.shape)
    for n, j in enumerate(order[1:], 1):
        out = jnp.where(pick == n, a[:, j : j + 1], out)
    return jnp.concatenate([out[i // 2 : i // 2 + 1] for i in range(2 * y)], axis=0)


def three(x):
    high = x.astype(jnp.bfloat16)
    rest = x - high.astype(F32)
    middle = rest.astype(jnp.bfloat16)
    low = (rest - middle.astype(F32)).astype(jnp.bfloat16)
    return jnp.concatenate([high, middle, low], axis=0)


def permute(x, matrix, side):
    n = x.shape[0]
    out = lax.dot_general(three(x), matrix, (((1,), (side,)), ((), ())), preferred_element_type=F32)
    return (out[0:n] + out[n : 2 * n]) + out[2 * n :]


def y_own(d, w):
    return slice(4, 12) if d == 0 else (slice(12 - w, 12) if d > 0 else slice(4, 4 + w))


def y_halo(d, w):
    return slice(4, 12) if d == 0 else (slice(12, 12 + w) if d > 0 else slice(4 - w, 4))


def x_own(d, w):
    return slice(0, 8) if d == 0 else (slice(8 - w, 8) if d > 0 else slice(0, w))


def x_halo(d, w):
    return slice(0, 8) if d == 0 else (slice(8, 8 + w) if d > 0 else slice(FINE - w, FINE))


def columns_of(dx):
    start = 6 + 4 * dx
    low, high = max(start, 0), min(start + 4, MID[1])
    return slice(low, high), slice(low - start, high - start)


def outer(part, d):
    return slice(part.stop - 1, part.stop) if d > 0 else slice(part.start, part.start + 1)


def block_part(way, far):
    dy, dx = WAYS[way]
    n = far if abs(dy) == 2 else (2 if abs(dx) == 2 and dy else 4)
    return slice(0, n) if dy > 0 else slice(4 - n, 4)


def kernel(nx, ny, g_ref, c_ref, v_out, r_out, perm, held, d0, g0, k0, ra, ba, rb, bb, bp, rc, bc, rd, bd,
           ax_s, ax_r, gx_s, gx_r, an_s, an_r, ac_s, ac_r, sx_s, sx_r, sc_s, sc_r, ex_s, ex_r, ec_s, ec_r,
           d1, g1, k1, mr, mb, mp, strip, blk_g, blk_x, in_c, in_g, in_x,
           gat, cc, kc, vc, zero_y, bulk, held_sem, lead_sem, out_sem, in_sem):
    gx, gy = lax.axis_index("gx"), lax.axis_index("gy")

    def inside(way):
        dy, dx = WAYS[way]
        tests = []
        if dy:
            tests.append(gy + dy >= 0 if dy < 0 else gy + dy < ny)
        if dx:
            tests.append(gx + dx >= 0 if dx < 0 else gx + dx < nx)
        return tests[0] if len(tests) == 1 else jnp.logical_and(*tests)

    def device(way):
        dy, dx = WAYS[way]
        out = {}
        if dx:
            out["gx"] = gx + dx
        if dy:
            out["gy"] = gy + dy
        return out

    has = [inside(way) for way in range(len(WAYS))]
    target = [device(way) for way in range(len(WAYS))]

    def each_peer(fn):
        if nx * ny <= 64:
            for s in range(1, nx * ny):
                fn(s, s // ny, s % ny)
        else:
            def body(s, carry):
                fn(s, s // ny, lax.rem(s, ny))
                return carry
            lax.fori_loop(1, nx * ny, body, 0)

    loads = [
        pltpu.make_async_copy(ref.at[i : i + 2], held.at[n, i : i + 2], held_sem)
        for n, ref in enumerate((c_ref, g_ref)) for i in range(0, 8, 2)
    ]
    for load in loads:
        load.start()

    barrier = pltpu.get_barrier_semaphore()

    def greet(s, sx, sy):
        pl.semaphore_signal(
            barrier, inc=1, device_id={"gx": lax.rem(gx + sx, nx), "gy": lax.rem(gy + sy, ny)}, device_id_type=MESH)

    each_peer(greet)

    for ref in (ax_r, gx_r, ex_r):
        ref[2] = jnp.zeros(ref.shape[1:], F32)
    for ref in (an_r, ac_r, ec_r):
        ref[4] = jnp.zeros(ref.shape[1:], F32)
    for n in range(2):
        sx_r[n, 2] = jnp.zeros(sx_r.shape[2:], F32)
        sc_r[n, 4] = jnp.zeros(sc_r.shape[2:], F32)
    in_c[4] = jnp.zeros(in_c.shape[1:], F32)
    for ref in (in_g, in_x):
        ref[len(WAYS)] = jnp.zeros(ref.shape[1:], F32)
    zero_y[...] = jnp.zeros(zero_y.shape, F32)
    vc[...] = jnp.zeros(vc.shape, F32)

    size_z = 4 * LANES
    row, col = iota((size_z, size_z), 0), iota((size_z, size_z), 1)
    perm[...] = (row == 4 * (col % LANES) + col // LANES).astype(F32).astype(jnp.bfloat16)

    def coarsen(red, black):
        pair = [pair_rows(red[b] + black[b]) for b in range(len(red))]
        if len(pair) == 1:
            return pair[0]
        first, second = split_even(pair[0], pair[1])
        return [first], [second]

    def remote(phase, way, src, dst):
        lead = phase == FIRST and way in YS
        return pltpu.make_async_remote_copy(
            src_ref=src, dst_ref=dst, send_sem=lead_sem.at[way] if lead else out_sem, recv_sem=in_sem.at[phase],
            device_id=target[way], device_id_type=MESH)

    def size(ref):
        return math.prod(ref.shape[:-1])

    def take(sem, rows):
        pltpu.make_async_copy(bulk.at[0:rows], bulk.at[0:rows], sem).wait()

    def ring_messages(src, dst, w, x_s, x_r, c_s, c_r):
        out = []
        for way in YS:
            dy = WAYS[way][0]
            out.append((way, src.at[:, y_own(dy, w), 0:8], dst.at[:, y_halo(-dy, w), 0:8], dst.at[:, y_halo(dy, w), 0:8], zero_y.at[:, 0:w]))
        for way in XS:
            out.append((way, x_s.at[way - 2], x_r.at[BACK[way] - 2], x_r.at[way - 2], x_r.at[2]))
        for way in CORNERS:
            out.append((way, c_s.at[way - 4], c_r.at[BACK[way] - 4], c_r.at[way - 4], c_r.at[4]))
        return out

    def ring_pack(src, cw, x_s, c_s):
        for way in XS:
            x_s[way - 2] = src[:, 4:12, x_own(WAYS[way][1], x_s.shape[-2])]
        for way in CORNERS:
            dy, dx = WAYS[way]
            c_s[way - 4] = src[:, y_own(dy, cw), x_own(dx, cw)]

    def ring_unpack(dst, cw, x_r, c_r):
        for way in XS:
            dst[:, 4:12, x_halo(WAYS[way][1], x_r.shape[-2])] = x_r[way - 2]
        for way in CORNERS:
            dy, dx = WAYS[way]
            dst[:, y_halo(dy, cw), x_halo(dx, cw)] = c_r[way - 4]

    def rows_y(ref, colour, w, only, way):
        dy = WAYS[way][0]
        own, there, here = y_own(dy, w), y_halo(-dy, w), y_halo(dy, w)
        if only:
            own, there, here = (outer(a, d) for a, d in ((own, -dy), (there, -dy), (here, dy)))
        n = 1 if only else w
        return (way, ref.at[colour, :, own, 0:8], ref.at[colour, :, there, 0:8], ref.at[colour, :, here, 0:8],
                zero_y.at[:, 0:n])

    def messages_first():
        out = []
        for way in YS:
            for ref, colour, w in ((d0, 0, 1), (d0, 1, 2), (g0, 0, 1)):
                out.append(rows_y(ref, colour, w, False, way))
        for way in CORNERS:
            out.append((way, an_s.at[way - 4], an_r.at[BACK[way] - 4], an_r.at[way - 4], an_r.at[4]))
        for way in XS:
            out.append((way, ax_s.at[way - 2], ax_r.at[BACK[way] - 2], ax_r.at[way - 2], ax_r.at[2]))
            out.append((way, gx_s.at[way - 2], gx_r.at[BACK[way] - 2], gx_r.at[way - 2], gx_r.at[2]))
        return out

    def messages_more():
        out = []
        for way in YS:
            for ref, colour, w in ((d0, 0, 2), (d0, 1, 3), (g0, 0, 2), (g0, 1, 1)):
                out.append(rows_y(ref, colour, w, True, way))
        for way in CORNERS:
            out.append((way, ac_s.at[way - 4], ac_r.at[BACK[way] - 4], ac_r.at[way - 4], ac_r.at[4]))
        return out

    def block_messages(src, dst, ways, far):
        out = []
        for way in ways:
            give, got = block_part(BACK[way], far), block_part(way, far)
            lead = (slice(None),) * (len(src.shape) - 3)
            out.append((way, src.at[(*lead, give)], dst.at[(BACK[way], *lead, give)], dst.at[(way, *lead, got)],
                        dst.at[(len(WAYS), *lead, got)]))
        return out

    def near_part(way, c):
        n = 4 if way in XS else ((4, 3)[c] if way in YS else (3, 2)[c])
        dy = WAYS[way][0]
        return slice(0, n) if dy > 0 else slice(4 - n, 4)

    def near_more(way, c):
        n = {YS: (0, 4), XS: (0, 0), CORNERS: (4, 3)}[YS if way in YS else (XS if way in XS else CORNERS)][c]
        dy = WAYS[way][0]
        return (slice(n - 1, n) if dy > 0 else slice(4 - n, 5 - n)) if n else None

    def source_message(way, c, part):
        give, got = part(BACK[way], c), part(way, c)
        return (way, blk_g.at[c, give], in_g.at[BACK[way], c, give], in_g.at[way, c, got], in_g.at[len(WAYS), c, got])

    def sources(part):
        for way in NEAR:
            y, (to, of) = 4 * (WAYS[way][0] + 2), columns_of(WAYS[way][1])
            for c in range(2):
                rows = part(way, c)
                if rows:
                    g1[c, 0, y + rows.start : y + rows.stop, to] = in_g[way, c, rows, of]

    def column_messages():
        out = []
        for way in (0, 1, 8, 9):
            dy = WAYS[way][0]
            give, there, here = {
                -1: (slice(6, 10), slice(10, 14), slice(2, 6)), 1: (slice(6, 10), slice(2, 6), slice(10, 14)),
                -2: (slice(6, 8), slice(14, 16), slice(0, 2)), 2: (slice(8, 10), slice(0, 2), slice(14, 16))}[dy]
            out.append((way, strip.at[:, give], strip.at[:, there], strip.at[:, here], in_c.at[4, :, give]))
        return out

    def strip_messages():
        out = []
        for n, way in enumerate((2, 3, 10, 11)):
            part = slice(0, 16) if n < 2 else slice(4, 12)
            out.append((way, strip.at[:, part], in_c.at[n ^ 1, :, part], in_c.at[n, :, part], in_c.at[4, :, part]))
        return out

    def columns():
        for c in range(2):
            d1[c, 0, 2:18, 6:10] = strip[c]
            for n, way in enumerate((2, 3, 10, 11)):
                part = slice(0, 16) if n < 2 else slice(4, 12)
                to, of = columns_of(WAYS[way][1])
                d1[c, 0, 2 + part.start : 2 + part.stop, to] = in_c[n, c, part, of]

    def by_way(messages):
        ways = {}
        for m in messages:
            ways.setdefault(m[0], []).append(m)
        return ways.items()

    sent = {}

    def start(phase, messages):
        for way, group in by_way(messages):
            @pl.when(has[way])
            def _():
                for _, src, there, here, zeros in group:
                    remote(phase, way, src, there).start()

            @pl.when(jnp.logical_not(has[way]))
            def _():
                for _, src, there, here, zeros in group:
                    pltpu.make_async_copy(zeros, here, in_sem.at[phase]).start()

            if phase != FIRST or way not in YS:
                sent[way] = sent.get(way, 0) + sum(size(m[1]) for m in group)

    def finish(phase, messages):
        take(in_sem.at[phase], sum(size(m[3]) for m in messages))

    def first_sent():
        for way in YS:
            @pl.when(has[way])
            def _():
                take(lead_sem.at[way], sum(size(m[1]) for m in first_part if m[0] == way))

    def all_sent():
        always = ((nx * ny - 1) + (ny - 1) + (nx - 1) * ny) * slot
        rows = {}
        for py in range(ny):
            for px in range(nx):
                there = tuple(
                    way for way, (dy, dx) in enumerate(WAYS) if 0 <= py + dy < ny and 0 <= px + dx < nx)
                rows.setdefault((min(py, 2), min(ny - 1 - py, 2), min(px, 2), min(nx - 1 - px, 2)), there)
        low_y, high_y = jnp.minimum(gy, 2), jnp.minimum(ny - 1 - gy, 2)
        low_x, high_x = jnp.minimum(gx, 2), jnp.minimum(nx - 1 - gx, 2)
        place = ((low_y * 3 + high_y) * 3 + low_x) * 3 + high_x
        for (a, b, c, d), there in rows.items():
            @pl.when(place == ((a * 3 + b) * 3 + c) * 3 + d)
            def _():
                take(out_sem, always + sum(sent[way] for way in there))

    me = gx * ny + gy
    def spread():
        def body(s, sx, sy):
            pltpu.make_async_remote_copy(
                src_ref=gat.at[1, me], dst_ref=gat.at[1, me], send_sem=out_sem, recv_sem=in_sem.at[GATHER],
                device_id={"gx": lax.rem(gx + sx, nx), "gy": lax.rem(gy + sy, ny)}, device_id_type=MESH).start()
        each_peer(body)

    slot = size(gat.at[0, 0])

    def along_y():
        for sy in range(1, ny):
            pltpu.make_async_remote_copy(
                src_ref=gat.at[0, me], dst_ref=gat.at[0, me], send_sem=out_sem, recv_sem=in_sem.at[LINE],
                device_id={"gy": lax.rem(gy + sy, ny)}, device_id_type=MESH).start()

    def along_x():
        take(in_sem.at[LINE], (ny - 1) * slot)
        line = gat.at[0, pl.ds(gx * ny, ny)]
        for sx in range(1, nx):
            pltpu.make_async_remote_copy(
                src_ref=line, dst_ref=line, send_sem=out_sem, recv_sem=in_sem.at[PLANE],
                device_id={"gx": lax.rem(gx + sx, nx)}, device_id_type=MESH).start()

    def setup(kref, dens, colour, scale, y0, y1, rows):
        for b, near in enumerate(around(dens.at[1 - colour], colour, y0, y1, rows)):
            here = dens[colour, b, y0:y1, 0:rows]
            total = None
            for f in range(6):
                face = (scale * 0.5) * (here + near[f])
                kref[colour, b, f, y0:y1, 0:rows] = face
                total = face if total is None else total + face
            kref[colour, b, 6, y0:y1, 0:rows] = total
            kref[colour, b, 7, y0:y1, 0:rows] = jnp.where(here > 0.0, 1.0 / total, 0.0)

    def weigh(kref, other, colour, y0, y1, rows):
        out = []
        for b, near in enumerate(around(other, colour, y0, y1, rows)):
            total = kref[colour, b, 0, y0:y1, 0:rows] * near[0]
            for f in range(1, 6):
                total = total + kref[colour, b, f, y0:y1, 0:rows] * near[f]
            out.append(total)
        return out

    def update(kref, g, other, dst, colour, y0, y1, rows):
        for b, n in enumerate(weigh(kref, other, colour, y0, y1, rows)):
            dst[b, y0:y1, 0:rows] = (g[colour, b, y0:y1, 0:rows] + n) * kref[colour, b, 7, y0:y1, 0:rows]

    def first(kref, g, dst, y0, y1, rows):
        for b in range(dst.shape[0]):
            dst[b, y0:y1, 0:rows] = g[0, b, y0:y1, 0:rows] * kref[0, b, 7, y0:y1, 0:rows]

    def residual(kref, g, red, black, y0, y1, rows, x0, x1):
        out = []
        for c, (v, other) in enumerate(((red, black), (black, red))):
            n = weigh(kref, other, c, y0, y1, rows)
            out.append([
                (g[c, b, y0:y1, 0:rows] - (kref[c, b, 6, y0:y1, 0:rows] * v[b, y0:y1, 0:rows] - n[b]))[:, x0:x1]
                for b in range(len(n))])
        return out

    pltpu.make_async_copy(held, held, held_sem).wait()
    flat = permute(held[...].reshape(-1, size_z), perm[...], 0)

    def fields(flat):
        quarters = [
            jnp.swapaxes(flat[:, q * LANES : (q + 1) * LANES].reshape(8, 8, LANES), 0, 1) for q in range(4)]
        pairs = [split_even(quarters[2 * b], quarters[2 * b + 1]) for b in range(2)]
        return [pairs[b][0] for b in range(2)], [pairs[b][1] for b in range(2)]

    dens, source = fields(flat[0:64]), fields(flat[64:128])
    for c in range(2):
        for b in range(2):
            d0[c, b, 4:12, 0:8] = dens[c][b]
            g0[c, b, 4:12, 0:8] = source[c][b]
    for way in XS:
        dx = WAYS[way][1]
        for c in range(2):
            ax_s[way - 2, c] = d0[c, :, 4:12, x_own(dx, 4)]
            gx_s[way - 2, c] = g0[c, :, 4:12, x_own(dx, 2)]
    for way in CORNERS:
        dy, dx = WAYS[way]
        for b in range(2):
            ac_s[way - 4, 2 * b : 2 * b + 2] = d0[1, b, y_own(dy, 2), x_own(dx, 2)]
            an_s[way - 4, :, b : b + 1] = d0[1, b, y_own(dy, 1), x_own(dx, 1)]
            ac_s[way - 4, 4:5, b : b + 1] = d0[0, b, y_own(dy, 1), x_own(dx, 1)]
            ac_s[way - 4, 5:6, b : b + 1] = g0[0, b, y_own(dy, 1), x_own(dx, 1)]
    dens_one = coarsen(*dens)
    for c in range(2):
        strip[c, 6:10] = dens_one[c][0]
    gat[0, me] = coarsen(*dens_one)

    pl.semaphore_wait(barrier, nx * ny - 1)
    first_part, more_part = messages_first(), messages_more()
    start(FIRST, first_part)
    first_sent()
    start(MORE, more_part)
    part_c, part_s = column_messages(), strip_messages()
    along_y()
    finish(FIRST, first_part)
    start(MID_C, part_c)
    for way in XS:
        dx = WAYS[way][1]
        for c in range(2):
            d0[c, :, 4:12, x_halo(dx, 4)] = ax_r[way - 2, c]
            g0[c, :, 4:12, x_halo(dx, 2)] = gx_r[way - 2, c]
    for way in CORNERS:
        dy, dx = WAYS[way]
        for b in range(2):
            d0[1, b, y_halo(dy, 1), x_halo(dx, 1)] = an_r[way - 4, :, b : b + 1]

    setup(k0, d0, 0, 1.0, 3, 13, FINE)
    setup(k0, d0, 1, 1.0, 4, 12, FINE)
    first(k0, g0, ra, 3, 13, FINE)
    update(k0, g0, ra, ba, 1, 4, 12, FINE)
    ring_pack(ba, 2, sx_s.at[0], sc_s.at[0])
    swap = ring_messages(ba, ba, 3, sx_s.at[0], sx_r.at[0], sc_s.at[0], sc_r.at[0])
    start(SWAP, swap)
    finish(MID_C, part_c)
    start(STRIP, part_s)
    finish(MORE, more_part)
    for way in CORNERS:
        dy, dx = WAYS[way]
        for b in range(2):
            d0[1, b, y_halo(dy, 2), x_halo(dx, 2)] = ac_r[way - 4, 2 * b : 2 * b + 2]
            d0[0, b, y_halo(dy, 1), x_halo(dx, 1)] = ac_r[way - 4, 4:5, b : b + 1]
            g0[0, b, y_halo(dy, 1), x_halo(dx, 1)] = ac_r[way - 4, 5:6, b : b + 1]
    setup(k0, d0, 0, 1.0, 2, 14, FINE)
    setup(k0, d0, 1, 1.0, 3, 13, FINE)
    along_x()
    finish(SWAP, swap)
    ring_unpack(ba, 2, sx_r.at[0], sc_r.at[0])
    update(k0, g0, ba, rb, 0, 2, 14, FINE)
    update(k0, g0, rb, bb, 1, 3, 13, FINE)
    source_one = coarsen(*residual(k0, g0, rb, bb, 4, 12, FINE, 0, 8))
    for c in range(2):
        blk_g[c] = source_one[c][0]
        g1[c, 0, 8:12, 6:10] = source_one[c][0]
    part_g, far_g = [], block_messages(blk_g, in_g, range(8, 12), 1)
    for way in NEAR:
        for c in range(2):
            part_g.append(source_message(way, c, near_part))
            if near_more(way, c):
                far_g.append(source_message(way, c, near_more))
    start(MID_G, part_g)

    def blocks(ref, got, ways, far):
        for way in ways:
            dy, dx = WAYS[way]
            part = block_part(way, far)
            y, (to, of) = 4 * (dy + 2), columns_of(dx)
            for c in range(2):
                ref[c, 0, y + part.start : y + part.stop, to] = got[way, c, part, of]

    finish(STRIP, part_s)
    columns()
    for c in range(2):
        setup(k1, d1, c, 0.25, 3 + c, 17 - c, MID[1])

    take(in_sem.at[PLANE], (nx - 1) * ny * slot)
    pairs, rows = ny, 2 * nx

    def assemble(n):
        for i in range(nx):
            for p in range(2):
                cc[p, :, 2 * i : 2 * i + 2] = gat[n, i * ny : (i + 1) * ny, p]
        even = (iota((pairs, rows, LANES), 1) + iota((pairs, rows, LANES), 2)) % 2 == 0
        return jnp.where(even, cc[0], cc[1]), jnp.where(even, cc[1], cc[0])

    shape = (pairs, rows, LANES)
    tested = (iota(shape, 1) + iota(shape, 2)) % 2

    def beside(other, colour):
        low = tested == colour
        return (
            jnp.where(low, jnp.concatenate([other[-1:], other[:-1]], axis=0), other),
            jnp.where(low, other, jnp.concatenate([other[1:], other[:1]], axis=0)),
            pltpu.roll(other, 1, 1), pltpu.roll(other, rows - 1, 1),
            pltpu.roll(other, 1, 2), pltpu.roll(other, LANES - 1, 2))

    centre = assemble(0)
    for c in range(2):
        low = tested == c
        edges = (
            jnp.logical_and(low, iota(shape, 0) == 0),
            jnp.logical_and(jnp.logical_not(low), iota(shape, 0) == pairs - 1),
            iota(shape, 1) == 0, iota(shape, 1) == rows - 1, iota(shape, 2) == 0, iota(shape, 2) == LANES - 1)
        total, faces = None, []
        for near, edge in zip(beside(centre[1 - c], c), edges):
            face = 0.03125 * (centre[c] + jnp.where(edge, 0.0, near))
            total = face if total is None else total + face
            faces.append(face)
        inverse = 1.0 / total
        faces = [jnp.where(edge, 0.0, face * inverse) for edge, face in zip(edges, faces)]
        faces[:2] = jnp.where(low, faces[1], faces[0]), jnp.where(low, faces[0], faces[1])
        for f in range(6):
            kc[c, f] = faces[f]
        kc[c, 6] = inverse

    finish(MID_G, part_g)
    sources(near_part)
    first(k1, g1, mr, 4, 16, 16)
    update(k1, g1, mr, mb, 1, 5, 15, 16)
    update(k1, g1, mb, mr, 0, 6, 14, 16)
    update(k1, g1, mr, mb, 1, 7, 13, 16)
    gat[1, me] = coarsen(*residual(k1, g1, mr, mb, 8, 12, 16, 6, 10))
    spread()
    start(FAR_G, far_g)
    ring_pack(bb, 2, sx_s.at[1], sc_s.at[1])
    keep = ring_messages(bb, bp, 3, sx_s.at[1], sx_r.at[1], sc_s.at[1], sc_r.at[1])
    start(KEEP, keep)
    blk_x[...] = mb[0, 8:12, 6:10]
    part_x = block_messages(blk_x, in_x, range(20), 2)
    start(MID_X, part_x)

    take(in_sem.at[GATHER], (nx * ny - 1) * slot)
    right = assemble(1)
    for c in range(2):
        kc[c, 7] = right[c] * kc[c, 6]

    def half(other, colour):
        total = kc[colour, 7]
        before, after = (jnp.concatenate(a, axis=0) for a in ((other[-1:], other[:-1]), (other[1:], other[:1])))
        nears = (other, jnp.where(tested == colour, before, after), *beside(other, colour)[2:])
        for f, near in enumerate(nears):
            total = total + kc[colour, f] * near
        return total

    def sweep(i, carry):
        red = half(carry[1], 0)
        return red, half(red, 1)

    red = kc[0, 7]
    red, black = lax.fori_loop(1, COARSE_SWEEPS, sweep, (red, half(red, 1)), unroll=True)
    even = tested == 0
    for i in range(nx):
        cut = slice(2 * i, 2 * i + 2)
        vc[2 + i, 2 : 2 + ny, 0] = jnp.where(even, red, black)[:, cut]
        vc[2 + i, 2 : 2 + ny, 1] = jnp.where(even, black, red)[:, cut]

    finish(MID_X, part_x)
    finish(FAR_G, far_g)
    blocks(g1, in_g, range(8, 12), 1)
    sources(near_more)
    mp[0, 8:12, 6:10] = blk_x[...]
    for way in range(20):
        dy, dx = WAYS[way]
        part = block_part(way, 2)
        y, (to, of) = 4 * (dy + 2), columns_of(dx)
        mp[0, y + part.start : y + part.stop, to] = in_x[way, part, of]
    for dx in range(5):
        window = vc[gx + dx, pl.ds(gy, 5)].reshape(10, 2, LANES)
        to, of = columns_of(dx - 2)
        mp[0, :, to] = mp[0, :, to] + double_rows(window, (0, 1))[:, of]
    update(k1, g1, mp, mr, 0, 3, 17, MID[1])
    update(k1, g1, mr, mb, 1, 4, 16, MID[1])
    update(k1, g1, mb, mr, 0, 5, 15, MID[1])
    update(k1, g1, mr, mb, 1, 6, 14, MID[1])

    finish(KEEP, keep)
    bp[:, 4:12, 0:8] = bb[:, 4:12, 0:8]
    ring_unpack(bp, 2, sx_r.at[1], sc_r.at[1])
    half_z = split_even(mr[0, 6:14], mb[0, 6:14])
    for b in range(2):
        bp[b] = bp[b] + double_rows(half_z[b], (6, 7, 8, 9, 10, 11, 4, 5))
    update(k0, g0, bp, rc, 0, 2, 14, FINE)
    update(k0, g0, rc, bc, 1, 3, 13, FINE)
    update(k0, g0, bc, rd, 0, 4, 12, FINE)
    ring_pack(rd, 1, ex_s, ec_s)
    last = ring_messages(rd, rd, 2, ex_s, ex_r, ec_s, ec_r)
    start(LAST, last)
    finish(LAST, last)
    ring_unpack(rd, 1, ex_r, ec_r)
    update(k0, g0, rd, bd, 1, 3, 13, FINE)
    left = residual(k0, g0, rd, bd, 4, 12, FINE, 0, 8)

    def lay(red, black):
        quarters = []
        for b in range(2):
            quarters.extend(split_even(red[b], black[b]))
        return jnp.concatenate([jnp.swapaxes(q, 0, 1).reshape(64, LANES) for q in quarters], axis=1)

    field = [[ref[b, 4:12, 0:8] for b in range(2)] for ref in (rd, bd)]
    flat = permute(jnp.concatenate([lay(*field), lay(*left)], axis=0), perm[...], 1)
    v_out[...] = flat[0:64].reshape(v_out.shape)
    r_out[...] = flat[64:128].reshape(r_out.shape)
    all_sent()


def hand_out(v_ref, r_ref, v_out, r_out, sem):
    pairs = ((v_ref, v_out), (r_ref, r_out))
    for n, (src, dst) in enumerate(pairs):
        for i in range(0, src.shape[0], 2):
            pltpu.make_async_copy(src.at[i : i + 2], dst.at[i : i + 2], sem.at[n]).start()
    for n, (src, dst) in enumerate(pairs):
        pltpu.make_async_copy(src, dst, sem.at[n]).wait()


def solution(mesh):
    nx, ny = mesh.shape["gx"], mesh.shape["gy"]

    def shards(right_side, inverse_density):
        x, y, z = right_side.shape
        assert (x, y, z) == (8, 8, 4 * LANES)

        def vmem(*shape):
            return pltpu.VMEM((*shape, LANES), F32)

        fine = (2, FINE, FINE)
        mid = (1, *MID)
        result = pltpu.VMEM(right_side.shape, F32)
        v, r = pl.pallas_call(
            functools.partial(kernel, nx, ny),
            out_shape=(result, result),
            in_specs=[pl.BlockSpec(memory_space=pl.ANY)] * 2,
            out_specs=(pl.BlockSpec(memory_space=pltpu.VMEM),) * 2,
            scratch_shapes=[
                pltpu.VMEM((z, z), jnp.bfloat16),
                pltpu.VMEM((2, x, y, z), F32),
                vmem(2, *fine), vmem(2, *fine), vmem(2, 2, 8, FINE, FINE),
                *[vmem(*fine)] * 9,
                vmem(2, 2, 2, 8, 4), vmem(3, 2, 2, 8, 4), vmem(2, 2, 2, 8, 2), vmem(3, 2, 2, 8, 2), vmem(4, 1, 2), vmem(5, 1, 2), vmem(4, 6, 2), vmem(5, 6, 2),
                vmem(2, 2, 2, 8, 4), vmem(2, 3, 2, 8, 4), vmem(2, 4, 2, 2, 2), vmem(2, 5, 2, 2, 2),
                vmem(2, 2, 8, 2), vmem(3, 2, 8, 2), vmem(4, 2, 1, 1), vmem(5, 2, 1, 1),
                vmem(2, *mid), vmem(2, *mid), vmem(2, 1, 8, *MID), *[vmem(*mid)] * 3,
                vmem(2, 16, 4), vmem(2, 4, 4), vmem(4, 4),
                vmem(5, 2, 16, 4), vmem(len(WAYS) + 1, 2, 4, 4), vmem(len(WAYS) + 1, 4, 4),
                vmem(2, nx * ny, 2, 2), vmem(2, ny, 2 * nx), vmem(2, 8, ny, 2 * nx), vmem(nx + 4, ny + 4, 2, 2),
                vmem(2, 3, 8), vmem(6144),
                pltpu.SemaphoreType.DMA,
                pltpu.SemaphoreType.DMA((2,)),
                pltpu.SemaphoreType.DMA,
                pltpu.SemaphoreType.DMA((PHASES,)),
            ],
            compiler_params=pltpu.CompilerParams(
                collective_id=0, has_side_effects=True, vmem_limit_bytes=40 * 1024 * 1024
            ),
        )(*(pltpu.with_memory_space_constraint(a, pltpu.HBM) for a in (right_side, inverse_density)))
        out = jax.ShapeDtypeStruct(right_side.shape, F32)
        return pl.pallas_call(
            hand_out,
            out_shape=(out, out),
            in_specs=[pl.BlockSpec(memory_space=pltpu.VMEM)] * 2,
            out_specs=(pl.BlockSpec(memory_space=pl.ANY),) * 2,
            scratch_shapes=[pltpu.SemaphoreType.DMA((2,))],
            compiler_params=pltpu.CompilerParams(vmem_limit_bytes=1024 * 1024),
        )(v, r)

    spec = P("gx", "gy", None)
    return jax.shard_map(shards, mesh=mesh, in_specs=(spec, spec), out_specs=(spec, spec), check_vma=False)
```

```python
import functools
import math

import jax
import jax.numpy as jnp
from jax import lax
from jax.experimental import pallas as pl
from jax.experimental.pallas import tpu as pltpu
from jax.sharding import PartitionSpec as P

SWEEPS = 2
COARSE_SWEEPS = 8
MESH = pl.DeviceIdType.MESH
LANES = 128
F32 = jnp.float32

FINE, MID = 16, (20, 16)

WAYS = ((-1, 0), (1, 0), (0, -1), (0, 1), (-1, -1), (-1, 1), (1, -1), (1, 1),
        (-2, 0), (2, 0), (0, -2), (0, 2),
        (-2, -1), (-2, 1), (2, -1), (2, 1), (-1, -2), (-1, 2), (1, -2), (1, 2))
BACK = tuple(WAYS.index((-dy, -dx)) for dy, dx in WAYS)
FIRST, MORE, SWAP, KEEP, LAST, MID_C, STRIP, MID_G, FAR_G, MID_X = range(10)
GATHER, LINE, PLANE = 10, 11, 12
PHASES = 13
YS, XS, CORNERS, NEAR = (0, 1), (2, 3), (4, 5, 6, 7), range(8)


def iota(shape, dim):
    return lax.broadcasted_iota(jnp.int32, shape, dim)


def lane_prev(a):
    return jnp.where(iota(a.shape, 2) == 0, 0.0, pltpu.roll(a, 1, 2))


def lane_next(a):
    return jnp.where(iota(a.shape, 2) == LANES - 1, 0.0, pltpu.roll(a, LANES - 1, 2))


def even_cells(shape):
    return (iota(shape, 0) + iota(shape, 1)) % 2 == 0


def z_other(o, colour, first):
    shape = o[0].shape
    even = (iota(shape, 0) + iota(shape, 1)) % 2 == first % 2
    low = even if colour == 0 else jnp.logical_not(even)
    last = len(o) - 1
    out = []
    for b in range(last + 1):
        before = o[b - 1] if b > 0 else lane_prev(o[last])
        after = o[b + 1] if b < last else lane_next(o[0])
        out.append(jnp.where(low, before, after))
    return out


def around(other, colour, y0, y1, rows):
    groups = range(other.shape[0])
    mid = [other[b, y0:y1, 0:rows] for b in groups]
    zo = z_other(mid, colour, y0)
    return [
        (
            other[b, y0 - 1 : y1 - 1, 0:rows],
            other[b, y0 + 1 : y1 + 1, 0:rows],
            pltpu.roll(mid[b], 1, 1),
            pltpu.roll(mid[b], rows - 1, 1),
            mid[b],
            zo[b],
        )
        for b in groups
    ]


def split_even(zero, one):
    even = even_cells(zero.shape)
    return jnp.where(even, zero, one), jnp.where(even, one, zero)


def pair_rows(a):
    rows = a.shape[1] // 2
    a = a.reshape(a.shape[0] // 2, 2, a.shape[1], LANES)
    a = a[:, 0] + a[:, 1]
    pick = iota((a.shape[0], rows, LANES), 1)
    out = a[:, 0:1] + a[:, 1:2]
    out = jnp.broadcast_to(out, pick.shape)
    for j in range(1, rows):
        out = jnp.where(pick == j, a[:, 2 * j : 2 * j + 1] + a[:, 2 * j + 1 : 2 * j + 2], out)
    return out * 0.125


def double_rows(a, order):
    y = a.shape[0]
    pick = iota((y, 2 * len(order), LANES), 1) // 2
    out = jnp.broadcast_to(a[:, order[0] : order[0] + 1], pick.shape)
    for n, j in enumerate(order[1:], 1):
        out = jnp.where(pick == n, a[:, j : j + 1], out)
    return jnp.concatenate([out[i // 2 : i // 2 + 1] for i in range(2 * y)], axis=0)


def three(x):
    high = x.astype(jnp.bfloat16)
    rest = x - high.astype(F32)
    middle = rest.astype(jnp.bfloat16)
    low = (rest - middle.astype(F32)).astype(jnp.bfloat16)
    return jnp.concatenate([high, middle, low], axis=0)


def permute(x, matrix, side):
    n = x.shape[0]
    out = lax.dot_general(three(x), matrix, (((1,), (side,)), ((), ())), preferred_element_type=F32)
    return (out[0:n] + out[n : 2 * n]) + out[2 * n :]


def y_own(d, w):
    return slice(4, 12) if d == 0 else (slice(12 - w, 12) if d > 0 else slice(4, 4 + w))


def y_halo(d, w):
    return slice(4, 12) if d == 0 else (slice(12, 12 + w) if d > 0 else slice(4 - w, 4))


def x_own(d, w):
    return slice(0, 8) if d == 0 else (slice(8 - w, 8) if d > 0 else slice(0, w))


def x_halo(d, w):
    return slice(0, 8) if d == 0 else (slice(8, 8 + w) if d > 0 else slice(FINE - w, FINE))


def columns_of(dx):
    start = 6 + 4 * dx
    low, high = max(start, 0), min(start + 4, MID[1])
    return slice(low, high), slice(low - start, high - start)


def outer(part, d):
    return slice(part.stop - 1, part.stop) if d > 0 else slice(part.start, part.start + 1)


def block_part(way, far):
    dy, dx = WAYS[way]
    n = far if abs(dy) == 2 else (2 if abs(dx) == 2 and dy else 4)
    return slice(0, n) if dy > 0 else slice(4 - n, 4)


def kernel(nx, ny, g_ref, c_ref, v_out, r_out, perm, held, d0, g0, k0, ra, ba, rb, bb, bp, rc, bc, rd, bd,
           ax_s, ax_r, gx_s, gx_r, an_s, an_r, ac_s, ac_r, sx_s, sx_r, sc_s, sc_r, ex_s, ex_r, ec_s, ec_r,
           d1, g1, k1, mr, mb, mp, strip, blk_g, blk_x, in_c, in_g, in_x,
           gat, cc, kc, vc, zero_y, bulk, held_sem, lead_sem, out_sem, in_sem):
    gx, gy = lax.axis_index("gx"), lax.axis_index("gy")

    def inside(way):
        dy, dx = WAYS[way]
        tests = []
        if dy:
            tests.append(gy + dy >= 0 if dy < 0 else gy + dy < ny)
        if dx:
            tests.append(gx + dx >= 0 if dx < 0 else gx + dx < nx)
        return tests[0] if len(tests) == 1 else jnp.logical_and(*tests)

    def device(way):
        dy, dx = WAYS[way]
        out = {}
        if dx:
            out["gx"] = gx + dx
        if dy:
            out["gy"] = gy + dy
        return out

    has = [inside(way) for way in range(len(WAYS))]
    target = [device(way) for way in range(len(WAYS))]

    def each_peer(fn):
        if nx * ny <= 64:
            for s in range(1, nx * ny):
                fn(s, s // ny, s % ny)
        else:
            def body(s, carry):
                fn(s, s // ny, lax.rem(s, ny))
                return carry
            lax.fori_loop(1, nx * ny, body, 0)

    loads = [
        pltpu.make_async_copy(ref.at[i : i + 2], held.at[n, i : i + 2], held_sem)
        for n, ref in enumerate((c_ref, g_ref)) for i in range(0, 8, 2)
    ]
    for load in loads:
        load.start()

    barrier = pltpu.get_barrier_semaphore()

    def greet(s, sx, sy):
        pl.semaphore_signal(
            barrier, inc=1, device_id={"gx": lax.rem(gx + sx, nx), "gy": lax.rem(gy + sy, ny)}, device_id_type=MESH)

    each_peer(greet)

    for ref in (ax_r, gx_r, ex_r):
        ref[2] = jnp.zeros(ref.shape[1:], F32)
    for ref in (an_r, ac_r, ec_r):
        ref[4] = jnp.zeros(ref.shape[1:], F32)
    for n in range(2):
        sx_r[n, 2] = jnp.zeros(sx_r.shape[2:], F32)
        sc_r[n, 4] = jnp.zeros(sc_r.shape[2:], F32)
    in_c[4] = jnp.zeros(in_c.shape[1:], F32)
    for ref in (in_g, in_x):
        ref[len(WAYS)] = jnp.zeros(ref.shape[1:], F32)
    zero_y[...] = jnp.zeros(zero_y.shape, F32)
    vc[...] = jnp.zeros(vc.shape, F32)

    size_z = 4 * LANES
    row, col = iota((size_z, size_z), 0), iota((size_z, size_z), 1)
    perm[...] = (row == 4 * (col % LANES) + col // LANES).astype(F32).astype(jnp.bfloat16)

    def coarsen(red, black):
        pair = [pair_rows(red[b] + black[b]) for b in range(len(red))]
        if len(pair) == 1:
            return pair[0]
        first, second = split_even(pair[0], pair[1])
        return [first], [second]

    def remote(phase, way, src, dst):
        lead = phase == FIRST and way in YS
        return pltpu.make_async_remote_copy(
            src_ref=src, dst_ref=dst, send_sem=lead_sem.at[way] if lead else out_sem, recv_sem=in_sem.at[phase],
            device_id=target[way], device_id_type=MESH)

    def size(ref):
        return math.prod(ref.shape[:-1])

    def take(sem, rows):
        pltpu.make_async_copy(bulk.at[0:rows], bulk.at[0:rows], sem).wait()

    def ring_messages(src, dst, w, x_s, x_r, c_s, c_r):
        out = []
        for way in YS:
            dy = WAYS[way][0]
            out.append((way, src.at[:, y_own(dy, w), 0:8], dst.at[:, y_halo(-dy, w), 0:8], dst.at[:, y_halo(dy, w), 0:8], zero_y.at[:, 0:w]))
        for way in XS:
            out.append((way, x_s.at[way - 2], x_r.at[BACK[way] - 2], x_r.at[way - 2], x_r.at[2]))
        for way in CORNERS:
            out.append((way, c_s.at[way - 4], c_r.at[BACK[way] - 4], c_r.at[way - 4], c_r.at[4]))
        return out

    def ring_pack(src, cw, x_s, c_s):
        for way in XS:
            x_s[way - 2] = src[:, 4:12, x_own(WAYS[way][1], x_s.shape[-2])]
        for way in CORNERS:
            dy, dx = WAYS[way]
            c_s[way - 4] = src[:, y_own(dy, cw), x_own(dx, cw)]

    def ring_unpack(dst, cw, x_r, c_r):
        for way in XS:
            dst[:, 4:12, x_halo(WAYS[way][1], x_r.shape[-2])] = x_r[way - 2]
        for way in CORNERS:
            dy, dx = WAYS[way]
            dst[:, y_halo(dy, cw), x_halo(dx, cw)] = c_r[way - 4]

    def rows_y(ref, colour, w, only, way):
        dy = WAYS[way][0]
        own, there, here = y_own(dy, w), y_halo(-dy, w), y_halo(dy, w)
        if only:
            own, there, here = (outer(a, d) for a, d in ((own, -dy), (there, -dy), (here, dy)))
        n = 1 if only else w
        return (way, ref.at[colour, :, own, 0:8], ref.at[colour, :, there, 0:8], ref.at[colour, :, here, 0:8],
                zero_y.at[:, 0:n])

    def messages_first():
        out = []
        for way in YS:
            for ref, colour, w in ((d0, 0, 1), (d0, 1, 2), (g0, 0, 1)):
                out.append(rows_y(ref, colour, w, False, way))
        for way in CORNERS:
            out.append((way, an_s.at[way - 4], an_r.at[BACK[way] - 4], an_r.at[way - 4], an_r.at[4]))
        for way in XS:
            out.append((way, ax_s.at[way - 2], ax_r.at[BACK[way] - 2], ax_r.at[way - 2], ax_r.at[2]))
            out.append((way, gx_s.at[way - 2], gx_r.at[BACK[way] - 2], gx_r.at[way - 2], gx_r.at[2]))
        return out

    def messages_more():
        out = []
        for way in YS:
            for ref, colour, w in ((d0, 0, 2), (d0, 1, 3), (g0, 0, 2), (g0, 1, 1)):
                out.append(rows_y(ref, colour, w, True, way))
        for way in CORNERS:
            out.append((way, ac_s.at[way - 4], ac_r.at[BACK[way] - 4], ac_r.at[way - 4], ac_r.at[4]))
        return out

    def block_messages(src, dst, ways, far):
        out = []
        for way in ways:
            give, got = block_part(BACK[way], far), block_part(way, far)
            lead = (slice(None),) * (len(src.shape) - 3)
            out.append((way, src.at[(*lead, give)], dst.at[(BACK[way], *lead, give)], dst.at[(way, *lead, got)],
                        dst.at[(len(WAYS), *lead, got)]))
        return out

    def near_part(way, c):
        n = 4 if way in XS else ((4, 3)[c] if way in YS else (3, 2)[c])
        dy = WAYS[way][0]
        return slice(0, n) if dy > 0 else slice(4 - n, 4)

    def near_more(way, c):
        n = {YS: (0, 4), XS: (0, 0), CORNERS: (4, 3)}[YS if way in YS else (XS if way in XS else CORNERS)][c]
        dy = WAYS[way][0]
        return (slice(n - 1, n) if dy > 0 else slice(4 - n, 5 - n)) if n else None

    def source_message(way, c, part):
        give, got = part(BACK[way], c), part(way, c)
        return (way, blk_g.at[c, give], in_g.at[BACK[way], c, give], in_g.at[way, c, got], in_g.at[len(WAYS), c, got])

    def sources(part):
        for way in NEAR:
            y, (to, of) = 4 * (WAYS[way][0] + 2), columns_of(WAYS[way][1])
            for c in range(2):
                rows = part(way, c)
                if rows:
                    g1[c, 0, y + rows.start : y + rows.stop, to] = in_g[way, c, rows, of]

    def column_messages():
        out = []
        for way in (0, 1, 8, 9):
            dy = WAYS[way][0]
            give, there, here = {
                -1: (slice(6, 10), slice(10, 14), slice(2, 6)), 1: (slice(6, 10), slice(2, 6), slice(10, 14)),
                -2: (slice(6, 8), slice(14, 16), slice(0, 2)), 2: (slice(8, 10), slice(0, 2), slice(14, 16))}[dy]
            out.append((way, strip.at[:, give], strip.at[:, there], strip.at[:, here], in_c.at[4, :, give]))
        return out

    def strip_messages():
        out = []
        for n, way in enumerate((2, 3, 10, 11)):
            part = slice(0, 16) if n < 2 else slice(4, 12)
            out.append((way, strip.at[:, part], in_c.at[n ^ 1, :, part], in_c.at[n, :, part], in_c.at[4, :, part]))
        return out

    def columns():
        for c in range(2):
            d1[c, 0, 2:18, 6:10] = strip[c]
            for n, way in enumerate((2, 3, 10, 11)):
                part = slice(0, 16) if n < 2 else slice(4, 12)
                to, of = columns_of(WAYS[way][1])
                d1[c, 0, 2 + part.start : 2 + part.stop, to] = in_c[n, c, part, of]

    def by_way(messages):
        ways = {}
        for m in messages:
            ways.setdefault(m[0], []).append(m)
        return ways.items()

    sent = {}

    def start(phase, messages):
        for way, group in by_way(messages):
            @pl.when(has[way])
            def _():
                for _, src, there, here, zeros in group:
                    remote(phase, way, src, there).start()

            @pl.when(jnp.logical_not(has[way]))
            def _():
                for _, src, there, here, zeros in group:
                    pltpu.make_async_copy(zeros, here, in_sem.at[phase]).start()

            if phase != FIRST or way not in YS:
                sent[way] = sent.get(way, 0) + sum(size(m[1]) for m in group)

    def finish(phase, messages):
        take(in_sem.at[phase], sum(size(m[3]) for m in messages))

    def first_sent():
        for way in YS:
            @pl.when(has[way])
            def _():
                take(lead_sem.at[way], sum(size(m[1]) for m in first_part if m[0] == way))

    def all_sent():
        always = ((nx * ny - 1) + (ny - 1) + (nx - 1) * ny) * slot
        rows = {}
        for py in range(ny):
            for px in range(nx):
                there = tuple(
                    way for way, (dy, dx) in enumerate(WAYS) if 0 <= py + dy < ny and 0 <= px + dx < nx)
                rows.setdefault((min(py, 2), min(ny - 1 - py, 2), min(px, 2), min(nx - 1 - px, 2)), there)
        low_y, high_y = jnp.minimum(gy, 2), jnp.minimum(ny - 1 - gy, 2)
        low_x, high_x = jnp.minimum(gx, 2), jnp.minimum(nx - 1 - gx, 2)
        place = ((low_y * 3 + high_y) * 3 + low_x) * 3 + high_x
        for (a, b, c, d), there in rows.items():
            @pl.when(place == ((a * 3 + b) * 3 + c) * 3 + d)
            def _():
                take(out_sem, always + sum(sent[way] for way in there))

    me = gx * ny + gy
    def spread():
        def body(s, sx, sy):
            pltpu.make_async_remote_copy(
                src_ref=gat.at[1, me], dst_ref=gat.at[1, me], send_sem=out_sem, recv_sem=in_sem.at[GATHER],
                device_id={"gx": lax.rem(gx + sx, nx), "gy": lax.rem(gy + sy, ny)}, device_id_type=MESH).start()
        each_peer(body)

    slot = size(gat.at[0, 0])

    def along_y():
        for sy in range(1, ny):
            pltpu.make_async_remote_copy(
                src_ref=gat.at[0, me], dst_ref=gat.at[0, me], send_sem=out_sem, recv_sem=in_sem.at[LINE],
                device_id={"gy": lax.rem(gy + sy, ny)}, device_id_type=MESH).start()

    def along_x():
        take(in_sem.at[LINE], (ny - 1) * slot)
        line = gat.at[0, pl.ds(gx * ny, ny)]
        for sx in range(1, nx):
            pltpu.make_async_remote_copy(
                src_ref=line, dst_ref=line, send_sem=out_sem, recv_sem=in_sem.at[PLANE],
                device_id={"gx": lax.rem(gx + sx, nx)}, device_id_type=MESH).start()

    def setup(kref, dens, colour, scale, y0, y1, rows):
        for b, near in enumerate(around(dens.at[1 - colour], colour, y0, y1, rows)):
            here = dens[colour, b, y0:y1, 0:rows]
            total = None
            for f in range(6):
                face = (scale * 0.5) * (here + near[f])
                kref[colour, b, f, y0:y1, 0:rows] = face
                total = face if total is None else total + face
            kref[colour, b, 6, y0:y1, 0:rows] = total
            kref[colour, b, 7, y0:y1, 0:rows] = jnp.where(here > 0.0, 1.0 / total, 0.0)

    def weigh(kref, other, colour, y0, y1, rows):
        out = []
        for b, near in enumerate(around(other, colour, y0, y1, rows)):
            total = kref[colour, b, 0, y0:y1, 0:rows] * near[0]
            for f in range(1, 6):
                total = total + kref[colour, b, f, y0:y1, 0:rows] * near[f]
            out.append(total)
        return out

    def update(kref, g, other, dst, colour, y0, y1, rows):
        for b, n in enumerate(weigh(kref, other, colour, y0, y1, rows)):
            dst[b, y0:y1, 0:rows] = (g[colour, b, y0:y1, 0:rows] + n) * kref[colour, b, 7, y0:y1, 0:rows]

    def first(kref, g, dst, y0, y1, rows):
        for b in range(dst.shape[0]):
            dst[b, y0:y1, 0:rows] = g[0, b, y0:y1, 0:rows] * kref[0, b, 7, y0:y1, 0:rows]

    def residual(kref, g, red, black, y0, y1, rows, x0, x1):
        out = []
        for c, (v, other) in enumerate(((red, black), (black, red))):
            n = weigh(kref, other, c, y0, y1, rows)
            out.append([
                (g[c, b, y0:y1, 0:rows] - (kref[c, b, 6, y0:y1, 0:rows] * v[b, y0:y1, 0:rows] - n[b]))[:, x0:x1]
                for b in range(len(n))])
        return out

    pltpu.make_async_copy(held, held, held_sem).wait()
    flat = permute(held[...].reshape(-1, size_z), perm[...], 0)

    def fields(flat):
        quarters = [
            jnp.swapaxes(flat[:, q * LANES : (q + 1) * LANES].reshape(8, 8, LANES), 0, 1) for q in range(4)]
        pairs = [split_even(quarters[2 * b], quarters[2 * b + 1]) for b in range(2)]
        return [pairs[b][0] for b in range(2)], [pairs[b][1] for b in range(2)]

    dens, source = fields(flat[0:64]), fields(flat[64:128])
    for c in range(2):
        for b in range(2):
            d0[c, b, 4:12, 0:8] = dens[c][b]
            g0[c, b, 4:12, 0:8] = source[c][b]
    for way in XS:
        dx = WAYS[way][1]
        for c in range(2):
            ax_s[way - 2, c] = d0[c, :, 4:12, x_own(dx, 4)]
            gx_s[way - 2, c] = g0[c, :, 4:12, x_own(dx, 2)]
    for way in CORNERS:
        dy, dx = WAYS[way]
        for b in range(2):
            ac_s[way - 4, 2 * b : 2 * b + 2] = d0[1, b, y_own(dy, 2), x_own(dx, 2)]
            an_s[way - 4, :, b : b + 1] = d0[1, b, y_own(dy, 1), x_own(dx, 1)]
            ac_s[way - 4, 4:5, b : b + 1] = d0[0, b, y_own(dy, 1), x_own(dx, 1)]
            ac_s[way - 4, 5:6, b : b + 1] = g0[0, b, y_own(dy, 1), x_own(dx, 1)]
    dens_one = coarsen(*dens)
    for c in range(2):
        strip[c, 6:10] = dens_one[c][0]
    gat[0, me] = coarsen(*dens_one)

    pl.semaphore_wait(barrier, nx * ny - 1)
    first_part, more_part = messages_first(), messages_more()
    start(FIRST, first_part)
    first_sent()
    start(MORE, more_part)
    part_c, part_s = column_messages(), strip_messages()
    along_y()
    finish(FIRST, first_part)
    start(MID_C, part_c)
    for way in XS:
        dx = WAYS[way][1]
        for c in range(2):
            d0[c, :, 4:12, x_halo(dx, 4)] = ax_r[way - 2, c]
            g0[c, :, 4:12, x_halo(dx, 2)] = gx_r[way - 2, c]
    for way in CORNERS:
        dy, dx = WAYS[way]
        for b in range(2):
            d0[1, b, y_halo(dy, 1), x_halo(dx, 1)] = an_r[way - 4, :, b : b + 1]

    setup(k0, d0, 0, 1.0, 3, 13, FINE)
    setup(k0, d0, 1, 1.0, 4, 12, FINE)
    first(k0, g0, ra, 3, 13, FINE)
    update(k0, g0, ra, ba, 1, 4, 12, FINE)
    ring_pack(ba, 2, sx_s.at[0], sc_s.at[0])
    swap = ring_messages(ba, ba, 3, sx_s.at[0], sx_r.at[0], sc_s.at[0], sc_r.at[0])
    start(SWAP, swap)
    finish(MID_C, part_c)
    start(STRIP, part_s)
    finish(MORE, more_part)
    for way in CORNERS:
        dy, dx = WAYS[way]
        for b in range(2):
            d0[1, b, y_halo(dy, 2), x_halo(dx, 2)] = ac_r[way - 4, 2 * b : 2 * b + 2]
            d0[0, b, y_halo(dy, 1), x_halo(dx, 1)] = ac_r[way - 4, 4:5, b : b + 1]
            g0[0, b, y_halo(dy, 1), x_halo(dx, 1)] = ac_r[way - 4, 5:6, b : b + 1]
    setup(k0, d0, 0, 1.0, 2, 14, FINE)
    setup(k0, d0, 1, 1.0, 3, 13, FINE)
    along_x()
    finish(SWAP, swap)
    ring_unpack(ba, 2, sx_r.at[0], sc_r.at[0])
    update(k0, g0, ba, rb, 0, 2, 14, FINE)
    update(k0, g0, rb, bb, 1, 3, 13, FINE)
    source_one = coarsen(*residual(k0, g0, rb, bb, 4, 12, FINE, 0, 8))
    for c in range(2):
        blk_g[c] = source_one[c][0]
        g1[c, 0, 8:12, 6:10] = source_one[c][0]
    part_g, far_g = [], block_messages(blk_g, in_g, range(8, 12), 1)
    for way in NEAR:
        for c in range(2):
            part_g.append(source_message(way, c, near_part))
            if near_more(way, c):
                far_g.append(source_message(way, c, near_more))
    start(MID_G, part_g)

    def blocks(ref, got, ways, far):
        for way in ways:
            dy, dx = WAYS[way]
            part = block_part(way, far)
            y, (to, of) = 4 * (dy + 2), columns_of(dx)
            for c in range(2):
                ref[c, 0, y + part.start : y + part.stop, to] = got[way, c, part, of]

    finish(STRIP, part_s)
    columns()
    for c in range(2):
        setup(k1, d1, c, 0.25, 3 + c, 17 - c, MID[1])

    take(in_sem.at[PLANE], (nx - 1) * ny * slot)
    pairs, rows = ny, 2 * nx

    def assemble(n):
        for i in range(nx):
            for p in range(2):
                cc[p, :, 2 * i : 2 * i + 2] = gat[n, i * ny : (i + 1) * ny, p]
        even = (iota((pairs, rows, LANES), 1) + iota((pairs, rows, LANES), 2)) % 2 == 0
        return jnp.where(even, cc[0], cc[1]), jnp.where(even, cc[1], cc[0])

    shape = (pairs, rows, LANES)
    tested = (iota(shape, 1) + iota(shape, 2)) % 2

    def beside(other, colour):
        low = tested == colour
        return (
            jnp.where(low, jnp.concatenate([other[-1:], other[:-1]], axis=0), other),
            jnp.where(low, other, jnp.concatenate([other[1:], other[:1]], axis=0)),
            pltpu.roll(other, 1, 1), pltpu.roll(other, rows - 1, 1),
            pltpu.roll(other, 1, 2), pltpu.roll(other, LANES - 1, 2))

    centre = assemble(0)
    for c in range(2):
        low = tested == c
        edges = (
            jnp.logical_and(low, iota(shape, 0) == 0),
            jnp.logical_and(jnp.logical_not(low), iota(shape, 0) == pairs - 1),
            iota(shape, 1) == 0, iota(shape, 1) == rows - 1, iota(shape, 2) == 0, iota(shape, 2) == LANES - 1)
        total, faces = None, []
        for near, edge in zip(beside(centre[1 - c], c), edges):
            face = 0.03125 * (centre[c] + jnp.where(edge, 0.0, near))
            total = face if total is None else total + face
            faces.append(face)
        inverse = 1.0 / total
        faces = [jnp.where(edge, 0.0, face * inverse) for edge, face in zip(edges, faces)]
        faces[:2] = jnp.where(low, faces[1], faces[0]), jnp.where(low, faces[0], faces[1])
        for f in range(6):
            kc[c, f] = faces[f]
        kc[c, 6] = inverse

    finish(MID_G, part_g)
    sources(near_part)
    first(k1, g1, mr, 4, 16, 16)
    update(k1, g1, mr, mb, 1, 5, 15, 16)
    update(k1, g1, mb, mr, 0, 6, 14, 16)
    update(k1, g1, mr, mb, 1, 7, 13, 16)
    gat[1, me] = coarsen(*residual(k1, g1, mr, mb, 8, 12, 16, 6, 10))
    spread()
    blk_x[...] = mb[0, 8:12, 6:10]
    part_x = block_messages(blk_x, in_x, range(20), 2)
    start(MID_X, part_x)
    start(FAR_G, far_g)
    ring_pack(bb, 2, sx_s.at[1], sc_s.at[1])
    keep = ring_messages(bb, bp, 3, sx_s.at[1], sx_r.at[1], sc_s.at[1], sc_r.at[1])
    start(KEEP, keep)

    take(in_sem.at[GATHER], (nx * ny - 1) * slot)
    right = assemble(1)
    for c in range(2):
        kc[c, 7] = right[c] * kc[c, 6]

    def half(other, colour):
        total = kc[colour, 7]
        before, after = (jnp.concatenate(a, axis=0) for a in ((other[-1:], other[:-1]), (other[1:], other[:1])))
        nears = (other, jnp.where(tested == colour, before, after), *beside(other, colour)[2:])
        for f, near in enumerate(nears):
            total = total + kc[colour, f] * near
        return total

    def sweep(i, carry):
        red = half(carry[1], 0)
        return red, half(red, 1)

    red = kc[0, 7]
    red, black = lax.fori_loop(1, COARSE_SWEEPS, sweep, (red, half(red, 1)), unroll=True)
    even = tested == 0
    for i in range(nx):
        cut = slice(2 * i, 2 * i + 2)
        vc[2 + i, 2 : 2 + ny, 0] = jnp.where(even, red, black)[:, cut]
        vc[2 + i, 2 : 2 + ny, 1] = jnp.where(even, black, red)[:, cut]

    finish(MID_X, part_x)
    finish(FAR_G, far_g)
    blocks(g1, in_g, range(8, 12), 1)
    sources(near_more)
    mp[0, 8:12, 6:10] = blk_x[...]
    for way in range(20):
        dy, dx = WAYS[way]
        part = block_part(way, 2)
        y, (to, of) = 4 * (dy + 2), columns_of(dx)
        mp[0, y + part.start : y + part.stop, to] = in_x[way, part, of]
    for dx in range(5):
        window = vc[gx + dx, pl.ds(gy, 5)].reshape(10, 2, LANES)
        to, of = columns_of(dx - 2)
        mp[0, :, to] = mp[0, :, to] + double_rows(window, (0, 1))[:, of]
    update(k1, g1, mp, mr, 0, 3, 17, MID[1])
    update(k1, g1, mr, mb, 1, 4, 16, MID[1])
    update(k1, g1, mb, mr, 0, 5, 15, MID[1])
    update(k1, g1, mr, mb, 1, 6, 14, MID[1])

    finish(KEEP, keep)
    bp[:, 4:12, 0:8] = bb[:, 4:12, 0:8]
    ring_unpack(bp, 2, sx_r.at[1], sc_r.at[1])
    half_z = split_even(mr[0, 6:14], mb[0, 6:14])
    for b in range(2):
        bp[b] = bp[b] + double_rows(half_z[b], (6, 7, 8, 9, 10, 11, 4, 5))
    update(k0, g0, bp, rc, 0, 2, 14, FINE)
    update(k0, g0, rc, bc, 1, 3, 13, FINE)
    update(k0, g0, bc, rd, 0, 4, 12, FINE)
    ring_pack(rd, 1, ex_s, ec_s)
    last = ring_messages(rd, rd, 2, ex_s, ex_r, ec_s, ec_r)
    start(LAST, last)
    finish(LAST, last)
    ring_unpack(rd, 1, ex_r, ec_r)
    update(k0, g0, rd, bd, 1, 3, 13, FINE)
    left = residual(k0, g0, rd, bd, 4, 12, FINE, 0, 8)

    def lay(red, black):
        quarters = []
        for b in range(2):
            quarters.extend(split_even(red[b], black[b]))
        return jnp.concatenate([jnp.swapaxes(q, 0, 1).reshape(64, LANES) for q in quarters], axis=1)

    field = [[ref[b, 4:12, 0:8] for b in range(2)] for ref in (rd, bd)]
    flat = permute(jnp.concatenate([lay(*field), lay(*left)], axis=0), perm[...], 1)
    v_out[...] = flat[0:64].reshape(v_out.shape)
    r_out[...] = flat[64:128].reshape(r_out.shape)
    all_sent()


def hand_out(v_ref, r_ref, v_out, r_out, sem):
    pairs = ((v_ref, v_out), (r_ref, r_out))
    for n, (src, dst) in enumerate(pairs):
        for i in range(0, src.shape[0], 2):
            pltpu.make_async_copy(src.at[i : i + 2], dst.at[i : i + 2], sem.at[n]).start()
    for n, (src, dst) in enumerate(pairs):
        pltpu.make_async_copy(src, dst, sem.at[n]).wait()


def solution(mesh):
    nx, ny = mesh.shape["gx"], mesh.shape["gy"]

    def shards(right_side, inverse_density):
        x, y, z = right_side.shape
        assert (x, y, z) == (8, 8, 4 * LANES)

        def vmem(*shape):
            return pltpu.VMEM((*shape, LANES), F32)

        fine = (2, FINE, FINE)
        mid = (1, *MID)
        result = pltpu.VMEM(right_side.shape, F32)
        v, r = pl.pallas_call(
            functools.partial(kernel, nx, ny),
            out_shape=(result, result),
            in_specs=[pl.BlockSpec(memory_space=pl.ANY)] * 2,
            out_specs=(pl.BlockSpec(memory_space=pltpu.VMEM),) * 2,
            scratch_shapes=[
                pltpu.VMEM((z, z), jnp.bfloat16),
                pltpu.VMEM((2, x, y, z), F32),
                vmem(2, *fine), vmem(2, *fine), vmem(2, 2, 8, FINE, FINE),
                *[vmem(*fine)] * 9,
                vmem(2, 2, 2, 8, 4), vmem(3, 2, 2, 8, 4), vmem(2, 2, 2, 8, 2), vmem(3, 2, 2, 8, 2), vmem(4, 1, 2), vmem(5, 1, 2), vmem(4, 6, 2), vmem(5, 6, 2),
                vmem(2, 2, 2, 8, 4), vmem(2, 3, 2, 8, 4), vmem(2, 4, 2, 2, 2), vmem(2, 5, 2, 2, 2),
                vmem(2, 2, 8, 2), vmem(3, 2, 8, 2), vmem(4, 2, 1, 1), vmem(5, 2, 1, 1),
                vmem(2, *mid), vmem(2, *mid), vmem(2, 1, 8, *MID), *[vmem(*mid)] * 3,
                vmem(2, 16, 4), vmem(2, 4, 4), vmem(4, 4),
                vmem(5, 2, 16, 4), vmem(len(WAYS) + 1, 2, 4, 4), vmem(len(WAYS) + 1, 4, 4),
                vmem(2, nx * ny, 2, 2), vmem(2, ny, 2 * nx), vmem(2, 8, ny, 2 * nx), vmem(nx + 4, ny + 4, 2, 2),
                vmem(2, 3, 8), vmem(6144),
                pltpu.SemaphoreType.DMA,
                pltpu.SemaphoreType.DMA((2,)),
                pltpu.SemaphoreType.DMA,
                pltpu.SemaphoreType.DMA((PHASES,)),
            ],
            compiler_params=pltpu.CompilerParams(
                collective_id=0, has_side_effects=True, vmem_limit_bytes=40 * 1024 * 1024
            ),
        )(*(pltpu.with_memory_space_constraint(a, pltpu.HBM) for a in (right_side, inverse_density)))
        out = jax.ShapeDtypeStruct(right_side.shape, F32)
        return pl.pallas_call(
            hand_out,
            out_shape=(out, out),
            in_specs=[pl.BlockSpec(memory_space=pltpu.VMEM)] * 2,
            out_specs=(pl.BlockSpec(memory_space=pl.ANY),) * 2,
            scratch_shapes=[pltpu.SemaphoreType.DMA((2,))],
            compiler_params=pltpu.CompilerParams(vmem_limit_bytes=1024 * 1024),
        )(v, r)

    spec = P("gx", "gy", None)
    return jax.shard_map(shards, mesh=mesh, in_specs=(spec, spec), out_specs=(spec, spec), check_vma=False)
```
